128 devices in a mesh: blk: 32 (over y, z, core), sub: 4 (over x).
Axes of the slice: x: 4, y: 4, z: 4, core: 2. Of those that a mesh axis runs over, the one named last changes fastest.
Arguments:
- pressure: float32 [2, 8, 8, 8, 65536], P(None, None, None, None, ('blk', 'sub')), may hold values from -6 to 6
- right_side: float32 [2, 8, 8, 8, 65536], P(None, None, None, None, ('blk', 'sub')), may hold values from -6 to 6
- geometry: float32 [6, 8, 8, 8, 65536], P(None, None, None, None, ('blk', 'sub')), may hold values from -0.03 to 0.08, as said below
- face_weight: float32 [64, 6, 65536], P(None, None, ('blk', 'sub')), may hold values from 0.004 to 0.02
- face_metric: float32 [64, 6, 65536], P(None, None, ('blk', 'sub')), may hold values from 0.5 to 2
- cross_slots: int32 [5, 128, 576], P(None, ('blk', 'sub')), may hold values from 0 to 511, as said below
- local_pairs: int32 [5, 65536], P(None, ('blk', 'sub')), may hold values from 0 to 511, as said below
- coarse_map: int32 [65536], P(('blk', 'sub')), may hold values from 0 to 255, as said below
- coarse_inverse: float32 [8, 8, 8192], P(None, None, 'blk'), may hold values from -0.12 to 0.48, as said below
Outputs:
- residual: float32 [2, 8, 8, 8, 65536], P(None, None, None, None, ('blk', 'sub'))
- corrected: float32 [2, 8, 8, 8, 65536], P(None, None, None, None, ('blk', 'sub'))
The draws below stay inside these ranges and needn't reach their ends.
Inputs may be any that keep to these rules, and one draw needn't show every extreme that they name: `cross_slots`: Rows: local element index, face 0 to 5 (low or high end of node axis 1, 2, 3), live flag, owner flag, orientation code 0 to 7. Columns come in 9 blocks of 64, block k for neighbour k of the device grid; block 4 (the device itself) has no live slot. The slot of device d at neighbour k, place c and the slot of neighbour k at column (8 - k) * 64 + c describe the same pair: equal live flags and codes, opposite owner flags. Within a block the live slots come first; every device shares exactly 64 pairs with some neighbour. Every (element, face) of a device appears at most once among its slots, live or not, and its local pairs. `local_pairs`: the columns of device d hold 512 pairs of its own elements; see cross_slots for the faces used. `coarse_map`: each coarse cell of a Morton block holds exactly 8 elements of that block. `geometry`: at each node the 3 x 3 matrix of the six rows is symmetric positive definite. `coarse_inverse`: each block is symmetric.
All inputs are finite; a program needn't handle non-finite values.
Results may differ from the reference program's by a relative error of at most 0.00016.
Values sent between devices are 32-bit elements; how exact they have to be, the bound alone decides.
A program may use at most 128 MiB of HBM per device.

```python
import math
import jax
import jax.numpy as jnp
import numpy as np
from jax import lax

NP = 8
FACE = 64
FIELDS = 2
E_DEV = 512
RANKS = 128
ELEMS = 65536
CAP = 64
CROW = 256
CCELLS = 8192
N_SUB = 4


def pair_tables(key):
    base_key = jax.random.fold_in(key, 7)
    sub_keys = jax.random.split(base_key, 7)
    row_ids = jnp.arange(RANKS, dtype=jnp.int32)[:, None]
    direction = jnp.arange(9, dtype=jnp.int32)[None, :]
    block_place = row_ids // N_SUB
    sub_place = row_ids % N_SUB
    peer_rank = (block_place + direction // 3 - 1) % (RANKS // N_SUB) * N_SUB + (sub_place + direction % 3 - 1) % N_SUB
    mirror_dir = jnp.broadcast_to(8 - direction, (RANKS, 9))
    lower = direction < 4
    upper = direction > 4
    raw_counts = jax.random.randint(sub_keys[0], (RANKS, 9), 0, CAP + 1, dtype=jnp.int32)
    full_dir = jax.random.randint(sub_keys[1], (), 0, 4, dtype=jnp.int32)
    raw_counts = jnp.where(direction == full_dir, CAP, raw_counts)
    counts = jnp.where(lower, raw_counts, jnp.where(upper, raw_counts[peer_rank, mirror_dir], 0))
    slot_place = jnp.arange(CAP, dtype=jnp.int32)[None, None, :]
    live_flag = (slot_place < counts[:, :, None]).astype(jnp.int32)
    weights_dev = jax.random.randint(sub_keys[2], (RANKS,), 1, 9, dtype=jnp.int32)
    coin_draw = jax.random.randint(sub_keys[3], (RANKS, 9), 0, 1 << 20, dtype=jnp.int32)
    own_weight = jnp.broadcast_to(weights_dev[:, None], (RANKS, 9))
    upper_own = (coin_draw % (own_weight + weights_dev[peer_rank]) < own_weight).astype(jnp.int32)
    owner_flag = jnp.where(lower, upper_own, jnp.where(upper, 1 - upper_own[peer_rank, mirror_dir], 0))
    owner_flag = jnp.broadcast_to(owner_flag[:, :, None], (RANKS, 9, CAP))
    raw_codes = jax.random.randint(sub_keys[4], (RANKS, 9, CAP), 0, 8, dtype=jnp.int32)
    place_ids = jnp.broadcast_to(slot_place, (RANKS, 9, CAP))
    mirrored_codes = raw_codes[peer_rank[:, :, None], mirror_dir[:, :, None], place_ids]
    orient_codes = jnp.where(lower[:, :, None], raw_codes, mirrored_codes)
    face_ids = jax.vmap(lambda rank_id: jax.random.permutation(jax.random.fold_in(sub_keys[5], rank_id), 6 * E_DEV))(jnp.arange(RANKS, dtype=jnp.int32)).astype(jnp.int32)
    cross_ids = face_ids[:, :9 * CAP]
    local_ids = face_ids[:, 9 * CAP:9 * CAP + 2 * E_DEV].reshape(RANKS, E_DEV, 2)
    cross_table = jnp.stack([cross_ids % E_DEV, cross_ids // E_DEV, live_flag.reshape(RANKS, 9 * CAP), owner_flag.reshape(RANKS, 9 * CAP), orient_codes.reshape(RANKS, 9 * CAP)])
    local_codes = jax.random.randint(sub_keys[6], (RANKS, E_DEV), 0, 8, dtype=jnp.int32)
    local_table = jnp.stack([local_ids[:, :, 0] % E_DEV, local_ids[:, :, 0] // E_DEV, local_ids[:, :, 1] % E_DEV, local_ids[:, :, 1] // E_DEV, local_codes]).reshape(5, RANKS * E_DEV)
    return (cross_table.astype(jnp.int32), local_table.astype(jnp.int32))


def draw_cross_slots(key, part):
    return pair_tables(key)[0]


def draw_local_pairs(key, part):
    return pair_tables(key)[1]


def draw_coarse_map(key, part):
    cell_ids = jnp.arange(CROW * 8, dtype=jnp.int32) // 8
    blocks = jax.vmap(lambda row_index: jax.random.permutation(jax.random.fold_in(key, row_index), cell_ids))(jnp.arange(CCELLS // CROW, dtype=jnp.int32))
    return blocks.reshape(-1).astype(jnp.int32)


def draw_geometry(key, part):
    sub_keys = jax.random.split(key, 2)
    shape_all = (3, NP, NP, NP, ELEMS)
    diagonal = jnp.exp(jax.random.uniform(sub_keys[0], shape_all, jnp.float32, math.log(0.004), math.log(0.02)))
    coupling = jax.random.uniform(sub_keys[1], shape_all, jnp.float32, -0.3, 0.3)
    result = jnp.stack([diagonal[0], diagonal[1], diagonal[2], coupling[0] * jnp.sqrt(diagonal[0] * diagonal[1]), coupling[1] * jnp.sqrt(diagonal[0] * diagonal[2]), coupling[2] * jnp.sqrt(diagonal[1] * diagonal[2])])
    return result.astype(jnp.float32)


def draw_coarse_inverse(key, part):
    sub_keys = jax.random.split(key, 2)
    diagonal = jnp.exp(jax.random.uniform(sub_keys[0], (8, CCELLS), jnp.float32, math.log(0.04), math.log(0.12)))
    noise_draw = jax.random.uniform(sub_keys[1], (8, 8, CCELLS), jnp.float32, -0.03, 0.03)
    symmetric = 0.5 * (noise_draw + jnp.transpose(noise_draw, (1, 0, 2)))
    identity = jnp.eye(8, dtype=jnp.float32)[:, :, None]
    blocks = symmetric * (1.0 - identity) + identity * diagonal[:, None, :]
    return blocks.astype(jnp.float32)


def block_scale(own_key, extent, pieces, smallest, top_value):
    def one(axis_at, parts):
        heights = jax.random.uniform(jax.random.fold_in(jax.random.fold_in(own_key, 6), axis_at), (parts,), jnp.float32, smallest / len(pieces), top_value / len(pieces))
        return jnp.repeat(jnp.exp(heights), extent[axis_at] // parts).reshape((-1,) + (1,) * (len(extent) - axis_at - 1))

    level = one(*pieces[0])
    for cut in pieces[1:]:
        level = level * one(*cut)
    return level


def gaussian(rng, extent, width, limit, shards=(), held_as=jnp.bfloat16):
    values = jax.random.normal(rng, extent, jnp.float32) * width
    if len(shards) > 0:
        values = block_scale(rng, extent, shards, -0.22, 0.18) * values
    return jnp.clip(values, min=-limit, max=limit).astype(held_as)


def setup_inputs(seed: int = 0) -> dict:
    key_list = jax.random.split(jax.random.key(seed), 10)
    pressure = gaussian(key_list[0], (FIELDS, NP, NP, NP, ELEMS), 1.0, 6.0, ((4, 128),), jnp.float32)
    right_side = gaussian(key_list[1], (FIELDS, NP, NP, NP, ELEMS), 1.0, 6.0, ((4, 128),), jnp.float32)
    geometry = draw_geometry(jax.random.fold_in(key_list[9], 71), 0)
    face_weight = jnp.clip(jnp.exp(math.log(0.02) - 1.6094378 * jax.random.uniform(key_list[3], (FACE, 6, ELEMS), jnp.float32) ** block_scale(key_list[3], (FACE, 6, ELEMS), ((2, 128),), -0.2, 0.2)), 0.004, 0.02)
    face_metric = jnp.clip(jnp.exp(math.log(2.0) - 1.3862944 * jax.random.uniform(key_list[4], (FACE, 6, ELEMS), jnp.float32) ** block_scale(key_list[4], (FACE, 6, ELEMS), ((2, 128),), -0.2, 0.2)), 0.5, 2.0)
    cross_slots = draw_cross_slots(jax.random.fold_in(key_list[9], 71), 0)
    local_pairs = draw_local_pairs(jax.random.fold_in(key_list[9], 71), 0)
    coarse_map = draw_coarse_map(jax.random.fold_in(key_list[9], 71), 0)
    coarse_inverse = draw_coarse_inverse(jax.random.fold_in(key_list[9], 71), 0)
    return {"pressure": pressure, "right_side": right_side, "geometry": geometry, "face_weight": face_weight, "face_metric": face_metric, "cross_slots": cross_slots, "local_pairs": local_pairs, "coarse_map": coarse_map, "coarse_inverse": coarse_inverse}


precise = lax.Precision.HIGHEST


def node_points(node_count):
    if node_count == 8:
        positive = [0.2092992179024789, 0.5917001814331423, 0.8717401485096066, 1.0]
    else:
        positive = [0.4472135954999579, 1.0]
    return np.array(sorted([-entry_value for entry_value in positive] + positive))


def derivative_matrix(node_count):
    points = node_points(node_count)
    weights = np.array([1.0 / np.prod([points[row_index] - points[col_index] for col_index in range(node_count) if col_index != row_index]) for row_index in range(node_count)])
    matrix = np.zeros((node_count, node_count))
    for row_index in range(node_count):
        for col_index in range(node_count):
            if row_index != col_index:
                matrix[row_index, col_index] = weights[col_index] / weights[row_index] / (points[row_index] - points[col_index])
        matrix[row_index, row_index] = -np.sum(matrix[row_index])
    return matrix


def edge_matrix(node_count):
    derivative = derivative_matrix(node_count)
    edge_rows = np.zeros((4, node_count))
    edge_rows[0, 0] = 1.0
    edge_rows[1] = -derivative[0]
    edge_rows[2, node_count - 1] = 1.0
    edge_rows[3] = derivative[node_count - 1]
    return edge_rows


def prolong_matrix(node_count):
    points = node_points(node_count)
    return np.stack([(1.0 - points) / 2.0, (1.0 + points) / 2.0], axis=1)


def orient_tables(node_count):
    forward = np.zeros((8, node_count * node_count), np.int32)
    for orient_code in range(8):
        for first_axis in range(node_count):
            for second_axis in range(node_count):
                if orient_code & 4:
                    source_one, source_two = second_axis, first_axis
                else:
                    source_one, source_two = first_axis, second_axis
                if orient_code & 1:
                    source_one = node_count - 1 - source_one
                if orient_code & 2:
                    source_two = node_count - 1 - source_two
                forward[orient_code, first_axis * node_count + second_axis] = source_one * node_count + source_two
    inverse = np.argsort(forward, axis=1).astype(np.int32)
    return forward, inverse


def reorient(traces, orient_codes, table):
    result = jnp.zeros_like(traces)
    for orient_code in range(8):
        permuted = jnp.take(traces, jnp.asarray(table[orient_code], jnp.int32), axis=-2)
        result = result + jnp.where(orient_codes == orient_code, permuted, 0.0)
    return result


def face_flux(first_side, second_side, orient_codes, node_count):
    forward, inverse = orient_tables(node_count)
    first_value, first_slope, first_weight, first_metric = first_side
    second_value = reorient(second_side[0], orient_codes, forward)
    second_slope = reorient(second_side[1], orient_codes, forward)
    second_weight = reorient(second_side[2], orient_codes, forward)
    second_metric = reorient(second_side[3], orient_codes, forward)
    penalty = node_count * (node_count + 1) / 2.0
    jump_value = first_value - second_value
    weight = 0.5 * (first_weight + second_weight)
    penalty_term = penalty * 0.5 * (first_metric + second_metric)
    normal_term = weight * (penalty_term * jump_value - 0.5 * (first_slope - second_slope))
    symmetric_term = -0.5 * weight * jump_value
    return (normal_term, symmetric_term * first_metric,
            -reorient(normal_term, orient_codes, inverse),
            -reorient(symmetric_term, orient_codes, inverse) * second_side[3])


def volume_term(fields, geometry, derivative):
    deriv_table = jnp.asarray(derivative, jnp.float32)
    slope_first = jnp.einsum('ik,fkjle->fijle', deriv_table, fields, precision=precise)
    slope_second = jnp.einsum('jk,fikle->fijle', deriv_table, fields, precision=precise)
    slope_third = jnp.einsum('lk,fijke->fijle', deriv_table, fields, precision=precise)
    flux_first = geometry[0] * slope_first + geometry[3] * slope_second + geometry[4] * slope_third
    flux_second = geometry[3] * slope_first + geometry[1] * slope_second + geometry[5] * slope_third
    flux_third = geometry[4] * slope_first + geometry[5] * slope_second + geometry[2] * slope_third
    result = jnp.einsum('ki,fkjle->fijle', deriv_table, flux_first, precision=precise)
    result = result + jnp.einsum('kj,fikle->fijle', deriv_table, flux_second, precision=precise)
    return result + jnp.einsum('kl,fijke->fijle', deriv_table, flux_third, precision=precise)


def face_traces(fields, face_metric, edge_rows):
    field_count = fields.shape[0]
    elem_count = fields.shape[-1]
    face_size = fields.shape[1] * fields.shape[1]
    einsum_forms = ['ak,fkjle->fajle', 'ak,fikle->faile', 'ak,fijke->faije']
    values = []
    slopes = []
    for einsum_form in einsum_forms:
        along_axis = jnp.einsum(einsum_form, edge_rows, fields, precision=precise)
        flat_rows = along_axis.reshape(field_count, 4, face_size, elem_count)
        values += [flat_rows[:, 0], flat_rows[:, 2]]
        slopes += [flat_rows[:, 1], flat_rows[:, 3]]
    value_all = jnp.stack(values, axis=2)
    slope_all = jnp.stack(slopes, axis=2) * face_metric
    return value_all.reshape(field_count, face_size, 6 * elem_count), slope_all.reshape(field_count, face_size, 6 * elem_count)


def lift_faces(value_sum, lift_sum, edge_rows, node_count):
    field_count, face_size, flat_count = value_sum.shape
    elem_count = flat_count // 6
    value_grid = value_sum.reshape(field_count, face_size, 6, elem_count)
    lift_grid = lift_sum.reshape(field_count, face_size, 6, elem_count)
    einsum_forms = ['ak,fajle->fkjle', 'ak,faile->fikle', 'ak,faije->fijke']
    result = 0.0
    for axis_number, einsum_form in enumerate(einsum_forms):
        stacked = jnp.stack([value_grid[:, :, 2 * axis_number], lift_grid[:, :, 2 * axis_number],
                             value_grid[:, :, 2 * axis_number + 1], lift_grid[:, :, 2 * axis_number + 1]], axis=1)
        stacked = stacked.reshape(field_count, 4, node_count, node_count, elem_count)
        result = result + jnp.einsum(einsum_form, edge_rows, stacked, precision=precise)
    return result


def deposit(running, slot_index, contribution, weight_mask):
    return running.at[:, :, slot_index].add(contribution * weight_mask)


def restrict(residual, prolong):
    coarse = jnp.einsum('ia,jb,kc,fijke->fabce', prolong, prolong, prolong, residual, precision=precise)
    return coarse.reshape(residual.shape[0], 8, residual.shape[-1])


def prolong_back(coarse, prolong):
    shaped = coarse.reshape(coarse.shape[0], 2, 2, 2, coarse.shape[-1])
    return jnp.einsum('ia,jb,kc,fabce->fijke', prolong, prolong, prolong, shaped, precision=precise)


def reference(pressure, right_side, geometry, face_weight, face_metric, cross_slots, local_pairs, coarse_map, coarse_inverse):
    derivative = derivative_matrix(NP)
    edge_rows = jnp.asarray(edge_matrix(NP), jnp.float32)
    volume = lax.map(lambda single: volume_term(single[None], geometry, derivative)[0], pressure)
    value_all, slope_all = face_traces(pressure, face_metric, edge_rows)
    weight_flat = face_weight.reshape(FACE, 6 * ELEMS)
    metric_flat = face_metric.reshape(FACE, 6 * ELEMS)

    def select_side(slot_index):
        return (jnp.take(value_all, slot_index, axis=2), jnp.take(slope_all, slot_index, axis=2),
                jnp.take(weight_flat, slot_index, axis=1), jnp.take(metric_flat, slot_index, axis=1))

    device_rank = jnp.arange(RANKS, dtype=jnp.int32)[:, None]
    slot_column = jnp.arange(9 * CAP, dtype=jnp.int32)[None, :]
    direction = slot_column // CAP
    block_place = device_rank // N_SUB
    sub_place = device_rank % N_SUB
    peer_rank = ((block_place + direction // 3 - 1) % (RANKS // N_SUB)) * N_SUB + (sub_place + direction % 3 - 1) % N_SUB
    mirror = (8 - direction) * CAP + slot_column % CAP
    second_elem = cross_slots[0][peer_rank, mirror]
    second_face = cross_slots[1][peer_rank, mirror]
    first_index = (cross_slots[1] * ELEMS + device_rank * E_DEV + cross_slots[0]).reshape(-1)
    second_index = (second_face * ELEMS + peer_rank * E_DEV + second_elem).reshape(-1)
    own_mask = (cross_slots[2] * cross_slots[3]).reshape(-1).astype(jnp.float32)
    orient_codes = cross_slots[4].reshape(-1)
    first_value, first_lift, second_value, second_lift = face_flux(select_side(first_index), select_side(second_index), orient_codes, NP)
    value_sum = jnp.zeros((FIELDS, FACE, 6 * ELEMS), jnp.float32)
    lift_sum = jnp.zeros((FIELDS, FACE, 6 * ELEMS), jnp.float32)
    value_sum = deposit(value_sum, first_index, first_value, own_mask)
    value_sum = deposit(value_sum, second_index, second_value, own_mask)
    lift_sum = deposit(lift_sum, first_index, first_lift, own_mask)
    lift_sum = deposit(lift_sum, second_index, second_lift, own_mask)
    local_rank = jnp.arange(ELEMS, dtype=jnp.int32) // E_DEV
    local_first = local_pairs[1] * ELEMS + local_rank * E_DEV + local_pairs[0]
    local_second = local_pairs[3] * ELEMS + local_rank * E_DEV + local_pairs[2]
    first_value, first_lift, second_value, second_lift = face_flux(select_side(local_first), select_side(local_second), local_pairs[4], NP)
    value_sum = deposit(value_sum, local_first, first_value, 1.0)
    value_sum = deposit(value_sum, local_second, second_value, 1.0)
    lift_sum = deposit(lift_sum, local_first, first_lift, 1.0)
    lift_sum = deposit(lift_sum, local_second, second_lift, 1.0)
    operated = volume + lift_faces(value_sum, lift_sum, edge_rows, NP)
    residual = right_side - operated
    prolong = jnp.asarray(prolong_matrix(NP), jnp.float32)
    restricted = restrict(residual, prolong)
    cell_ids = (jnp.arange(ELEMS, dtype=jnp.int32) // (8 * CROW)) * CROW + coarse_map
    cell_sums = jax.ops.segment_sum(jnp.moveaxis(restricted, 2, 0), cell_ids, num_segments=CCELLS)
    correction = jnp.einsum('ijc,cfj->cfi', coarse_inverse, cell_sums, precision=precise)
    spread = jnp.moveaxis(correction[cell_ids], 0, 2)
    corrected = pressure + prolong_back(spread, prolong)
    return residual, corrected
```

```python
import functools

import jax
import jax.numpy as jnp
import numpy as np
from jax import lax
from jax.experimental import pallas as pl
from jax.experimental.pallas import tpu as pltpu
from jax.sharding import PartitionSpec as P

NODES = 8
FACE = NODES * NODES
BRICK = NODES * FACE
LANES = 128
MESH = pl.DeviceIdType.MESH
VMEM = pltpu.MemorySpace.VMEM
SMEM = pltpu.MemorySpace.SMEM


def node_points():
    positive = [0.2092992179024789, 0.5917001814331423, 0.8717401485096066, 1.0]
    return np.array(sorted([-entry for entry in positive] + positive))


def derivative_matrix():
    points = node_points()
    count = len(points)
    weights = np.array(
        [
            1.0 / np.prod([points[row] - points[col] for col in range(count) if col != row])
            for row in range(count)
        ]
    )
    matrix = np.zeros((count, count))
    for row in range(count):
        for col in range(count):
            if row != col:
                matrix[row, col] = weights[col] / weights[row] / (points[row] - points[col])
        matrix[row, row] = -np.sum(matrix[row])
    return matrix


DERIV = derivative_matrix()
POINTS = node_points()
MODES = np.stack([(1.0 - POINTS) / 2.0, (1.0 + POINTS) / 2.0], axis=1)


def split_constant(matrix):
    high = matrix.astype(jnp.bfloat16)
    low = (matrix - high.astype(np.float64)).astype(jnp.bfloat16)
    return np.concatenate([high, low, high], axis=1)


def forward_table():
    eye = np.eye(NODES)
    return split_constant(np.concatenate([np.kron(DERIV, eye), np.kron(eye, DERIV)], axis=0))


def backward_table():
    eye = np.eye(NODES)
    return split_constant(np.concatenate([np.kron(DERIV.T, eye), np.kron(eye, DERIV.T)], axis=1))


def lift_table():
    eye = np.eye(NODES)
    rows = [eye[:, :1], -DERIV[:1].T, eye[:, -1:], DERIV[-1:].T]
    second = [np.kron(row, eye) for row in rows]
    third = [np.kron(eye, row) for row in rows]
    return split_constant(np.concatenate(second + third, axis=1))


def split_rows(values):
    high = values.astype(jnp.bfloat16)
    low = (values - high.astype(jnp.float32)).astype(jnp.bfloat16)
    return jnp.concatenate([high, high, low], axis=0)


def product(table, values):
    return lax.dot_general(
        table, split_rows(values), (((1,), (0,)), ((), ())), preferred_element_type=jnp.float32
    )


def even_odd(matrix, layers):
    half = NODES // 2
    sums = [layers[k] + layers[NODES - 1 - k] for k in range(half)]
    gaps = [layers[k] - layers[NODES - 1 - k] for k in range(half)]
    result = [None] * NODES
    for row in range(half):
        even = None
        odd = None
        for k in range(half):
            first = float((matrix[row, k] + matrix[row, NODES - 1 - k]) / 2)
            second = float((matrix[row, k] - matrix[row, NODES - 1 - k]) / 2)
            even = first * sums[k] if even is None else even + first * sums[k]
            odd = second * gaps[k] if odd is None else odd + second * gaps[k]
        result[row] = odd + even
        result[NODES - 1 - row] = odd - even
    return result


def weighted(coefficients, layers):
    total = None
    for factor, layer in zip(coefficients, layers):
        term = float(factor) * layer
        total = term if total is None else total + term
    return total


def pack_kernel(slots, p_ref, fw_ref, fm_ref, t_ref, send_ref):
    step = pl.program_id(0)
    elems = t_ref.shape[0] // 6
    fields = p_ref.shape[0] // BRICK
    base = step * LANES
    for axis in range(3):
        values = []
        slopes = []
        for field in range(fields):
            start = field * BRICK
            layers = []
            for k in range(NODES):
                if axis == 0:
                    layers.append(p_ref[start + k * FACE : start + (k + 1) * FACE, :])
                elif axis == 1:
                    rows = [
                        p_ref[start + i * FACE + k * NODES : start + i * FACE + (k + 1) * NODES, :]
                        for i in range(NODES)
                    ]
                    layers.append(jnp.concatenate(rows, axis=0))
                else:
                    layers.append(p_ref[pl.ds(start + k, FACE, stride=NODES), :])
            values.append((layers[0], layers[-1]))
            slopes.append((weighted(-DERIV[0], layers), weighted(DERIV[-1], layers)))
        for side in range(2):
            face = 2 * axis + side
            metric = fm_ref[face]
            rows = pl.ds(pl.multiple_of(face * elems + base, LANES), LANES)
            value = jnp.concatenate([entry[side] for entry in values], axis=0)
            slope = jnp.concatenate([entry[side] * metric for entry in slopes], axis=0)
            t_ref[rows, 0:LANES] = value.T
            t_ref[rows, LANES : 2 * LANES] = slope.T
            t_ref[rows, 2 * LANES :] = jnp.concatenate([fw_ref[face], metric], axis=0).T

    @pl.when(step == pl.num_programs(0) - 1)
    def _():
        def move(c, carry):
            row = slots[1, 0, c] * elems + slots[0, 0, c]
            send_ref[pl.ds(c, 1), :] = t_ref[pl.ds(row, 1), :]
            return carry

        lax.fori_loop(0, send_ref.shape[0], move, 0, unroll=8)


def exchange_kernel(n_blk, n_sub, send_ref, recv_ref, send_sem, recv_sem):
    place = lax.axis_index("blk")
    sub = lax.axis_index("sub")
    width = send_ref.shape[0] // 9

    def peer(k):
        return (
            lax.rem(place + (k // 3 - 1) + n_blk, n_blk),
            lax.rem(sub + (k % 3 - 1) + n_sub, n_sub),
        )

    others = [k for k in (0, 2, 6, 8, 1, 7, 3, 5)]
    barrier = pltpu.get_barrier_semaphore()
    for k in others:
        pl.semaphore_signal(barrier, inc=1, device_id=peer(k), device_id_type=MESH)
    pl.semaphore_wait(barrier, len(others))
    copies = []
    for k in others:
        copies.append(
            pltpu.make_async_remote_copy(
                src_ref=send_ref.at[pl.ds(k * width, width)],
                dst_ref=recv_ref.at[pl.ds((8 - k) * width, width)],
                send_sem=send_sem.at[k],
                recv_sem=recv_sem.at[8 - k],
                device_id=peer(k),
                device_id_type=MESH,
            )
        )
        copies[-1].start()
    recv_ref[4 * width : 5 * width, :] = jnp.zeros((width, recv_ref.shape[1]), jnp.float32)
    for copy in copies:
        copy.wait()


def volume_kernel(p_ref, g_ref, fwd_ref, bwd_ref, out_ref, s_ref):
    fields = p_ref.shape[0]

    def first(n, carry):
        f = n // NODES
        rows = pl.ds(pl.multiple_of((n % NODES) * NODES, NODES), NODES)
        layers = [p_ref[f, k, rows, :] for k in range(NODES)]
        for k, value in enumerate(even_odd(DERIV, layers)):
            s_ref[f, k, rows, :] = value
        return carry

    lax.fori_loop(0, fields * NODES, first, 0)

    def middle(i, carry):
        for f in range(fields):
            both = product(fwd_ref[...], p_ref[f, i])
            s1 = s_ref[f, i]
            s2 = both[:FACE]
            s3 = both[FACE:]
            q1 = g_ref[0, i] * s1 + g_ref[3, i] * s2 + g_ref[4, i] * s3
            q2 = g_ref[3, i] * s1 + g_ref[1, i] * s2 + g_ref[5, i] * s3
            q3 = g_ref[4, i] * s1 + g_ref[5, i] * s2 + g_ref[2, i] * s3
            s_ref[f, i] = q1
            out_ref[f, i] = product(bwd_ref[...], jnp.concatenate([q2, q3], axis=0))
        return carry

    lax.fori_loop(0, NODES, middle, 0)

    def last(n, carry):
        f = n // NODES
        rows = pl.ds(pl.multiple_of((n % NODES) * NODES, NODES), NODES)
        layers = [s_ref[f, k, rows, :] for k in range(NODES)]
        for k, value in enumerate(even_odd(DERIV.T, layers)):
            out_ref[f, k, rows, :] += value
        return carry

    lax.fori_loop(0, fields * NODES, last, 0)


def inverse_code(code):
    swapped = 4 + 2 * (code & 1) + ((code >> 1) & 1)
    return jnp.where((code & 4) != 0, swapped, code)


def lane_pick(values, index):
    return jnp.take_along_axis(values, index, axis=1, mode="promise_in_bounds")


def pair_flux(own, peer, code):
    lane = lax.broadcasted_iota(jnp.int32, code.shape, 1)
    node = lane & (FACE - 1)
    swapped = ((node & (NODES - 1)) << 3) | (node >> 3)
    source = jnp.where((code & 4) != 0, swapped, node)
    source = source ^ ((code & 1) * 56) ^ (((code >> 1) & 1) * 7)
    both = source | (lane & FACE)
    v1 = own[:, 0:LANES]
    g1 = own[:, LANES : 2 * LANES]
    wm1 = own[:, 2 * LANES :]
    v2 = lane_pick(peer[:, 0:LANES], both)
    g2 = lane_pick(peer[:, LANES : 2 * LANES], both)
    wm2 = peer[:, 2 * LANES :]
    w2 = lane_pick(wm2, source)
    m2 = lane_pick(wm2, source + FACE)
    w1 = lane_pick(wm1, node)
    m1 = lane_pick(wm1, node + FACE)
    penalty = NODES * (NODES + 1) / 2.0
    jump = v1 - v2
    weight = 0.5 * (w1 + w2)
    tau = (penalty * 0.5) * (m1 + m2)
    value = weight * (tau * jump - 0.5 * (g1 - g2))
    lift = (-0.5 * weight * jump) * m1
    return value, lift


def combine_kernel(
    slots, pairs, slots_v, pairs_v, own_ref, recv_ref, t_ref, vol_ref, rhs_ref, lift_ref, modes_ref,
    cells_ref, res_ref, sums_ref, vt, lt, lb, vb, hb, cb, pad, fv, fl, cs,
):
    elems = t_ref.shape[0] // 6
    slot_total = own_ref.shape[0]
    pair_total = lb.shape[0] // 2
    width = slot_total // 9
    fields = 2

    def clear(n, carry):
        rows = pl.ds(pl.multiple_of(n * FACE, FACE), FACE)
        zero = jnp.zeros((FACE, LANES), jnp.float32)
        vt[rows, :] = zero
        lt[rows, :] = zero
        return carry

    lax.fori_loop(0, vt.shape[0] // FACE, clear, 0)

    def gather(c, carry):
        first = pairs[1, c] * elems + pairs[0, c]
        second = pairs[3, c] * elems + pairs[2, c]
        lb[pl.ds(c, 1), :] = t_ref[pl.ds(first, 1), :]
        lb[pl.ds(c + pair_total, 1), :] = t_ref[pl.ds(second, 1), :]
        return carry

    lax.fori_loop(0, pair_total, gather, 0, unroll=8)

    raw = slots_v[4]
    code = jnp.where(slots_v[3] != 0, raw, inverse_code(raw)) + 8 * slots_v[2]
    pad[0:1, 0:slot_total] = code.astype(jnp.float32)
    pad[0:1, slot_total:] = jnp.zeros((1, pad.shape[1] - slot_total), jnp.float32)
    for t in range(pad.shape[1] // LANES):
        row = jnp.broadcast_to(pad[0:1, t * LANES : (t + 1) * LANES], (LANES, LANES))
        rows = min(LANES, slot_total - t * LANES)
        cb[t * LANES : t * LANES + rows, :] = row.T.astype(jnp.int32)[:rows]
    local = pairs_v[4:5, :]
    for side, codes in enumerate((local, inverse_code(local))):
        for t in range(pair_total // LANES):
            row = codes[:, t * LANES : (t + 1) * LANES].astype(jnp.float32)
            start = slot_total + side * pair_total + t * LANES
            cb[start : start + LANES, :] = jnp.broadcast_to(row, (LANES, LANES)).T.astype(jnp.int32)

    def cross_flux(n, carry):
        rows = pl.ds(pl.multiple_of(n * 8, 8), 8)
        codes = cb[rows, :]
        value, lift = pair_flux(own_ref[rows, :], recv_ref[rows, :], codes & 7)
        live = codes >= 8
        vb[rows, :] = jnp.where(live, value, 0.0)
        hb[rows, :] = jnp.where(live, lift, 0.0)
        return carry

    lax.fori_loop(0, slot_total // 8, cross_flux, 0, unroll=2)

    def local_flux(n, carry):
        first = pl.ds(pl.multiple_of(n * 8, 8), 8)
        second = pl.ds(pl.multiple_of(n * 8 + pair_total, 8), 8)
        for own, peer in ((first, second), (second, first)):
            rows = pl.ds(pl.multiple_of(own.start + slot_total, 8), 8)
            value, lift = pair_flux(lb[own, :], lb[peer, :], cb[rows, :])
            vb[rows, :] = value
            hb[rows, :] = lift
        return carry

    lax.fori_loop(0, pair_total // 8, local_flux, 0)

    def scatter_cross(c, carry):
        row = slots[1, 0, c] * elems + slots[0, 0, c]
        vt[pl.ds(row, 1), :] = vb[pl.ds(c, 1), :]
        lt[pl.ds(row, 1), :] = hb[pl.ds(c, 1), :]
        return carry

    lax.fori_loop(0, slot_total, scatter_cross, 0, unroll=8)

    def scatter_local(c, carry):
        first = pairs[1, c] * elems + pairs[0, c]
        second = pairs[3, c] * elems + pairs[2, c]
        one = slot_total + c
        two = one + pair_total
        vt[pl.ds(first, 1), :] = vb[pl.ds(one, 1), :]
        lt[pl.ds(first, 1), :] = hb[pl.ds(one, 1), :]
        vt[pl.ds(second, 1), :] = vb[pl.ds(two, 1), :]
        lt[pl.ds(second, 1), :] = hb[pl.ds(two, 1), :]
        return carry

    lax.fori_loop(0, pair_total, scatter_local, 0, unroll=4)

    def turn(face, carry):
        for t in range(elems // LANES):
            rows = pl.ds(pl.multiple_of(face * elems + t * LANES, LANES), LANES)
            cols = slice(t * LANES, (t + 1) * LANES)
            value = vt[rows, :].T
            lift = lt[rows, :].T
            for f in range(fields):
                fv[f, face, :, cols] = value[f * FACE : (f + 1) * FACE]
                fl[f, face, :, cols] = lift[f * FACE : (f + 1) * FACE]
        return carry

    lax.fori_loop(0, 6, turn, 0)

    half = elems // 2

    def finish(n, carry):
        f = n // 2
        cols = pl.ds(pl.multiple_of((n % 2) * half, half), half)
        low_lift = fl[f, 0, :, cols]
        high_lift = fl[f, 1, :, cols]
        coarse = [None, None]
        for i in range(NODES):
            part = slice(i * NODES, (i + 1) * NODES)
            stack = []
            for face in range(2, 6):
                stack += [fv[f, face, part, cols], fl[f, face, part, cols]]
            value = rhs_ref[f, i, :, cols] - vol_ref[f, i, :, cols]
            value = value - product(lift_ref[...], jnp.concatenate(stack, axis=0))
            value = value + float(DERIV[0, i]) * low_lift - float(DERIV[-1, i]) * high_lift
            if i == 0:
                value = value - fv[f, 0, :, cols]
            if i == NODES - 1:
                value = value - fv[f, 1, :, cols]
            res_ref[f, i, :, cols] = value
            for a in range(2):
                if MODES[i, a] != 0.0:
                    term = float(MODES[i, a]) * value
                    coarse[a] = term if coarse[a] is None else coarse[a] + term
        for a in range(2):
            for b in range(2):
                layers = [coarse[a][j * NODES : (j + 1) * NODES] for j in range(NODES)]
                level = weighted(MODES[:, b], layers)
                for c in range(2):
                    column = modes_ref[c * NODES : (c + 1) * NODES, 0:1]
                    row = f * NODES + 4 * a + 2 * b + c
                    cs[pl.ds(row, 1), cols] = jnp.sum(level * column, axis=0, keepdims=True)
        return carry

    lax.fori_loop(0, 2 * fields, finish, 0)

    row_cells = sums_ref.shape[1]
    hot = lax.broadcasted_iota(jnp.int32, (row_cells, elems), 0) == cells_ref[...]
    hot = hot.astype(jnp.float32).astype(jnp.bfloat16)
    coarse = cs[...]
    high = coarse.astype(jnp.bfloat16)
    low = (coarse - high.astype(jnp.float32)).astype(jnp.bfloat16)
    both = lax.dot_general(
        jnp.concatenate([high, low], axis=0),
        hot,
        (((1,), (1,)), ((), ())),
        preferred_element_type=jnp.float32,
    )
    sums_ref[...] = both[: coarse.shape[0]] + both[coarse.shape[0] :]


def reduce_kernel(n_sub, sums_ref, total_ref, box, send_sem, recv_sem):
    place = lax.axis_index("blk")
    sub = lax.axis_index("sub")
    barrier = pltpu.get_barrier_semaphore()
    peers = [(place, lax.rem(sub + step, n_sub)) for step in range(1, n_sub)]
    for peer in peers:
        pl.semaphore_signal(barrier, inc=1, device_id=peer, device_id_type=MESH)
    pl.semaphore_wait(barrier, n_sub - 1)
    copies = []
    for step, peer in enumerate(peers):
        copies.append(
            pltpu.make_async_remote_copy(
                src_ref=sums_ref,
                dst_ref=box.at[step],
                send_sem=send_sem.at[step],
                recv_sem=recv_sem.at[step],
                device_id=peer,
                device_id_type=MESH,
            )
        )
        copies[-1].start()
    for copy in copies:
        copy.wait()
    total = sums_ref[...]
    for step in range(n_sub - 1):
        total = total + box[step]
    total_ref[...] = total


def correct_kernel(total_ref, inverse_ref, cells_ref, modes_ref, p_ref, out_ref):
    fields = p_ref.shape[0]
    elems = p_ref.shape[-1]
    row_cells = total_ref.shape[1]
    rows = []
    for f in range(fields):
        level = None
        for j in range(NODES):
            term = inverse_ref[j] * total_ref[f * NODES + j : f * NODES + j + 1, :]
            level = term if level is None else level + term
        rows.append(level)
    level = jnp.concatenate(rows, axis=0)
    high = level.astype(jnp.bfloat16)
    low = (level - high.astype(jnp.float32)).astype(jnp.bfloat16)
    hot = lax.broadcasted_iota(jnp.int32, (row_cells, elems), 0) == cells_ref[...]
    hot = hot.astype(jnp.float32).astype(jnp.bfloat16)
    spread = lax.dot_general(
        jnp.concatenate([high, low], axis=0),
        hot,
        (((1,), (0,)), ((), ())),
        preferred_element_type=jnp.float32,
    )
    spread = spread[: level.shape[0]] + spread[level.shape[0] :]
    columns = [modes_ref[c * NODES : (c + 1) * NODES, 0:1] for c in range(2)]
    for f in range(fields):
        planes = []
        for a in range(2):
            lines = []
            for b in range(2):
                start = f * NODES + 4 * a + 2 * b
                lines.append(
                    columns[0] * spread[start : start + 1] + columns[1] * spread[start + 1 : start + 2]
                )
            planes.append([weighted(MODES[j], lines) for j in range(NODES)])
        for j in range(NODES):
            part = slice(j * NODES, (j + 1) * NODES)
            for i in range(NODES):
                grown = weighted(MODES[i], [planes[0][j], planes[1][j]])
                out_ref[f, i, part, :] = p_ref[f, i, part, :] + grown


def whole(shape, space=VMEM):
    return pl.BlockSpec(shape, lambda *_: (0,) * len(shape), memory_space=space)


def limits(mib, **extra):
    return pltpu.CompilerParams(vmem_limit_bytes=mib << 20, **extra)


def shaped(*shape):
    return jax.ShapeDtypeStruct(shape, jnp.float32)


def on_device(
    n_blk,
    n_sub,
    pressure,
    right_side,
    geometry,
    face_weight,
    face_metric,
    cross_slots,
    local_pairs,
    coarse_map,
    coarse_inverse,
):
    fields = pressure.shape[0]
    elems = pressure.shape[-1]
    slot_total = cross_slots.shape[2]
    pair_total = local_pairs.shape[1]
    row_cells = coarse_inverse.shape[-1]
    tiles = elems // LANES
    record = 3 * LANES
    slabs = (fields, NODES, FACE, elems)
    flat_p = pressure.reshape(fields * BRICK, elems)
    p = pressure.reshape(slabs)
    weights = jnp.transpose(face_weight, (1, 0, 2))
    metrics = jnp.transpose(face_metric, (1, 0, 2))
    cells = coarse_map.reshape(1, elems)
    modes = jnp.asarray(np.repeat(MODES.T.reshape(2 * NODES, 1), LANES, axis=1), jnp.float32)

    table, send = pl.pallas_call(
        pack_kernel,
        grid=(tiles,),
        in_specs=[
            whole(cross_slots.shape, SMEM),
            pl.BlockSpec((fields * BRICK, LANES), lambda t: (0, t)),
            pl.BlockSpec((6, FACE, LANES), lambda t: (0, 0, t)),
            pl.BlockSpec((6, FACE, LANES), lambda t: (0, 0, t)),
        ],
        out_specs=[whole((6 * elems, record)), whole((slot_total, record))],
        out_shape=[shaped(6 * elems, record), shaped(slot_total, record)],
        compiler_params=limits(32),
        name="pack",
    )(cross_slots, flat_p, weights, metrics)

    received = pl.pallas_call(
        functools.partial(exchange_kernel, n_blk, n_sub),
        in_specs=[pl.BlockSpec(memory_space=VMEM)],
        out_specs=pl.BlockSpec(memory_space=VMEM),
        out_shape=shaped(slot_total, record),
        scratch_shapes=[pltpu.SemaphoreType.DMA((9,)), pltpu.SemaphoreType.DMA((9,))],
        compiler_params=limits(8, collective_id=0, has_side_effects=True),
        name="exchange",
    )(send)

    chunk = min(elems, 256)
    volume = pl.pallas_call(
        volume_kernel,
        grid=(elems // chunk,),
        in_specs=[
            pl.BlockSpec((fields, NODES, FACE, chunk), lambda t: (0, 0, 0, t)),
            pl.BlockSpec((6, NODES, FACE, chunk), lambda t: (0, 0, 0, t)),
            whole((2 * FACE, 3 * FACE)),
            whole((FACE, 6 * FACE)),
        ],
        out_specs=pl.BlockSpec((fields, NODES, FACE, chunk), lambda t: (0, 0, 0, t)),
        out_shape=shaped(*slabs),
        scratch_shapes=[pltpu.VMEM((fields, NODES, FACE, chunk), jnp.float32)],
        compiler_params=limits(32),
        name="volume",
    )(p, geometry.reshape(6, NODES, FACE, elems), jnp.asarray(forward_table()), jnp.asarray(backward_table()))

    pad_width = -(-slot_total // LANES) * LANES
    side_total = slot_total + 2 * pair_total
    residual, sums = pl.pallas_call(
        combine_kernel,
        in_specs=[
            pl.BlockSpec(memory_space=SMEM),
            pl.BlockSpec(memory_space=SMEM),
        ]
        + [pl.BlockSpec(memory_space=VMEM)] * 10,
        out_specs=[pl.BlockSpec(memory_space=VMEM)] * 2,
        out_shape=[shaped(*slabs), shaped(fields * NODES, row_cells)],
        scratch_shapes=[
            pltpu.VMEM((6 * elems, LANES), jnp.float32),
            pltpu.VMEM((6 * elems, LANES), jnp.float32),
            pltpu.VMEM((2 * pair_total, record), jnp.float32),
            pltpu.VMEM((side_total, LANES), jnp.float32),
            pltpu.VMEM((side_total, LANES), jnp.float32),
            pltpu.VMEM((side_total, LANES), jnp.int32),
            pltpu.VMEM((8, pad_width), jnp.float32),
            pltpu.VMEM((fields, 6, FACE, elems), jnp.float32),
            pltpu.VMEM((fields, 6, FACE, elems), jnp.float32),
            pltpu.VMEM((fields * NODES, elems), jnp.float32),
        ],
        compiler_params=limits(48),
        name="combine",
    )(
        cross_slots, local_pairs, cross_slots, local_pairs, send, received, table, volume,
        right_side.reshape(slabs), jnp.asarray(lift_table()), modes, cells,
    )

    totals = pl.pallas_call(
        functools.partial(reduce_kernel, n_sub),
        in_specs=[pl.BlockSpec(memory_space=VMEM)],
        out_specs=pl.BlockSpec(memory_space=VMEM),
        out_shape=shaped(fields * NODES, row_cells),
        scratch_shapes=[
            pltpu.VMEM((n_sub - 1, fields * NODES, row_cells), jnp.float32),
            pltpu.SemaphoreType.DMA((n_sub - 1,)),
            pltpu.SemaphoreType.DMA((n_sub - 1,)),
        ],
        compiler_params=limits(8, collective_id=1, has_side_effects=True),
        name="reduce",
    )(sums)

    corrected = pl.pallas_call(
        correct_kernel,
        grid=(elems // chunk,),
        in_specs=[
            whole((fields * NODES, row_cells)),
            whole((NODES, NODES, row_cells)),
            pl.BlockSpec((1, chunk), lambda t: (0, t)),
            whole((2 * NODES, LANES)),
            pl.BlockSpec((fields, NODES, FACE, chunk), lambda t: (0, 0, 0, t)),
        ],
        out_specs=pl.BlockSpec((fields, NODES, FACE, chunk), lambda t: (0, 0, 0, t)),
        out_shape=shaped(*slabs),
        compiler_params=limits(32),
        name="correct",
    )(totals, coarse_inverse, cells, modes, p)
    return residual.reshape(pressure.shape), corrected.reshape(pressure.shape)


def solution(mesh):
    return jax.shard_map(
        functools.partial(on_device, mesh.shape["blk"], mesh.shape["sub"]),
        mesh=mesh,
        in_specs=(
            P(None, None, None, None, ("blk", "sub")),
            P(None, None, None, None, ("blk", "sub")),
            P(None, None, None, None, ("blk", "sub")),
            P(None, None, ("blk", "sub")),
            P(None, None, ("blk", "sub")),
            P(None, ("blk", "sub"), None),
            P(None, ("blk", "sub")),
            P(("blk", "sub")),
            P(None, None, "blk"),
        ),
        out_specs=(
            P(None, None, None, None, ("blk", "sub")),
            P(None, None, None, None, ("blk", "sub")),
        ),
        check_vma=False,
    )
```

```python
import functools

import jax
import jax.numpy as jnp
import numpy as np
from jax import lax
from jax.experimental import pallas as pl
from jax.experimental.pallas import tpu as pltpu
from jax.sharding import PartitionSpec as P

NODES = 8
FACE = NODES * NODES
BRICK = NODES * FACE
LANES = 128
MESH = pl.DeviceIdType.MESH
VMEM = pltpu.MemorySpace.VMEM
SMEM = pltpu.MemorySpace.SMEM


def node_points():
    positive = [0.2092992179024789, 0.5917001814331423, 0.8717401485096066, 1.0]
    return np.array(sorted([-entry for entry in positive] + positive))


def derivative_matrix():
    points = node_points()
    count = len(points)
    weights = np.array(
        [
            1.0 / np.prod([points[row] - points[col] for col in range(count) if col != row])
            for row in range(count)
        ]
    )
    matrix = np.zeros((count, count))
    for row in range(count):
        for col in range(count):
            if row != col:
                matrix[row, col] = weights[col] / weights[row] / (points[row] - points[col])
        matrix[row, row] = -np.sum(matrix[row])
    return matrix


DERIV = derivative_matrix()
POINTS = node_points()
MODES = np.stack([(1.0 - POINTS) / 2.0, (1.0 + POINTS) / 2.0], axis=1)


def split_constant(matrix):
    high = matrix.astype(jnp.bfloat16)
    low = (matrix - high.astype(np.float64)).astype(jnp.bfloat16)
    return np.concatenate([high, low, high], axis=1)


def forward_table():
    eye = np.eye(NODES)
    return split_constant(np.kron(eye, DERIV))


def backward_table():
    eye = np.eye(NODES)
    return split_constant(np.kron(eye, DERIV.T))


def lift_table():
    eye = np.eye(NODES)
    rows = [eye[:, :1], -DERIV[:1].T, eye[:, -1:], DERIV[-1:].T]
    second = [np.kron(row, eye) for row in rows]
    third = [np.kron(eye, row) for row in rows]
    return split_constant(np.concatenate(second + third, axis=1))


def split_rows(values):
    high = values.astype(jnp.bfloat16)
    low = (values - high.astype(jnp.float32)).astype(jnp.bfloat16)
    return jnp.concatenate([high, high, low], axis=0)


def product(table, values):
    return lax.dot_general(
        table, split_rows(values), (((1,), (0,)), ((), ())), preferred_element_type=jnp.float32
    )


def even_odd(matrix, layers):
    half = NODES // 2
    sums = [layers[k] + layers[NODES - 1 - k] for k in range(half)]
    gaps = [layers[k] - layers[NODES - 1 - k] for k in range(half)]
    result = [None] * NODES
    for row in range(half):
        even = None
        odd = None
        for k in range(half):
            first = float((matrix[row, k] + matrix[row, NODES - 1 - k]) / 2)
            second = float((matrix[row, k] - matrix[row, NODES - 1 - k]) / 2)
            even = first * sums[k] if even is None else even + first * sums[k]
            odd = second * gaps[k] if odd is None else odd + second * gaps[k]
        result[row] = odd + even
        result[NODES - 1 - row] = odd - even
    return result


def weighted(coefficients, layers):
    total = None
    for factor, layer in zip(coefficients, layers):
        term = float(factor) * layer
        total = term if total is None else total + term
    return total


def inverse_code(code):
    swapped = 4 + 2 * (code & 1) + ((code >> 1) & 1)
    return jnp.where((code & 4) != 0, swapped, code)


def lane_pick(values, index):
    return jnp.take_along_axis(values, index, axis=1, mode="promise_in_bounds")


def pair_flux(own, peer, code):
    v1, g1, wm1 = own
    v2, g2, wm2 = peer
    lane = lax.broadcasted_iota(jnp.int32, code.shape, 1)
    node = lane & (FACE - 1)
    swapped = ((node & (NODES - 1)) << 3) | (node >> 3)
    source = jnp.where((code & 4) != 0, swapped, node)
    source = source ^ ((code & 1) * 56) ^ (((code >> 1) & 1) * 7)
    both = source | (lane & FACE)
    v2 = lane_pick(v2, both)
    g2 = lane_pick(g2, both)
    w2 = lane_pick(wm2, source)
    m2 = lane_pick(wm2, source + FACE)
    w1 = lane_pick(wm1, node)
    m1 = lane_pick(wm1, node + FACE)
    penalty = NODES * (NODES + 1) / 2.0
    jump = v1 - v2
    weight = 0.5 * (w1 + w2)
    tau = (penalty * 0.5) * (m1 + m2)
    value = weight * (tau * jump - 0.5 * (g1 - g2))
    lift = (-0.5 * weight * jump) * m1
    return value, lift


def row_numbers(slots, pairs, elems, staged, rows, sem):
    staged[0][...] = slots[1] * elems + slots[0]
    staged[1][...] = pairs[1:2] * elems + pairs[0:1]
    staged[2][...] = pairs[3:4] * elems + pairs[2:3]
    return [pltpu.make_async_copy(staged[n], rows[n], sem.at[n]) for n in range(3)]


def code_rows(slots, pairs, pad, cb):
    slot_total = slots.shape[2]
    pair_total = pairs.shape[1]
    raw = slots[4]
    code = jnp.where(slots[3] != 0, raw, inverse_code(raw)) + 8 * slots[2]
    pad[0:1, 0:slot_total] = code.astype(jnp.float32)
    pad[0:1, slot_total:] = jnp.zeros((1, pad.shape[1] - slot_total), jnp.float32)
    for t in range(pad.shape[1] // LANES):
        row = jnp.broadcast_to(pad[0:1, t * LANES : (t + 1) * LANES], (LANES, LANES))
        count = min(LANES, slot_total - t * LANES)
        cb[t * LANES : t * LANES + count, :] = row.T.astype(jnp.int32)[:count]
    local = pairs[4:5, :]
    for side, codes in enumerate((local, inverse_code(local))):
        for t in range(pair_total // LANES):
            row = codes[:, t * LANES : (t + 1) * LANES].astype(jnp.float32)
            start = slot_total + side * pair_total + t * LANES
            cb[start : start + LANES, :] = jnp.broadcast_to(row, (LANES, LANES)).T.astype(jnp.int32)


def aligned(start, size):
    return pl.ds(pl.multiple_of(start, size), size)


def trace_tile(t, elems, p_s, fw_s, fm_s, tables):
    fields = p_s.shape[1] // BRICK
    for axis in range(3):
        values = []
        slopes = []
        for field in range(fields):
            start = field * BRICK
            layers = []
            for k in range(NODES):
                if axis == 0:
                    layers.append(p_s[t, start + k * FACE : start + (k + 1) * FACE, :])
                elif axis == 1:
                    rows = [
                        p_s[t, start + i * FACE + k * NODES : start + i * FACE + (k + 1) * NODES, :]
                        for i in range(NODES)
                    ]
                    layers.append(jnp.concatenate(rows, axis=0))
                else:
                    layers.append(p_s[t, pl.ds(start + k, FACE, stride=NODES), :])
            values.append((layers[0], layers[-1]))
            slopes.append((weighted(-DERIV[0], layers), weighted(DERIV[-1], layers)))
        for side in range(2):
            face = 2 * axis + side
            metric = fm_s[t, face]
            rows = aligned(face * elems + t * LANES, LANES)
            value = jnp.concatenate([entry[side] for entry in values], axis=0)
            slope = jnp.concatenate([entry[side] * metric for entry in slopes], axis=0)
            tables[0][rows, :] = value.T
            tables[1][rows, :] = slope.T
            tables[2][rows, :] = jnp.concatenate([fw_s[t, face], metric], axis=0).T


def volume_half(h, p_s, g_s, fwd, bwd, out, s_ref):
    fields = p_s.shape[1] // BRICK
    tiles = (2 * h, 2 * h + 1)

    def wide(ref, rows):
        return jnp.concatenate([ref[tiles[0], rows, :], ref[tiles[1], rows, :]], axis=1)

    def first(n, carry):
        f = n // NODES
        r = n % NODES
        where = [aligned(f * BRICK + k * FACE + r * NODES, NODES) for k in range(NODES)]
        for q, value in enumerate(even_odd(DERIV, [wide(p_s, rows) for rows in where])):
            s_ref[where[q], :] = value
        return carry

    lax.fori_loop(0, fields * NODES, first, 0, unroll=4)

    def middle(i, carry):
        g = [wide(g_s, aligned(n * BRICK + i * FACE, FACE)) for n in range(6)]
        for f in range(fields):
            rows = aligned(f * BRICK + i * FACE, FACE)
            x = wide(p_s, rows)
            s3 = product(fwd[...], x)
            s2 = jnp.concatenate(
                even_odd(DERIV, [x[j * NODES : (j + 1) * NODES] for j in range(NODES)]), axis=0
            )
            s1 = s_ref[rows, :]
            q1 = g[0] * s1 + g[3] * s2 + g[4] * s3
            q2 = g[3] * s1 + g[1] * s2 + g[5] * s3
            q3 = g[4] * s1 + g[5] * s2 + g[2] * s3
            s_ref[rows, :] = q1
            r2 = jnp.concatenate(
                even_odd(DERIV.T, [q2[j * NODES : (j + 1) * NODES] for j in range(NODES)]), axis=0
            )
            r23 = product(bwd[...], q3) + r2
            out[tiles[0], rows, :] = r23[:, :LANES]
            out[tiles[1], rows, :] = r23[:, LANES:]
        return carry

    lax.fori_loop(0, NODES, middle, 0, unroll=4)

    def last(n, carry):
        f = n // NODES
        r = n % NODES
        where = [aligned(f * BRICK + k * FACE + r * NODES, NODES) for k in range(NODES)]
        for q, value in enumerate(even_odd(DERIV.T, [s_ref[rows, :] for rows in where])):
            out[tiles[0], where[q], :] += value[:, :LANES]
            out[tiles[1], where[q], :] += value[:, LANES:]
        return carry

    lax.fori_loop(0, fields * NODES, last, 0, unroll=4)


def front_kernel(
    n_blk, n_sub,
    slots, pairs, p_hbm, fw_hbm, fm_hbm, g_hbm, fwd, bwd,
    vol, vb, hb,
    p_s, fw_s, fm_s, g_s, s_ref, tv, tg, tw, la, lb, lc, cb, pad, send, recv,
    st0, st1, st2, rw0, rw1, rw2,
    load_sem, geo_sem, row_sem, send_sem, recv_sem,
):
    elems = tv.shape[0] // 6
    tiles = elems // LANES
    slot_total = slots.shape[2]
    pair_total = pairs.shape[1]
    width = slot_total // 9
    tables = (tv, tg, tw)
    locals_ = (la, lb, lc)
    place = lax.axis_index("blk")
    sub = lax.axis_index("sub")

    def peer(k):
        return (
            lax.rem(place + (k // 3 - 1) + n_blk, n_blk),
            lax.rem(sub + (k % 3 - 1) + n_sub, n_sub),
        )

    others = [0, 2, 6, 8, 1, 7, 3, 5]
    loads = []
    for t in range(tiles):
        cols = pl.ds(t * LANES, LANES)
        loads.append(
            [
                pltpu.make_async_copy(p_hbm.at[:, cols], p_s.at[t], load_sem.at[t, 0]),
                pltpu.make_async_copy(fw_hbm.at[:, :, cols], fw_s.at[t], load_sem.at[t, 1]),
                pltpu.make_async_copy(fm_hbm.at[:, :, cols], fm_s.at[t], load_sem.at[t, 2]),
            ]
        )
        for copy in loads[-1]:
            copy.start()
    geo = []
    for t in range(tiles):
        cols = pl.ds(t * LANES, LANES)
        geo.append(pltpu.make_async_copy(g_hbm.at[:, cols], g_s.at[t], geo_sem.at[t]))
        geo[-1].start()
    barrier = pltpu.get_barrier_semaphore()
    for k in others:
        pl.semaphore_signal(barrier, inc=1, device_id=peer(k), device_id_type=MESH)
    numbers = row_numbers(slots, pairs, elems, (st0, st1, st2), (rw0, rw1, rw2), row_sem)
    for copy in numbers:
        copy.start()
    code_rows(slots, pairs, pad, cb)
    for t in range(tiles):
        for copy in loads[t]:
            copy.wait()
        trace_tile(t, elems, p_s, fw_s, fm_s, tables)
    for copy in numbers:
        copy.wait()
    pl.semaphore_wait(barrier, len(others))
    copies = []
    for k in others:

        def gather(n, carry, k=k):
            base = n * 16
            rows = [rw0[0, k * width + base + u] for u in range(16)]
            for j in range(3):
                found = [tables[j][pl.ds(row, 1), :] for row in rows]
                for u in range(16):
                    send[k, j, pl.ds(base + u, 1), :] = found[u]
            return carry

        lax.fori_loop(0, width // 16, gather, 0)
        copies.append(
            pltpu.make_async_remote_copy(
                src_ref=send.at[k],
                dst_ref=recv.at[8 - k],
                send_sem=send_sem.at[k],
                recv_sem=recv_sem.at[8 - k],
                device_id=peer(k),
                device_id_type=MESH,
            )
        )
        copies[-1].start()

    for side, numbers in enumerate((rw1, rw2)):

        def gather_local(n, carry, side=side, numbers=numbers):
            base = n * 16
            rows = [numbers[0, base + u] for u in range(16)]
            for j in range(3):
                found = [tables[j][pl.ds(row, 1), :] for row in rows]
                for u in range(16):
                    locals_[j][pl.ds(side * pair_total + base + u, 1), :] = found[u]
            return carry

        lax.fori_loop(0, pair_total // 16, gather_local, 0)

    def local_flux(n, carry):
        own = aligned(n * LANES, LANES)
        other = aligned((n * LANES + pair_total) % (2 * pair_total), LANES)
        rows = aligned(n * LANES + slot_total, FACE)
        rows = pl.ds(rows.start, LANES)
        value, lift = pair_flux(
            [table[own, :] for table in locals_], [table[other, :] for table in locals_], cb[rows, :]
        )
        vb[rows, :] = value
        hb[rows, :] = lift
        return carry

    lax.fori_loop(0, 2 * pair_total // LANES, local_flux, 0)
    for copy in geo:
        copy.wait()

    def volume(h, carry):
        volume_half(h, p_s, g_s, fwd, bwd, vol, s_ref)
        return carry

    lax.fori_loop(0, tiles // 2, volume, 0)
    for copy in copies:
        copy.wait()

    def cross_flux(n, carry):
        for shift in (0, 5):
            k = n + shift
            rows = aligned(k * width, FACE)
            codes = cb[rows, :]
            value, lift = pair_flux(
                [send[k, j] for j in range(3)], [recv[k, j] for j in range(3)], codes & 7
            )
            live = codes >= 8
            vb[rows, :] = jnp.where(live, value, 0.0)
            hb[rows, :] = jnp.where(live, lift, 0.0)
        return carry

    lax.fori_loop(0, 4, cross_flux, 0)
    vb[4 * width : 5 * width, :] = jnp.zeros((width, LANES), jnp.float32)
    hb[4 * width : 5 * width, :] = jnp.zeros((width, LANES), jnp.float32)


def combine_kernel(
    slots, pairs, vb, hb, vol, rhs, lift_ref, modes, cells,
    res, sums,
    vt, lt, fv, fl, cs, st0, st1, st2, rw0, rw1, rw2, row_sem,
):
    elems = vt.shape[0] // 6
    tiles = elems // LANES
    slot_total = slots.shape[2]
    pair_total = pairs.shape[1]
    fields = 2
    numbers = row_numbers(slots, pairs, elems, (st0, st1, st2), (rw0, rw1, rw2), row_sem)
    for copy in numbers:
        copy.start()

    def clear(n, carry):
        rows = aligned(n * LANES, LANES)
        zero = jnp.zeros((LANES, LANES), jnp.float32)
        vt[rows, :] = zero
        lt[rows, :] = zero
        return carry

    lax.fori_loop(0, vt.shape[0] // LANES, clear, 0)
    for copy in numbers:
        copy.wait()
    for start, count, numbers in (
        (0, slot_total, rw0),
        (slot_total, pair_total, rw1),
        (slot_total + pair_total, pair_total, rw2),
    ):

        def scatter(n, carry, start=start, numbers=numbers):
            base = n * 16
            rows = [numbers[0, base + u] for u in range(16)]
            for source, table in ((vb, vt), (hb, lt)):
                found = [source[pl.ds(start + base + u, 1), :] for u in range(16)]
                for u in range(16):
                    table[pl.ds(rows[u], 1), :] = found[u]
            return carry

        lax.fori_loop(0, count // 16, scatter, 0)

    for face in range(6):
        for t in range(tiles):
            rows = slice(face * elems + t * LANES, face * elems + (t + 1) * LANES)
            value = vt[rows, :].T
            lift = lt[rows, :].T
            for f in range(fields):
                fv[t, f, face] = value[f * FACE : (f + 1) * FACE]
                fl[t, f, face] = lift[f * FACE : (f + 1) * FACE]

    half = 2 * LANES

    def finish(n, carry):
        f = n // (tiles // 2)
        h = n % (tiles // 2)
        cols = aligned(h * half, half)

        def wide(ref, *where):
            return jnp.concatenate([ref[2 * h, *where], ref[2 * h + 1, *where]], axis=-1)

        low_lift = wide(fl, f, 0)
        high_lift = wide(fl, f, 1)
        coarse = [None, None]
        for i in range(NODES):
            part = slice(i * NODES, (i + 1) * NODES)
            stack = []
            for face in range(2, 6):
                stack += [wide(fv, f, face, part), wide(fl, f, face, part)]
            rows = aligned(f * BRICK + i * FACE, FACE)
            value = rhs[f, i, :, cols] - wide(vol, rows)
            value = value - product(lift_ref[...], jnp.concatenate(stack, axis=0))
            value = value + float(DERIV[0, i]) * low_lift - float(DERIV[-1, i]) * high_lift
            if i == 0:
                value = value - wide(fv, f, 0)
            if i == NODES - 1:
                value = value - wide(fv, f, 1)
            res[f, i, :, cols] = value
            for a in range(2):
                if MODES[i, a] != 0.0:
                    term = float(MODES[i, a]) * value
                    coarse[a] = term if coarse[a] is None else coarse[a] + term
        for a in range(2):
            for b in range(2):
                layers = [coarse[a][j * NODES : (j + 1) * NODES] for j in range(NODES)]
                level = weighted(MODES[:, b], layers)
                for c in range(2):
                    column = modes[c * NODES : (c + 1) * NODES, 0:1]
                    row = f * NODES + 4 * a + 2 * b + c
                    cs[pl.ds(row, 1), cols] = jnp.sum(level * column, axis=0, keepdims=True)
        return carry

    lax.fori_loop(0, fields * tiles // 2, finish, 0)

    row_cells = sums.shape[1]
    hot = lax.broadcasted_iota(jnp.int32, (row_cells, elems), 0) == cells[...]
    hot = hot.astype(jnp.float32).astype(jnp.bfloat16)
    coarse = cs[...]
    high = coarse.astype(jnp.bfloat16)
    low = (coarse - high.astype(jnp.float32)).astype(jnp.bfloat16)
    both = lax.dot_general(
        jnp.concatenate([high, low], axis=0),
        hot,
        (((1,), (1,)), ((), ())),
        preferred_element_type=jnp.float32,
    )
    sums[...] = both[: coarse.shape[0]] + both[coarse.shape[0] :]


def reduce_kernel(n_sub, sums_ref, total_ref, box, send_sem, recv_sem):
    place = lax.axis_index("blk")
    sub = lax.axis_index("sub")
    barrier = pltpu.get_barrier_semaphore()
    peers = [(place, lax.rem(sub + step, n_sub)) for step in range(1, n_sub)]
    for peer in peers:
        pl.semaphore_signal(barrier, inc=1, device_id=peer, device_id_type=MESH)
    pl.semaphore_wait(barrier, n_sub - 1)
    copies = []
    for step, peer in enumerate(peers):
        copies.append(
            pltpu.make_async_remote_copy(
                src_ref=sums_ref,
                dst_ref=box.at[step],
                send_sem=send_sem.at[step],
                recv_sem=recv_sem.at[step],
                device_id=peer,
                device_id_type=MESH,
            )
        )
        copies[-1].start()
    for copy in copies:
        copy.wait()
    total = sums_ref[...]
    for step in range(n_sub - 1):
        total = total + box[step]
    total_ref[...] = total


def correct_kernel(total_ref, inverse_ref, cells_ref, modes_ref, p_ref, out_ref):
    fields = p_ref.shape[0]
    elems = p_ref.shape[-1]
    row_cells = total_ref.shape[1]
    rows = []
    for f in range(fields):
        level = None
        for j in range(NODES):
            term = inverse_ref[j] * total_ref[f * NODES + j : f * NODES + j + 1, :]
            level = term if level is None else level + term
        rows.append(level)
    level = jnp.concatenate(rows, axis=0)
    high = level.astype(jnp.bfloat16)
    low = (level - high.astype(jnp.float32)).astype(jnp.bfloat16)
    hot = lax.broadcasted_iota(jnp.int32, (row_cells, elems), 0) == cells_ref[...]
    hot = hot.astype(jnp.float32).astype(jnp.bfloat16)
    spread = lax.dot_general(
        jnp.concatenate([high, low], axis=0),
        hot,
        (((1,), (0,)), ((), ())),
        preferred_element_type=jnp.float32,
    )
    spread = spread[: level.shape[0]] + spread[level.shape[0] :]
    columns = [modes_ref[c * NODES : (c + 1) * NODES, 0:1] for c in range(2)]
    for f in range(fields):
        planes = []
        for a in range(2):
            lines = []
            for b in range(2):
                start = f * NODES + 4 * a + 2 * b
                lines.append(
                    columns[0] * spread[start : start + 1] + columns[1] * spread[start + 1 : start + 2]
                )
            planes.append([weighted(MODES[j], lines) for j in range(NODES)])
        for j in range(NODES):
            part = slice(j * NODES, (j + 1) * NODES)
            for i in range(NODES):
                grown = weighted(MODES[i], [planes[0][j], planes[1][j]])
                out_ref[f, i, part, :] = p_ref[f, i, part, :] + grown


def whole(shape, space=VMEM):
    return pl.BlockSpec(shape, lambda *_: (0,) * len(shape), memory_space=space)


def limits(mib, **extra):
    return pltpu.CompilerParams(vmem_limit_bytes=mib << 20, **extra)


def shaped(*shape):
    return jax.ShapeDtypeStruct(shape, jnp.float32)


def on_device(
    n_blk,
    n_sub,
    pressure,
    right_side,
    geometry,
    face_weight,
    face_metric,
    cross_slots,
    local_pairs,
    coarse_map,
    coarse_inverse,
):
    fields = pressure.shape[0]
    elems = pressure.shape[-1]
    slot_total = cross_slots.shape[2]
    pair_total = local_pairs.shape[1]
    row_cells = coarse_inverse.shape[-1]
    tiles = elems // LANES
    width = slot_total // 9
    slabs = (fields, NODES, FACE, elems)
    rows = fields * BRICK
    p = pressure.reshape(slabs)
    weights = jnp.transpose(face_weight, (1, 0, 2))
    metrics = jnp.transpose(face_metric, (1, 0, 2))
    cells = coarse_map.reshape(1, elems)
    modes = jnp.asarray(np.repeat(MODES.T.reshape(2 * NODES, 1), LANES, axis=1), jnp.float32)
    pad_width = -(-slot_total // LANES) * LANES
    side_total = slot_total + 2 * pair_total
    f32 = jnp.float32
    i32 = jnp.int32
    inside = pl.BlockSpec(memory_space=VMEM)
    outside = pl.BlockSpec(memory_space=pltpu.MemorySpace.HBM)
    number_scratch = [
        pltpu.VMEM((1, slot_total), i32),
        pltpu.VMEM((1, pair_total), i32),
        pltpu.VMEM((1, pair_total), i32),
        pltpu.SMEM((1, slot_total), i32),
        pltpu.SMEM((1, pair_total), i32),
        pltpu.SMEM((1, pair_total), i32),
    ]
    dma = pltpu.SemaphoreType.DMA

    volume, values, lifts = pl.pallas_call(
        functools.partial(front_kernel, n_blk, n_sub),
        in_specs=[inside] * 2 + [outside] * 4 + [inside] * 2,
        out_specs=[inside] * 3,
        out_shape=[shaped(tiles, rows, LANES), shaped(side_total, LANES), shaped(side_total, LANES)],
        scratch_shapes=[
            pltpu.VMEM((tiles, rows, LANES), f32),
            pltpu.VMEM((tiles, 6, FACE, LANES), f32),
            pltpu.VMEM((tiles, 6, FACE, LANES), f32),
            pltpu.VMEM((tiles, 6 * BRICK, LANES), f32),
            pltpu.VMEM((rows, 2 * LANES), f32),
        ]
        + [pltpu.VMEM((6 * elems, LANES), f32)] * 3
        + [pltpu.VMEM((2 * pair_total, LANES), f32)] * 3
        + [
            pltpu.VMEM((side_total, LANES), i32),
            pltpu.VMEM((8, pad_width), f32),
            pltpu.VMEM((9, 3, width, LANES), f32),
            pltpu.VMEM((9, 3, width, LANES), f32),
        ]
        + number_scratch
        + [dma((tiles, 3)), dma((tiles,)), dma((3,)), dma((9,)), dma((9,))],
        compiler_params=limits(36, collective_id=0, has_side_effects=True),
        name="front",
    )(
        cross_slots,
        local_pairs,
        pressure.reshape(rows, elems),
        weights,
        metrics,
        geometry.reshape(6 * BRICK, elems),
        jnp.asarray(forward_table()),
        jnp.asarray(backward_table()),
    )

    residual, sums = pl.pallas_call(
        combine_kernel,
        in_specs=[inside] * 9,
        out_specs=[inside] * 2,
        out_shape=[shaped(*slabs), shaped(fields * NODES, row_cells)],
        scratch_shapes=[
            pltpu.VMEM((6 * elems, LANES), f32),
            pltpu.VMEM((6 * elems, LANES), f32),
            pltpu.VMEM((tiles, fields, 6, FACE, LANES), f32),
            pltpu.VMEM((tiles, fields, 6, FACE, LANES), f32),
            pltpu.VMEM((fields * NODES, elems), f32),
        ]
        + number_scratch
        + [dma((3,))],
        compiler_params=limits(32),
        name="combine",
    )(
        cross_slots,
        local_pairs,
        values,
        lifts,
        volume,
        right_side.reshape(slabs),
        jnp.asarray(lift_table()),
        modes,
        cells,
    )

    totals = pl.pallas_call(
        functools.partial(reduce_kernel, n_sub),
        in_specs=[inside],
        out_specs=inside,
        out_shape=shaped(fields * NODES, row_cells),
        scratch_shapes=[
            pltpu.VMEM((n_sub - 1, fields * NODES, row_cells), f32),
            dma((n_sub - 1,)),
            dma((n_sub - 1,)),
        ],
        compiler_params=limits(8, collective_id=1, has_side_effects=True),
        name="reduce",
    )(sums)

    chunk = min(elems, 256)
    corrected = pl.pallas_call(
        correct_kernel,
        grid=(elems // chunk,),
        in_specs=[
            whole((fields * NODES, row_cells)),
            whole((NODES, NODES, row_cells)),
            pl.BlockSpec((1, chunk), lambda t: (0, t)),
            whole((2 * NODES, LANES)),
            pl.BlockSpec((fields, NODES, FACE, chunk), lambda t: (0, 0, 0, t)),
        ],
        out_specs=pl.BlockSpec((fields, NODES, FACE, chunk), lambda t: (0, 0, 0, t)),
        out_shape=shaped(*slabs),
        compiler_params=limits(32),
        name="correct",
    )(totals, coarse_inverse, cells, modes, p)
    return residual.reshape(pressure.shape), corrected.reshape(pressure.shape)


def solution(mesh):
    return jax.shard_map(
        functools.partial(on_device, mesh.shape["blk"], mesh.shape["sub"]),
        mesh=mesh,
        in_specs=(
            P(None, None, None, None, ("blk", "sub")),
            P(None, None, None, None, ("blk", "sub")),
            P(None, None, None, None, ("blk", "sub")),
            P(None, None, ("blk", "sub")),
            P(None, None, ("blk", "sub")),
            P(None, ("blk", "sub"), None),
            P(None, ("blk", "sub")),
            P(("blk", "sub")),
            P(None, None, "blk"),
        ),
        out_specs=(
            P(None, None, None, None, ("blk", "sub")),
            P(None, None, None, None, ("blk", "sub")),
        ),
        check_vma=False,
    )
```

```python
import functools

import jax
import jax.numpy as jnp
import numpy as np
from jax import lax
from jax.experimental import pallas as pl
from jax.experimental.pallas import tpu as pltpu
from jax.sharding import PartitionSpec as P

NODES = 8
FACE = NODES * NODES
BRICK = NODES * FACE
LANES = 128
MESH = pl.DeviceIdType.MESH
VMEM = pltpu.MemorySpace.VMEM
SMEM = pltpu.MemorySpace.SMEM


def node_points():
    positive = [0.2092992179024789, 0.5917001814331423, 0.8717401485096066, 1.0]
    return np.array(sorted([-entry for entry in positive] + positive))


def derivative_matrix():
    points = node_points()
    count = len(points)
    weights = np.array(
        [
            1.0 / np.prod([points[row] - points[col] for col in range(count) if col != row])
            for row in range(count)
        ]
    )
    matrix = np.zeros((count, count))
    for row in range(count):
        for col in range(count):
            if row != col:
                matrix[row, col] = weights[col] / weights[row] / (points[row] - points[col])
        matrix[row, row] = -np.sum(matrix[row])
    return matrix


DERIV = derivative_matrix()
POINTS = node_points()
MODES = np.stack([(1.0 - POINTS) / 2.0, (1.0 + POINTS) / 2.0], axis=1)


def split_constant(matrix):
    high = matrix.astype(jnp.bfloat16)
    low = (matrix - high.astype(np.float64)).astype(jnp.bfloat16)
    return np.concatenate([high, low, high], axis=1)


def forward_table():
    eye = np.eye(NODES)
    return split_constant(np.kron(eye, DERIV))


def backward_table():
    eye = np.eye(NODES)
    return split_constant(np.kron(eye, DERIV.T))


def lift_table():
    eye = np.eye(NODES)
    rows = [eye[:, :1], -DERIV[:1].T, eye[:, -1:], DERIV[-1:].T]
    second = [np.kron(row, eye) for row in rows]
    third = [np.kron(eye, row) for row in rows]
    return split_constant(np.concatenate(second + third, axis=1))


def split_rows(values):
    high = values.astype(jnp.bfloat16)
    low = (values - high.astype(jnp.float32)).astype(jnp.bfloat16)
    return jnp.concatenate([high, high, low], axis=0)


def product(table, values):
    return lax.dot_general(
        table, split_rows(values), (((1,), (0,)), ((), ())), preferred_element_type=jnp.float32
    )


def even_odd(matrix, layers):
    half = NODES // 2
    sums = [layers[k] + layers[NODES - 1 - k] for k in range(half)]
    gaps = [layers[k] - layers[NODES - 1 - k] for k in range(half)]
    result = [None] * NODES
    for row in range(half):
        even = None
        odd = None
        for k in range(half):
            first = float((matrix[row, k] + matrix[row, NODES - 1 - k]) / 2)
            second = float((matrix[row, k] - matrix[row, NODES - 1 - k]) / 2)
            even = first * sums[k] if even is None else even + first * sums[k]
            odd = second * gaps[k] if odd is None else odd + second * gaps[k]
        result[row] = odd + even
        result[NODES - 1 - row] = odd - even
    return result


def weighted(coefficients, layers):
    total = None
    for factor, layer in zip(coefficients, layers):
        term = float(factor) * layer
        total = term if total is None else total + term
    return total


def inverse_code(code):
    swapped = 4 + 2 * (code & 1) + ((code >> 1) & 1)
    return jnp.where((code & 4) != 0, swapped, code)


def lane_pick(values, index):
    return jnp.take_along_axis(values, index, axis=1, mode="promise_in_bounds")


def pair_flux(own, peer, code):
    wm1, v1, g1 = own
    wm2, v2, g2 = peer
    lane = lax.broadcasted_iota(jnp.int32, code.shape, 1)
    low = lane < FACE
    node = lane & (FACE - 1)
    swapped = ((node & (NODES - 1)) << 3) | (node >> 3)
    source = jnp.where((code & 4) != 0, swapped, node)
    source = source ^ ((code & 1) * 56) ^ (((code >> 1) & 1) * 7)
    source = source | (lane & FACE)
    penalty = NODES * (NODES + 1) / 2.0
    jump = v1 - lane_pick(v2, source)
    gap = g1 - lane_pick(g2, source)
    total = wm1 + lane_pick(wm2, source)
    turned = pltpu.roll(total, FACE, 1)
    weight = 0.5 * jnp.where(low, total, turned)
    tau = (penalty * 0.5) * jnp.where(low, turned, total)
    metric = jnp.where(low, pltpu.roll(wm1, FACE, 1), wm1)
    value = weight * (tau * jump - 0.5 * gap)
    lift = (-0.5 * weight * jump) * metric
    return value, lift


def row_numbers(slots, pairs, elems, staged, rows, sem):
    staged[0][...] = slots[1] * elems + slots[0]
    staged[1][...] = pairs[1:2] * elems + pairs[0:1]
    staged[2][...] = pairs[3:4] * elems + pairs[2:3]
    return [pltpu.make_async_copy(staged[n], rows[n], sem.at[n]) for n in range(3)]


def code_rows(slots, pairs, pad, cb):
    slot_total = slots.shape[2]
    pair_total = pairs.shape[1]
    raw = slots[4]
    code = jnp.where(slots[3] != 0, raw, inverse_code(raw)) + 8 * slots[2]
    pad[0:1, 0:slot_total] = code.astype(jnp.float32)
    pad[0:1, slot_total:] = jnp.zeros((1, pad.shape[1] - slot_total), jnp.float32)
    for t in range(pad.shape[1] // LANES):
        row = jnp.broadcast_to(pad[0:1, t * LANES : (t + 1) * LANES], (LANES, LANES))
        count = min(LANES, slot_total - t * LANES)
        cb[t * LANES : t * LANES + count, :] = row.T.astype(jnp.int32)[:count]
    local = pairs[4:5, :]
    for side, codes in enumerate((local, inverse_code(local))):
        for t in range(pair_total // LANES):
            row = codes[:, t * LANES : (t + 1) * LANES].astype(jnp.float32)
            start = slot_total + side * pair_total + t * LANES
            cb[start : start + LANES, :] = jnp.broadcast_to(row, (LANES, LANES)).T.astype(jnp.int32)


def aligned(start, size):
    return pl.ds(pl.multiple_of(start, size), size)


def node_layers(t, axis, start, p_s):
    layers = []
    for k in range(NODES):
        if axis == 0:
            layers.append(p_s[t, start + k * FACE : start + (k + 1) * FACE, :])
        elif axis == 1:
            rows = [
                p_s[t, start + i * FACE + k * NODES : start + i * FACE + (k + 1) * NODES, :]
                for i in range(NODES)
            ]
            layers.append(jnp.concatenate(rows, axis=0))
        else:
            layers.append(p_s[t, pl.ds(start + k, FACE, stride=NODES), :])
    return layers


def face_rows(face, t, elems):
    return aligned(face * elems + t * LANES, LANES)


def fixed_tile(t, elems, fw_s, fm_s, table):
    for face in range(6):
        both = jnp.concatenate([fw_s[t, face], fm_s[t, face]], axis=0)
        table[face_rows(face, t, elems), :] = both.T


def value_tile(t, elems, p_s, table):
    for axis in range(3):
        for side in range(2):
            ends = []
            for start in range(0, p_s.shape[1], BRICK):
                k = side * (NODES - 1)
                if axis == 0:
                    ends.append(p_s[t, start + k * FACE : start + (k + 1) * FACE, :])
                elif axis == 1:
                    ends += [
                        p_s[t, start + i * FACE + k * NODES : start + i * FACE + (k + 1) * NODES, :]
                        for i in range(NODES)
                    ]
                else:
                    ends.append(p_s[t, pl.ds(start + k, FACE, stride=NODES), :])
            table[face_rows(2 * axis + side, t, elems), :] = jnp.concatenate(ends, axis=0).T


def slope_tile(t, elems, p_s, fm_s, table):
    for axis in range(3):
        slopes = []
        for start in range(0, p_s.shape[1], BRICK):
            layers = node_layers(t, axis, start, p_s)
            slopes.append((weighted(-DERIV[0], layers), weighted(DERIV[-1], layers)))
        for side in range(2):
            face = 2 * axis + side
            slope = jnp.concatenate([entry[side] * fm_s[t, face] for entry in slopes], axis=0)
            table[face_rows(face, t, elems), :] = slope.T


def volume_half(h, p_s, g_s, fwd, bwd, out, s_ref):
    fields = p_s.shape[1] // BRICK
    tiles = (2 * h, 2 * h + 1)

    def wide(ref, rows):
        return jnp.concatenate([ref[tiles[0], rows, :], ref[tiles[1], rows, :]], axis=1)

    def first(n, carry):
        f = n // NODES
        r = n % NODES
        where = [aligned(f * BRICK + k * FACE + r * NODES, NODES) for k in range(NODES)]
        for q, value in enumerate(even_odd(DERIV, [wide(p_s, rows) for rows in where])):
            s_ref[where[q], :] = value
        return carry

    lax.fori_loop(0, fields * NODES, first, 0, unroll=4)

    def middle(i, carry):
        g = [wide(g_s, aligned(n * BRICK + i * FACE, FACE)) for n in range(6)]
        for f in range(fields):
            rows = aligned(f * BRICK + i * FACE, FACE)
            x = wide(p_s, rows)
            s3 = product(fwd[...], x)
            s2 = jnp.concatenate(
                even_odd(DERIV, [x[j * NODES : (j + 1) * NODES] for j in range(NODES)]), axis=0
            )
            s1 = s_ref[rows, :]
            q1 = g[0] * s1 + g[3] * s2 + g[4] * s3
            q2 = g[3] * s1 + g[1] * s2 + g[5] * s3
            q3 = g[4] * s1 + g[5] * s2 + g[2] * s3
            s_ref[rows, :] = q1
            r2 = jnp.concatenate(
                even_odd(DERIV.T, [q2[j * NODES : (j + 1) * NODES] for j in range(NODES)]), axis=0
            )
            r23 = product(bwd[...], q3) + r2
            out[tiles[0], rows, :] = r23[:, :LANES]
            out[tiles[1], rows, :] = r23[:, LANES:]
        return carry

    lax.fori_loop(0, NODES, middle, 0, unroll=4)

    def last(n, carry):
        f = n // NODES
        r = n % NODES
        where = [aligned(f * BRICK + k * FACE + r * NODES, NODES) for k in range(NODES)]
        for q, value in enumerate(even_odd(DERIV.T, [s_ref[rows, :] for rows in where])):
            out[tiles[0], where[q], :] += value[:, :LANES]
            out[tiles[1], where[q], :] += value[:, LANES:]
        return carry

    lax.fori_loop(0, fields * NODES, last, 0, unroll=4)


def front_kernel(
    n_blk, n_sub,
    slots_hbm, pairs_hbm, p_hbm, fw_hbm, fm_hbm, g_hbm, fwd_hbm, bwd_hbm,
    vol, vb, hb,
    slots, pairs, fwd, bwd, p_s, fw_s, fm_s, g_s, s_ref, tv, tg, tw, la, lb, lc, cb, pad, send, recv,
    st0, st1, st2, rw0, rw1, rw2,
    small_sem, load_sem, geo_sem, row_sem, send_sem, recv_sem,
):
    elems = tv.shape[0] // 6
    tiles = elems // LANES
    slot_total = slots.shape[2]
    pair_total = pairs.shape[1]
    width = slot_total // 9
    tables = (tw, tv, tg)
    locals_ = (la, lb, lc)
    place = lax.axis_index("blk")
    sub = lax.axis_index("sub")

    def peer(k):
        return (
            lax.rem(place + (k // 3 - 1) + n_blk, n_blk),
            lax.rem(sub + (k % 3 - 1) + n_sub, n_sub),
        )

    others = [2, 0, 8, 6, 5, 3, 1, 7]
    small = [
        pltpu.make_async_copy(source, target, small_sem.at[n])
        for n, (source, target) in enumerate(
            ((slots_hbm, slots), (pairs_hbm, pairs), (fwd_hbm, fwd), (bwd_hbm, bwd))
        )
    ]
    for copy in small[:2]:
        copy.start()
    loads = []
    for t in range(tiles):
        cols = pl.ds(t * LANES, LANES)
        loads.append(
            [
                pltpu.make_async_copy(fw_hbm.at[:, :, cols], fw_s.at[t], load_sem.at[t, 0]),
                pltpu.make_async_copy(fm_hbm.at[:, :, cols], fm_s.at[t], load_sem.at[t, 1]),
                pltpu.make_async_copy(p_hbm.at[:, cols], p_s.at[t], load_sem.at[t, 2]),
            ]
        )
    for t in range(tiles):
        loads[t][0].start()
        loads[t][1].start()
    for t in range(tiles):
        loads[t][2].start()
    barrier = pltpu.get_barrier_semaphore()
    for k in others:
        pl.semaphore_signal(barrier, inc=1, device_id=peer(k), device_id_type=MESH)
    for copy in small[:2]:
        copy.wait()
    numbers = row_numbers(slots, pairs, elems, (st0, st1, st2), (rw0, rw1, rw2), row_sem)
    for copy in numbers:
        copy.start()
    for t in range(tiles):
        loads[t][0].wait()
        loads[t][1].wait()
        fixed_tile(t, elems, fw_s, fm_s, tw)
    for t in range(tiles):
        loads[t][2].wait()
        value_tile(t, elems, p_s, tv)
    for copy in numbers:
        copy.wait()
    pl.semaphore_wait(barrier, len(others))
    copies = []
    for part, chosen in enumerate(((0, 1), (2,))):
        if part == 1:
            for t in range(tiles):
                slope_tile(t, elems, p_s, fm_s, tg)
        for k in others:

            def gather(n, carry, k=k, chosen=chosen):
                base = n * 16
                rows = [rw0[0, k * width + base + u] for u in range(16)]
                for j in chosen:
                    found = [tables[j][pl.ds(row, 1), :] for row in rows]
                    for u in range(16):
                        send[k, j, pl.ds(base + u, 1), :] = found[u]
                return carry

            lax.fori_loop(0, width // 16, gather, 0)
            piece = pl.ds(chosen[0], len(chosen))
            copies.append(
                pltpu.make_async_remote_copy(
                    src_ref=send.at[k, piece],
                    dst_ref=recv.at[8 - k, piece],
                    send_sem=send_sem.at[k, part],
                    recv_sem=recv_sem.at[8 - k, part],
                    device_id=peer(k),
                    device_id_type=MESH,
                )
            )
            copies[-1].start()

    geo = []
    for t in range(tiles):
        cols = pl.ds(t * LANES, LANES)
        geo.append(pltpu.make_async_copy(g_hbm.at[:, cols], g_s.at[t], geo_sem.at[t]))
        geo[-1].start()
    for copy in small[2:]:
        copy.start()
    code_rows(slots, pairs, pad, cb)

    for side, numbers in enumerate((rw1, rw2)):

        def gather_local(n, carry, side=side, numbers=numbers):
            base = n * 16
            rows = [numbers[0, base + u] for u in range(16)]
            for j in range(3):
                found = [tables[j][pl.ds(row, 1), :] for row in rows]
                for u in range(16):
                    locals_[j][pl.ds(side * pair_total + base + u, 1), :] = found[u]
            return carry

        lax.fori_loop(0, pair_total // 16, gather_local, 0)

    def local_flux(n, carry):
        own = aligned(n * group, group)
        other = aligned((n * group + pair_total) % (2 * pair_total), group)
        rows = pl.ds(pl.multiple_of(n * group + slot_total, FACE), group)
        value, lift = pair_flux(
            [table[own, :] for table in locals_], [table[other, :] for table in locals_], cb[rows, :]
        )
        vb[rows, :] = value
        hb[rows, :] = lift
        return carry

    group = 2 * LANES
    lax.fori_loop(0, 2 * pair_total // group, local_flux, 0)
    for copy in geo + small[2:]:
        copy.wait()

    def volume(h, carry):
        volume_half(h, p_s, g_s, fwd, bwd, vol, s_ref)
        return carry

    lax.fori_loop(0, tiles // 2, volume, 0)
    for copy in copies:
        copy.wait()

    def cross_flux(n, carry):
        for shift in (0, 1, 5, 6):
            k = 2 * n + shift
            rows = aligned(k * width, FACE)
            codes = cb[rows, :]
            value, lift = pair_flux(
                [send[k, j] for j in range(3)], [recv[k, j] for j in range(3)], codes & 7
            )
            live = codes >= 8
            vb[rows, :] = jnp.where(live, value, 0.0)
            hb[rows, :] = jnp.where(live, lift, 0.0)
        return carry

    lax.fori_loop(0, 2, cross_flux, 0)
    vb[4 * width : 5 * width, :] = jnp.zeros((width, LANES), jnp.float32)
    hb[4 * width : 5 * width, :] = jnp.zeros((width, LANES), jnp.float32)


def combine_kernel(
    slots, pairs, vb, hb, vol, rhs, lift_ref, modes,
    res, cs,
    vt, lt, fv, fl, st0, st1, st2, rw0, rw1, rw2, row_sem,
):
    elems = vt.shape[0] // 6
    tiles = elems // LANES
    slot_total = slots.shape[2]
    pair_total = pairs.shape[1]
    fields = 2
    numbers = row_numbers(slots, pairs, elems, (st0, st1, st2), (rw0, rw1, rw2), row_sem)
    for copy in numbers:
        copy.start()

    def clear(n, carry):
        rows = aligned(n * LANES, LANES)
        zero = jnp.zeros((LANES, LANES), jnp.float32)
        vt[rows, :] = zero
        lt[rows, :] = zero
        return carry

    lax.fori_loop(0, vt.shape[0] // LANES, clear, 0)
    for copy in numbers:
        copy.wait()
    for start, count, numbers in (
        (0, slot_total, rw0),
        (slot_total, pair_total, rw1),
        (slot_total + pair_total, pair_total, rw2),
    ):

        def scatter(n, carry, start=start, numbers=numbers):
            base = n * 16
            rows = [numbers[0, base + u] for u in range(16)]
            for source, table in ((vb, vt), (hb, lt)):
                found = [source[pl.ds(start + base + u, 1), :] for u in range(16)]
                for u in range(16):
                    table[pl.ds(rows[u], 1), :] = found[u]
            return carry

        lax.fori_loop(0, count // 16, scatter, 0)

    for face in range(6):
        for t in range(tiles):
            rows = slice(face * elems + t * LANES, face * elems + (t + 1) * LANES)
            value = vt[rows, :].T
            lift = lt[rows, :].T
            for f in range(fields):
                fv[t, f, face] = value[f * FACE : (f + 1) * FACE]
                fl[t, f, face] = lift[f * FACE : (f + 1) * FACE]

    half = 2 * LANES

    def finish(n, carry):
        f = n // (tiles // 2)
        h = n % (tiles // 2)
        cols = aligned(h * half, half)

        def wide(ref, *where):
            return jnp.concatenate([ref[2 * h, *where], ref[2 * h + 1, *where]], axis=-1)

        low_lift = wide(fl, f, 0)
        high_lift = wide(fl, f, 1)
        coarse = [None, None]
        for i in range(NODES):
            part = slice(i * NODES, (i + 1) * NODES)
            stack = []
            for face in range(2, 6):
                stack += [wide(fv, f, face, part), wide(fl, f, face, part)]
            rows = aligned(f * BRICK + i * FACE, FACE)
            value = rhs[f, i, :, cols] - wide(vol, rows)
            value = value - product(lift_ref[...], jnp.concatenate(stack, axis=0))
            value = value + float(DERIV[0, i]) * low_lift - float(DERIV[-1, i]) * high_lift
            if i == 0:
                value = value - wide(fv, f, 0)
            if i == NODES - 1:
                value = value - wide(fv, f, 1)
            res[f, i, :, cols] = value
            for a in range(2):
                if MODES[i, a] != 0.0:
                    term = float(MODES[i, a]) * value
                    coarse[a] = term if coarse[a] is None else coarse[a] + term
        for a in range(2):
            for b in range(2):
                layers = [coarse[a][j * NODES : (j + 1) * NODES] for j in range(NODES)]
                level = weighted(MODES[:, b], layers)
                for c in range(2):
                    column = modes[c * NODES : (c + 1) * NODES, 0:1]
                    row = f * NODES + 4 * a + 2 * b + c
                    cs[pl.ds(row, 1), cols] = jnp.sum(level * column, axis=0, keepdims=True)
        return carry

    lax.fori_loop(0, fields * tiles // 2, finish, 0)


def reduce_kernel(n_sub, coarse_ref, cells, total_ref, sums_ref, box, send_sem, recv_sem):
    place = lax.axis_index("blk")
    sub = lax.axis_index("sub")
    barrier = pltpu.get_barrier_semaphore()
    peers = [(place, lax.rem(sub + step, n_sub)) for step in range(1, n_sub)]
    for peer in peers:
        pl.semaphore_signal(barrier, inc=1, device_id=peer, device_id_type=MESH)
    row_cells = sums_ref.shape[1]
    coarse = coarse_ref[...]
    hot = lax.broadcasted_iota(jnp.int32, (row_cells, coarse.shape[1]), 0) == cells[...]
    hot = hot.astype(jnp.float32).astype(jnp.bfloat16)
    high = coarse.astype(jnp.bfloat16)
    low = (coarse - high.astype(jnp.float32)).astype(jnp.bfloat16)
    both = lax.dot_general(
        jnp.concatenate([high, low], axis=0),
        hot,
        (((1,), (1,)), ((), ())),
        preferred_element_type=jnp.float32,
    )
    sums_ref[...] = both[: coarse.shape[0]] + both[coarse.shape[0] :]
    pl.semaphore_wait(barrier, n_sub - 1)
    copies = []
    for step, peer in enumerate(peers):
        copies.append(
            pltpu.make_async_remote_copy(
                src_ref=sums_ref,
                dst_ref=box.at[step],
                send_sem=send_sem.at[step],
                recv_sem=recv_sem.at[step],
                device_id=peer,
                device_id_type=MESH,
            )
        )
        copies[-1].start()
    for copy in copies:
        copy.wait()
    total = sums_ref[...]
    for step in range(n_sub - 1):
        total = total + box[step]
    total_ref[...] = total


def correct_kernel(total_ref, inverse_ref, cells_ref, modes_ref, p_ref, out_ref):
    fields = p_ref.shape[0]
    elems = p_ref.shape[-1]
    row_cells = total_ref.shape[1]
    rows = []
    for f in range(fields):
        level = None
        for j in range(NODES):
            term = inverse_ref[j] * total_ref[f * NODES + j : f * NODES + j + 1, :]
            level = term if level is None else level + term
        rows.append(level)
    level = jnp.concatenate(rows, axis=0)
    high = level.astype(jnp.bfloat16)
    low = (level - high.astype(jnp.float32)).astype(jnp.bfloat16)
    hot = lax.broadcasted_iota(jnp.int32, (row_cells, elems), 0) == cells_ref[...]
    hot = hot.astype(jnp.float32).astype(jnp.bfloat16)
    spread = lax.dot_general(
        jnp.concatenate([high, low], axis=0),
        hot,
        (((1,), (0,)), ((), ())),
        preferred_element_type=jnp.float32,
    )
    spread = spread[: level.shape[0]] + spread[level.shape[0] :]
    columns = [modes_ref[c * NODES : (c + 1) * NODES, 0:1] for c in range(2)]
    for f in range(fields):
        planes = []
        for a in range(2):
            lines = []
            for b in range(2):
                start = f * NODES + 4 * a + 2 * b
                lines.append(
                    columns[0] * spread[start : start + 1] + columns[1] * spread[start + 1 : start + 2]
                )
            planes.append([weighted(MODES[j], lines) for j in range(NODES)])
        for j in range(NODES):
            part = slice(j * NODES, (j + 1) * NODES)
            for i in range(NODES):
                grown = weighted(MODES[i], [planes[0][j], planes[1][j]])
                out_ref[f, i, part, :] = p_ref[f, i, part, :] + grown


def whole(shape, space=VMEM):
    return pl.BlockSpec(shape, lambda *_: (0,) * len(shape), memory_space=space)


def limits(mib, **extra):
    return pltpu.CompilerParams(vmem_limit_bytes=mib << 20, **extra)


def shaped(*shape):
    return jax.ShapeDtypeStruct(shape, jnp.float32)


def on_device(
    n_blk,
    n_sub,
    pressure,
    right_side,
    geometry,
    face_weight,
    face_metric,
    cross_slots,
    local_pairs,
    coarse_map,
    coarse_inverse,
):
    fields = pressure.shape[0]
    elems = pressure.shape[-1]
    slot_total = cross_slots.shape[2]
    pair_total = local_pairs.shape[1]
    row_cells = coarse_inverse.shape[-1]
    tiles = elems // LANES
    width = slot_total // 9
    slabs = (fields, NODES, FACE, elems)
    rows = fields * BRICK
    p = pressure.reshape(slabs)
    weights = jnp.transpose(face_weight, (1, 0, 2))
    metrics = jnp.transpose(face_metric, (1, 0, 2))
    cells = coarse_map.reshape(1, elems)
    modes = jnp.asarray(np.repeat(MODES.T.reshape(2 * NODES, 1), LANES, axis=1), jnp.float32)
    pad_width = -(-slot_total // LANES) * LANES
    side_total = slot_total + 2 * pair_total
    f32 = jnp.float32
    i32 = jnp.int32
    inside = pl.BlockSpec(memory_space=VMEM)
    outside = pl.BlockSpec(memory_space=pltpu.MemorySpace.HBM)
    number_scratch = [
        pltpu.VMEM((1, slot_total), i32),
        pltpu.VMEM((1, pair_total), i32),
        pltpu.VMEM((1, pair_total), i32),
        pltpu.SMEM((1, slot_total), i32),
        pltpu.SMEM((1, pair_total), i32),
        pltpu.SMEM((1, pair_total), i32),
    ]
    dma = pltpu.SemaphoreType.DMA

    volume, values, lifts = pl.pallas_call(
        functools.partial(front_kernel, n_blk, n_sub),
        in_specs=[outside] * 8,
        out_specs=[inside] * 3,
        out_shape=[shaped(tiles, rows, LANES), shaped(side_total, LANES), shaped(side_total, LANES)],
        scratch_shapes=[
            pltpu.VMEM(cross_slots.shape, i32),
            pltpu.VMEM(local_pairs.shape, i32),
            pltpu.VMEM((FACE, 3 * FACE), jnp.bfloat16),
            pltpu.VMEM((FACE, 3 * FACE), jnp.bfloat16),
            pltpu.VMEM((tiles, rows, LANES), f32),
            pltpu.VMEM((tiles, 6, FACE, LANES), f32),
            pltpu.VMEM((tiles, 6, FACE, LANES), f32),
            pltpu.VMEM((tiles, 6 * BRICK, LANES), f32),
            pltpu.VMEM((rows, 2 * LANES), f32),
        ]
        + [pltpu.VMEM((6 * elems, LANES), f32)] * 3
        + [pltpu.VMEM((2 * pair_total, LANES), f32)] * 3
        + [
            pltpu.VMEM((side_total, LANES), i32),
            pltpu.VMEM((8, pad_width), f32),
            pltpu.VMEM((9, 3, width, LANES), f32),
            pltpu.VMEM((9, 3, width, LANES), f32),
        ]
        + number_scratch
        + [dma((4,)), dma((tiles, 3)), dma((tiles,)), dma((3,)), dma((9, 2)), dma((9, 2))],
        compiler_params=limits(36, collective_id=0, has_side_effects=True),
        name="front",
    )(
        *[
            pltpu.with_memory_space_constraint(value, pltpu.MemorySpace.HBM)
            for value in (
                cross_slots,
                local_pairs,
                pressure.reshape(rows, elems),
                weights,
                metrics,
                geometry.reshape(6 * BRICK, elems),
                jnp.asarray(forward_table()),
                jnp.asarray(backward_table()),
            )
        ]
    )

    residual, coarse = pl.pallas_call(
        combine_kernel,
        in_specs=[inside] * 8,
        out_specs=[inside] * 2,
        out_shape=[shaped(*slabs), shaped(fields * NODES, elems)],
        scratch_shapes=[
            pltpu.VMEM((6 * elems, LANES), f32),
            pltpu.VMEM((6 * elems, LANES), f32),
            pltpu.VMEM((tiles, fields, 6, FACE, LANES), f32),
            pltpu.VMEM((tiles, fields, 6, FACE, LANES), f32),
        ]
        + number_scratch
        + [dma((3,))],
        compiler_params=limits(32),
        name="combine",
    )(
        cross_slots,
        local_pairs,
        values,
        lifts,
        volume,
        right_side.reshape(slabs),
        jnp.asarray(lift_table()),
        modes,
    )

    totals = pl.pallas_call(
        functools.partial(reduce_kernel, n_sub),
        in_specs=[inside] * 2,
        out_specs=inside,
        out_shape=shaped(fields * NODES, row_cells),
        scratch_shapes=[
            pltpu.VMEM((fields * NODES, row_cells), f32),
            pltpu.VMEM((n_sub - 1, fields * NODES, row_cells), f32),
            dma((n_sub - 1,)),
            dma((n_sub - 1,)),
        ],
        compiler_params=limits(8, collective_id=1, has_side_effects=True),
        name="reduce",
    )(coarse, cells)

    chunk = min(elems, 256)
    corrected = pl.pallas_call(
        correct_kernel,
        grid=(elems // chunk,),
        in_specs=[
            whole((fields * NODES, row_cells)),
            whole((NODES, NODES, row_cells)),
            pl.BlockSpec((1, chunk), lambda t: (0, t)),
            whole((2 * NODES, LANES)),
            pl.BlockSpec((fields, NODES, FACE, chunk), lambda t: (0, 0, 0, t)),
        ],
        out_specs=pl.BlockSpec((fields, NODES, FACE, chunk), lambda t: (0, 0, 0, t)),
        out_shape=shaped(*slabs),
        compiler_params=limits(32),
        name="correct",
    )(totals, coarse_inverse, cells, modes, p)
    return residual.reshape(pressure.shape), corrected.reshape(pressure.shape)


def solution(mesh):
    return jax.shard_map(
        functools.partial(on_device, mesh.shape["blk"], mesh.shape["sub"]),
        mesh=mesh,
        in_specs=(
            P(None, None, None, None, ("blk", "sub")),
            P(None, None, None, None, ("blk", "sub")),
            P(None, None, None, None, ("blk", "sub")),
            P(None, None, ("blk", "sub")),
            P(None, None, ("blk", "sub")),
            P(None, ("blk", "sub"), None),
            P(None, ("blk", "sub")),
            P(("blk", "sub")),
            P(None, None, "blk"),
        ),
        out_specs=(
            P(None, None, None, None, ("blk", "sub")),
            P(None, None, None, None, ("blk", "sub")),
        ),
        check_vma=False,
    )
```

```python
import functools

import jax
import jax.numpy as jnp
import numpy as np
from jax import lax
from jax.experimental import pallas as pl
from jax.experimental.pallas import tpu as pltpu
from jax.sharding import PartitionSpec as P

NODES = 8
FACE = NODES * NODES
BRICK = NODES * FACE
LANES = 128
MESH = pl.DeviceIdType.MESH
VMEM = pltpu.MemorySpace.VMEM
SMEM = pltpu.MemorySpace.SMEM


def node_points():
    positive = [0.2092992179024789, 0.5917001814331423, 0.8717401485096066, 1.0]
    return np.array(sorted([-entry for entry in positive] + positive))


def derivative_matrix():
    points = node_points()
    count = len(points)
    weights = np.array(
        [
            1.0 / np.prod([points[row] - points[col] for col in range(count) if col != row])
            for row in range(count)
        ]
    )
    matrix = np.zeros((count, count))
    for row in range(count):
        for col in range(count):
            if row != col:
                matrix[row, col] = weights[col] / weights[row] / (points[row] - points[col])
        matrix[row, row] = -np.sum(matrix[row])
    return matrix


DERIV = derivative_matrix()
POINTS = node_points()
MODES = np.stack([(1.0 - POINTS) / 2.0, (1.0 + POINTS) / 2.0], axis=1)


def split_constant(matrix):
    high = matrix.astype(jnp.bfloat16)
    low = (matrix - high.astype(np.float64)).astype(jnp.bfloat16)
    return np.concatenate([high, low, high], axis=1)


def forward_table():
    eye = np.eye(NODES)
    return split_constant(np.kron(eye, DERIV))


def backward_table():
    eye = np.eye(NODES)
    return split_constant(np.kron(eye, DERIV.T))


def lift_table():
    eye = np.eye(NODES)
    rows = [eye[:, :1], -DERIV[:1].T, eye[:, -1:], DERIV[-1:].T]
    second = [np.kron(row, eye) for row in rows]
    third = [np.kron(eye, row) for row in rows]
    return split_constant(np.concatenate(second + third, axis=1))


def split_rows(values):
    high = values.astype(jnp.bfloat16)
    low = (values - high.astype(jnp.float32)).astype(jnp.bfloat16)
    return jnp.concatenate([high, high, low], axis=0)


def product(table, values):
    return lax.dot_general(
        table, split_rows(values), (((1,), (0,)), ((), ())), preferred_element_type=jnp.float32
    )


def even_odd(matrix, layers):
    half = NODES // 2
    sums = [layers[k] + layers[NODES - 1 - k] for k in range(half)]
    gaps = [layers[k] - layers[NODES - 1 - k] for k in range(half)]
    result = [None] * NODES
    for row in range(half):
        even = None
        odd = None
        for k in range(half):
            first = float((matrix[row, k] + matrix[row, NODES - 1 - k]) / 2)
            second = float((matrix[row, k] - matrix[row, NODES - 1 - k]) / 2)
            even = first * sums[k] if even is None else even + first * sums[k]
            odd = second * gaps[k] if odd is None else odd + second * gaps[k]
        result[row] = odd + even
        result[NODES - 1 - row] = odd - even
    return result


def weighted(coefficients, layers):
    total = None
    for factor, layer in zip(coefficients, layers):
        term = float(factor) * layer
        total = term if total is None else total + term
    return total


def inverse_code(code):
    swapped = 4 + 2 * (code & 1) + ((code >> 1) & 1)
    return jnp.where((code & 4) != 0, swapped, code)


def lane_pick(values, index):
    return jnp.take_along_axis(values, index, axis=1, mode="promise_in_bounds")


def pair_flux(own, peer, code):
    wm1, v1, g1 = own
    wm2, v2, g2 = peer
    lane = lax.broadcasted_iota(jnp.int32, code.shape, 1)
    low = lane < FACE
    node = lane & (FACE - 1)
    swapped = ((node & (NODES - 1)) << 3) | (node >> 3)
    source = jnp.where((code & 4) != 0, swapped, node)
    source = source ^ ((code & 1) * 56) ^ (((code >> 1) & 1) * 7)
    source = source | (lane & FACE)
    penalty = NODES * (NODES + 1) / 2.0
    jump = v1 - lane_pick(v2, source)
    gap = g1 - lane_pick(g2, source)
    total = wm1 + lane_pick(wm2, source)
    turned = pltpu.roll(total, FACE, 1)
    weight = 0.5 * jnp.where(low, total, turned)
    tau = (penalty * 0.5) * jnp.where(low, turned, total)
    metric = jnp.where(low, pltpu.roll(wm1, FACE, 1), wm1)
    value = weight * (tau * jump - 0.5 * gap)
    lift = (-0.5 * weight * jump) * metric
    return value, lift


def row_numbers(slots, pairs, elems, staged, rows, sem):
    staged[0][...] = slots[1] * elems + slots[0]
    staged[1][...] = pairs[1:2] * elems + pairs[0:1]
    staged[2][...] = pairs[3:4] * elems + pairs[2:3]
    return [pltpu.make_async_copy(staged[n], rows[n], sem.at[n]) for n in range(3)]


def code_rows(slots, pairs, pad, cb):
    slot_total = slots.shape[2]
    pair_total = pairs.shape[1]
    raw = slots[4]
    code = jnp.where(slots[3] != 0, raw, inverse_code(raw)) + 8 * slots[2]
    pad[0:1, 0:slot_total] = code.astype(jnp.float32)
    pad[0:1, slot_total:] = jnp.zeros((1, pad.shape[1] - slot_total), jnp.float32)
    for t in range(pad.shape[1] // LANES):
        row = jnp.broadcast_to(pad[0:1, t * LANES : (t + 1) * LANES], (LANES, LANES))
        count = min(LANES, slot_total - t * LANES)
        cb[t * LANES : t * LANES + count, :] = row.T.astype(jnp.int32)[:count]
    local = pairs[4:5, :]
    for side, codes in enumerate((local, inverse_code(local))):
        for t in range(pair_total // LANES):
            row = codes[:, t * LANES : (t + 1) * LANES].astype(jnp.float32)
            start = slot_total + side * pair_total + t * LANES
            cb[start : start + LANES, :] = jnp.broadcast_to(row, (LANES, LANES)).T.astype(jnp.int32)


def aligned(start, size):
    return pl.ds(pl.multiple_of(start, size), size)


def node_layers(t, axis, start, p_s):
    layers = []
    for k in range(NODES):
        if axis == 0:
            layers.append(p_s[t, start + k * FACE : start + (k + 1) * FACE, :])
        elif axis == 1:
            rows = [
                p_s[t, start + i * FACE + k * NODES : start + i * FACE + (k + 1) * NODES, :]
                for i in range(NODES)
            ]
            layers.append(jnp.concatenate(rows, axis=0))
        else:
            layers.append(p_s[t, pl.ds(start + k, FACE, stride=NODES), :])
    return layers


def face_rows(face, t, elems):
    return aligned(face * elems + t * LANES, LANES)


def fixed_tile(t, elems, fw_s, fm_s, table):
    for face in range(6):
        both = jnp.concatenate([fw_s[t, face], fm_s[t, face]], axis=0)
        table[face_rows(face, t, elems), :] = both.T


def value_tile(t, elems, p_s, table):
    for axis in range(3):
        for side in range(2):
            ends = []
            for start in range(0, p_s.shape[1], BRICK):
                k = side * (NODES - 1)
                if axis == 0:
                    ends.append(p_s[t, start + k * FACE : start + (k + 1) * FACE, :])
                elif axis == 1:
                    ends += [
                        p_s[t, start + i * FACE + k * NODES : start + i * FACE + (k + 1) * NODES, :]
                        for i in range(NODES)
                    ]
                else:
                    ends.append(p_s[t, pl.ds(start + k, FACE, stride=NODES), :])
            table[face_rows(2 * axis + side, t, elems), :] = jnp.concatenate(ends, axis=0).T


def slope_tile(t, elems, p_s, fm_s, table):
    for axis in range(3):
        slopes = []
        for start in range(0, p_s.shape[1], BRICK):
            layers = node_layers(t, axis, start, p_s)
            slopes.append((weighted(-DERIV[0], layers), weighted(DERIV[-1], layers)))
        for side in range(2):
            face = 2 * axis + side
            slope = jnp.concatenate([entry[side] * fm_s[t, face] for entry in slopes], axis=0)
            table[face_rows(face, t, elems), :] = slope.T


def volume_half(h, p_s, g_s, fwd, bwd, out, s_ref):
    fields = p_s.shape[1] // BRICK
    tiles = (2 * h, 2 * h + 1)

    def wide(ref, rows):
        return jnp.concatenate([ref[tiles[0], rows, :], ref[tiles[1], rows, :]], axis=1)

    def first(n, carry):
        f = n // NODES
        r = n % NODES
        where = [aligned(f * BRICK + k * FACE + r * NODES, NODES) for k in range(NODES)]
        for q, value in enumerate(even_odd(DERIV, [wide(p_s, rows) for rows in where])):
            s_ref[where[q], :] = value
        return carry

    lax.fori_loop(0, fields * NODES, first, 0, unroll=4)

    def middle(i, carry):
        g = [wide(g_s, aligned(n * BRICK + i * FACE, FACE)) for n in range(6)]
        for f in range(fields):
            rows = aligned(f * BRICK + i * FACE, FACE)
            x = wide(p_s, rows)
            s3 = product(fwd[...], x)
            s2 = jnp.concatenate(
                even_odd(DERIV, [x[j * NODES : (j + 1) * NODES] for j in range(NODES)]), axis=0
            )
            s1 = s_ref[rows, :]
            q1 = g[0] * s1 + g[3] * s2 + g[4] * s3
            q2 = g[3] * s1 + g[1] * s2 + g[5] * s3
            q3 = g[4] * s1 + g[5] * s2 + g[2] * s3
            s_ref[rows, :] = q1
            r2 = jnp.concatenate(
                even_odd(DERIV.T, [q2[j * NODES : (j + 1) * NODES] for j in range(NODES)]), axis=0
            )
            r23 = product(bwd[...], q3) + r2
            out[tiles[0], rows, :] = r23[:, :LANES]
            out[tiles[1], rows, :] = r23[:, LANES:]
        return carry

    lax.fori_loop(0, NODES, middle, 0, unroll=4)

    def last(n, carry):
        f = n // NODES
        r = n % NODES
        where = [aligned(f * BRICK + k * FACE + r * NODES, NODES) for k in range(NODES)]
        for q, value in enumerate(even_odd(DERIV.T, [s_ref[rows, :] for rows in where])):
            out[tiles[0], where[q], :] += value[:, :LANES]
            out[tiles[1], where[q], :] += value[:, LANES:]
        return carry

    lax.fori_loop(0, fields * NODES, last, 0, unroll=4)


def front_kernel(
    n_blk, n_sub,
    slots_hbm, pairs_hbm, p_hbm, fw_hbm, fm_hbm, g_hbm, fwd_hbm, bwd_hbm,
    vol, vb, hb,
    slots, pairs, fwd, bwd, p_s, fw_s, fm_s, g_s, s_ref, tv, tg, tw, la, lb, lc, cb, pad, send, recv,
    st0, st1, st2, rw0, rw1, rw2,
    small_sem, load_sem, geo_sem, row_sem, send_sem, recv_sem,
):
    elems = tv.shape[0] // 6
    tiles = elems // LANES
    slot_total = slots.shape[2]
    pair_total = pairs.shape[1]
    width = slot_total // 9
    tables = (tw, tv, tg)
    locals_ = (la, lb, lc)
    place = lax.axis_index("blk")
    sub = lax.axis_index("sub")

    def peer(k):
        return (
            lax.rem(place + (k // 3 - 1) + n_blk, n_blk),
            lax.rem(sub + (k % 3 - 1) + n_sub, n_sub),
        )

    others = [2, 0, 8, 6, 5, 3, 1, 7]
    barrier = pltpu.get_barrier_semaphore()
    for k in others:
        pl.semaphore_signal(barrier, inc=1, device_id=peer(k), device_id_type=MESH)
    small = [
        pltpu.make_async_copy(source, target, small_sem.at[n])
        for n, (source, target) in enumerate(
            ((slots_hbm, slots), (pairs_hbm, pairs), (fwd_hbm, fwd), (bwd_hbm, bwd))
        )
    ]
    for copy in small[:2]:
        copy.start()
    loads = []
    for t in range(tiles):
        cols = pl.ds(t * LANES, LANES)
        loads.append(
            [
                pltpu.make_async_copy(fw_hbm.at[:, :, cols], fw_s.at[t], load_sem.at[t, 0]),
                pltpu.make_async_copy(fm_hbm.at[:, :, cols], fm_s.at[t], load_sem.at[t, 1]),
                pltpu.make_async_copy(p_hbm.at[:, cols], p_s.at[t], load_sem.at[t, 2]),
            ]
        )
    for t in range(tiles):
        loads[t][0].start()
        loads[t][1].start()
    for t in range(tiles):
        loads[t][2].start()
    for copy in small[:2]:
        copy.wait()
    numbers = row_numbers(slots, pairs, elems, (st0, st1, st2), (rw0, rw1, rw2), row_sem)
    for copy in numbers:
        copy.start()
    for t in range(tiles):
        loads[t][0].wait()
        loads[t][1].wait()
        fixed_tile(t, elems, fw_s, fm_s, tw)
    for t in range(tiles):
        loads[t][2].wait()
        value_tile(t, elems, p_s, tv)
        slope_tile(t, elems, p_s, fm_s, tg)
    geo = []
    for t in range(tiles):
        cols = pl.ds(t * LANES, LANES)
        geo.append(pltpu.make_async_copy(g_hbm.at[:, cols], g_s.at[t], geo_sem.at[t]))
        geo[-1].start()
    for copy in small[2:]:
        copy.start()
    for copy in numbers:
        copy.wait()
    for k in others:

        def gather(n, carry, k=k):
            base = n * 16
            rows = [rw0[0, k * width + base + u] for u in range(16)]
            for j in range(3):
                found = [tables[j][pl.ds(row, 1), :] for row in rows]
                for u in range(16):
                    send[k, j, pl.ds(base + u, 1), :] = found[u]
            return carry

        lax.fori_loop(0, width // 16, gather, 0)
    code_rows(slots, pairs, pad, cb)

    for side, numbers in enumerate((rw1, rw2)):

        def gather_local(n, carry, side=side, numbers=numbers):
            base = n * 16
            rows = [numbers[0, base + u] for u in range(16)]
            for j in range(3):
                found = [tables[j][pl.ds(row, 1), :] for row in rows]
                for u in range(16):
                    locals_[j][pl.ds(side * pair_total + base + u, 1), :] = found[u]
            return carry

        lax.fori_loop(0, pair_total // 16, gather_local, 0)

    pl.semaphore_wait(barrier, len(others))
    copies = []
    for k in others:
        copies.append(
            pltpu.make_async_remote_copy(
                src_ref=send.at[k],
                dst_ref=recv.at[8 - k],
                send_sem=send_sem.at[k],
                recv_sem=recv_sem.at[8 - k],
                device_id=peer(k),
                device_id_type=MESH,
            )
        )
        copies[-1].start()

    def local_flux(n, carry):
        own = aligned(n * group, group)
        other = aligned((n * group + pair_total) % (2 * pair_total), group)
        rows = pl.ds(pl.multiple_of(n * group + slot_total, FACE), group)
        value, lift = pair_flux(
            [table[own, :] for table in locals_], [table[other, :] for table in locals_], cb[rows, :]
        )
        vb[rows, :] = value
        hb[rows, :] = lift
        return carry

    group = 2 * LANES
    lax.fori_loop(0, 2 * pair_total // group, local_flux, 0)
    for copy in geo + small[2:]:
        copy.wait()

    def volume(h, carry):
        volume_half(h, p_s, g_s, fwd, bwd, vol, s_ref)
        return carry

    lax.fori_loop(0, tiles // 2, volume, 0)
    for copy in copies:
        copy.wait()

    def cross_flux(n, carry):
        for shift in (0, 1, 5, 6):
            k = 2 * n + shift
            rows = aligned(k * width, FACE)
            codes = cb[rows, :]
            value, lift = pair_flux(
                [send[k, j] for j in range(3)], [recv[k, j] for j in range(3)], codes & 7
            )
            live = codes >= 8
            vb[rows, :] = jnp.where(live, value, 0.0)
            hb[rows, :] = jnp.where(live, lift, 0.0)
        return carry

    lax.fori_loop(0, 2, cross_flux, 0)
    vb[4 * width : 5 * width, :] = jnp.zeros((width, LANES), jnp.float32)
    hb[4 * width : 5 * width, :] = jnp.zeros((width, LANES), jnp.float32)


def combine_kernel(
    slots, pairs, vb, hb, vol, rhs, lift_ref, modes,
    res, cs,
    vt, lt, fv, fl, st0, st1, st2, rw0, rw1, rw2, row_sem,
):
    elems = vt.shape[0] // 6
    tiles = elems // LANES
    slot_total = slots.shape[2]
    pair_total = pairs.shape[1]
    fields = 2
    numbers = row_numbers(slots, pairs, elems, (st0, st1, st2), (rw0, rw1, rw2), row_sem)
    for copy in numbers:
        copy.start()

    def clear(n, carry):
        rows = aligned(n * LANES, LANES)
        zero = jnp.zeros((LANES, LANES), jnp.float32)
        vt[rows, :] = zero
        lt[rows, :] = zero
        return carry

    lax.fori_loop(0, vt.shape[0] // LANES, clear, 0)
    for copy in numbers:
        copy.wait()
    for start, count, numbers in (
        (0, slot_total, rw0),
        (slot_total, pair_total, rw1),
        (slot_total + pair_total, pair_total, rw2),
    ):

        def scatter(n, carry, start=start, numbers=numbers):
            base = n * 16
            rows = [numbers[0, base + u] for u in range(16)]
            for source, table in ((vb, vt), (hb, lt)):
                found = [source[pl.ds(start + base + u, 1), :] for u in range(16)]
                for u in range(16):
                    table[pl.ds(rows[u], 1), :] = found[u]
            return carry

        lax.fori_loop(0, count // 16, scatter, 0)

    for face in range(6):
        for t in range(tiles):
            rows = slice(face * elems + t * LANES, face * elems + (t + 1) * LANES)
            value = vt[rows, :].T
            lift = lt[rows, :].T
            for f in range(fields):
                fv[t, f, face] = value[f * FACE : (f + 1) * FACE]
                fl[t, f, face] = lift[f * FACE : (f + 1) * FACE]

    half = 2 * LANES

    def finish(n, carry):
        f = n // (tiles // 2)
        h = n % (tiles // 2)
        cols = aligned(h * half, half)

        def wide(ref, *where):
            return jnp.concatenate([ref[2 * h, *where], ref[2 * h + 1, *where]], axis=-1)

        low_lift = wide(fl, f, 0)
        high_lift = wide(fl, f, 1)
        coarse = [None, None]
        for i in range(NODES):
            part = slice(i * NODES, (i + 1) * NODES)
            stack = []
            for face in range(2, 6):
                stack += [wide(fv, f, face, part), wide(fl, f, face, part)]
            rows = aligned(f * BRICK + i * FACE, FACE)
            value = rhs[f, i, :, cols] - wide(vol, rows)
            value = value - product(lift_ref[...], jnp.concatenate(stack, axis=0))
            value = value + float(DERIV[0, i]) * low_lift - float(DERIV[-1, i]) * high_lift
            if i == 0:
                value = value - wide(fv, f, 0)
            if i == NODES - 1:
                value = value - wide(fv, f, 1)
            res[f, i, :, cols] = value
            for a in range(2):
                if MODES[i, a] != 0.0:
                    term = float(MODES[i, a]) * value
                    coarse[a] = term if coarse[a] is None else coarse[a] + term
        for a in range(2):
            for b in range(2):
                layers = [coarse[a][j * NODES : (j + 1) * NODES] for j in range(NODES)]
                level = weighted(MODES[:, b], layers)
                for c in range(2):
                    column = modes[c * NODES : (c + 1) * NODES, 0:1]
                    row = f * NODES + 4 * a + 2 * b + c
                    cs[pl.ds(row, 1), cols] = jnp.sum(level * column, axis=0, keepdims=True)
        return carry

    lax.fori_loop(0, fields * tiles // 2, finish, 0)


def reduce_kernel(n_sub, coarse_ref, cells, total_ref, sums_ref, box, send_sem, recv_sem):
    place = lax.axis_index("blk")
    sub = lax.axis_index("sub")
    barrier = pltpu.get_barrier_semaphore()
    peers = [(place, lax.rem(sub + step, n_sub)) for step in range(1, n_sub)]
    for peer in peers:
        pl.semaphore_signal(barrier, inc=1, device_id=peer, device_id_type=MESH)
    row_cells = sums_ref.shape[1]
    coarse = coarse_ref[...]
    hot = lax.broadcasted_iota(jnp.int32, (row_cells, coarse.shape[1]), 0) == cells[...]
    hot = hot.astype(jnp.float32).astype(jnp.bfloat16)
    high = coarse.astype(jnp.bfloat16)
    low = (coarse - high.astype(jnp.float32)).astype(jnp.bfloat16)
    both = lax.dot_general(
        jnp.concatenate([high, low], axis=0),
        hot,
        (((1,), (1,)), ((), ())),
        preferred_element_type=jnp.float32,
    )
    sums_ref[...] = both[: coarse.shape[0]] + both[coarse.shape[0] :]
    pl.semaphore_wait(barrier, n_sub - 1)
    copies = []
    for step, peer in enumerate(peers):
        copies.append(
            pltpu.make_async_remote_copy(
                src_ref=sums_ref,
                dst_ref=box.at[step],
                send_sem=send_sem.at[step],
                recv_sem=recv_sem.at[step],
                device_id=peer,
                device_id_type=MESH,
            )
        )
        copies[-1].start()
    for copy in copies:
        copy.wait()
    total = sums_ref[...]
    for step in range(n_sub - 1):
        total = total + box[step]
    total_ref[...] = total


def correct_kernel(total_ref, inverse_ref, cells_ref, modes_ref, p_ref, out_ref):
    fields = p_ref.shape[0]
    elems = p_ref.shape[-1]
    row_cells = total_ref.shape[1]
    rows = []
    for f in range(fields):
        level = None
        for j in range(NODES):
            term = inverse_ref[j] * total_ref[f * NODES + j : f * NODES + j + 1, :]
            level = term if level is None else level + term
        rows.append(level)
    level = jnp.concatenate(rows, axis=0)
    high = level.astype(jnp.bfloat16)
    low = (level - high.astype(jnp.float32)).astype(jnp.bfloat16)
    hot = lax.broadcasted_iota(jnp.int32, (row_cells, elems), 0) == cells_ref[...]
    hot = hot.astype(jnp.float32).astype(jnp.bfloat16)
    spread = lax.dot_general(
        jnp.concatenate([high, low], axis=0),
        hot,
        (((1,), (0,)), ((), ())),
        preferred_element_type=jnp.float32,
    )
    spread = spread[: level.shape[0]] + spread[level.shape[0] :]
    columns = [modes_ref[c * NODES : (c + 1) * NODES, 0:1] for c in range(2)]
    for f in range(fields):
        planes = []
        for a in range(2):
            lines = []
            for b in range(2):
                start = f * NODES + 4 * a + 2 * b
                lines.append(
                    columns[0] * spread[start : start + 1] + columns[1] * spread[start + 1 : start + 2]
                )
            planes.append([weighted(MODES[j], lines) for j in range(NODES)])
        for j in range(NODES):
            part = slice(j * NODES, (j + 1) * NODES)
            for i in range(NODES):
                grown = weighted(MODES[i], [planes[0][j], planes[1][j]])
                out_ref[f, i, part, :] = p_ref[f, i, part, :] + grown


def whole(shape, space=VMEM):
    return pl.BlockSpec(shape, lambda *_: (0,) * len(shape), memory_space=space)


def limits(mib, **extra):
    return pltpu.CompilerParams(vmem_limit_bytes=mib << 20, **extra)


def shaped(*shape):
    return jax.ShapeDtypeStruct(shape, jnp.float32)


def on_device(
    n_blk,
    n_sub,
    pressure,
    right_side,
    geometry,
    face_weight,
    face_metric,
    cross_slots,
    local_pairs,
    coarse_map,
    coarse_inverse,
):
    fields = pressure.shape[0]
    elems = pressure.shape[-1]
    slot_total = cross_slots.shape[2]
    pair_total = local_pairs.shape[1]
    row_cells = coarse_inverse.shape[-1]
    tiles = elems // LANES
    width = slot_total // 9
    slabs = (fields, NODES, FACE, elems)
    rows = fields * BRICK
    p = pressure.reshape(slabs)
    weights = jnp.transpose(face_weight, (1, 0, 2))
    metrics = jnp.transpose(face_metric, (1, 0, 2))
    cells = coarse_map.reshape(1, elems)
    modes = jnp.asarray(np.repeat(MODES.T.reshape(2 * NODES, 1), LANES, axis=1), jnp.float32)
    pad_width = -(-slot_total // LANES) * LANES
    side_total = slot_total + 2 * pair_total
    f32 = jnp.float32
    i32 = jnp.int32
    inside = pl.BlockSpec(memory_space=VMEM)
    outside = pl.BlockSpec(memory_space=pltpu.MemorySpace.HBM)
    number_scratch = [
        pltpu.VMEM((1, slot_total), i32),
        pltpu.VMEM((1, pair_total), i32),
        pltpu.VMEM((1, pair_total), i32),
        pltpu.SMEM((1, slot_total), i32),
        pltpu.SMEM((1, pair_total), i32),
        pltpu.SMEM((1, pair_total), i32),
    ]
    dma = pltpu.SemaphoreType.DMA

    volume, values, lifts = pl.pallas_call(
        functools.partial(front_kernel, n_blk, n_sub),
        in_specs=[outside] * 8,
        out_specs=[inside] * 3,
        out_shape=[shaped(tiles, rows, LANES), shaped(side_total, LANES), shaped(side_total, LANES)],
        scratch_shapes=[
            pltpu.VMEM(cross_slots.shape, i32),
            pltpu.VMEM(local_pairs.shape, i32),
            pltpu.VMEM((FACE, 3 * FACE), jnp.bfloat16),
            pltpu.VMEM((FACE, 3 * FACE), jnp.bfloat16),
            pltpu.VMEM((tiles, rows, LANES), f32),
            pltpu.VMEM((tiles, 6, FACE, LANES), f32),
            pltpu.VMEM((tiles, 6, FACE, LANES), f32),
            pltpu.VMEM((tiles, 6 * BRICK, LANES), f32),
            pltpu.VMEM((rows, 2 * LANES), f32),
        ]
        + [pltpu.VMEM((6 * elems, LANES), f32)] * 3
        + [pltpu.VMEM((2 * pair_total, LANES), f32)] * 3
        + [
            pltpu.VMEM((side_total, LANES), i32),
            pltpu.VMEM((8, pad_width), f32),
            pltpu.VMEM((9, 3, width, LANES), f32),
            pltpu.VMEM((9, 3, width, LANES), f32),
        ]
        + number_scratch
        + [dma((4,)), dma((tiles, 3)), dma((tiles,)), dma((3,)), dma((9,)), dma((9,))],
        compiler_params=limits(36, collective_id=0, has_side_effects=True),
        name="front",
    )(
        *[
            pltpu.with_memory_space_constraint(value, pltpu.MemorySpace.HBM)
            for value in (
                cross_slots,
                local_pairs,
                pressure.reshape(rows, elems),
                weights,
                metrics,
                geometry.reshape(6 * BRICK, elems),
                jnp.asarray(forward_table()),
                jnp.asarray(backward_table()),
            )
        ]
    )

    residual, coarse = pl.pallas_call(
        combine_kernel,
        in_specs=[inside] * 8,
        out_specs=[inside] * 2,
        out_shape=[shaped(*slabs), shaped(fields * NODES, elems)],
        scratch_shapes=[
            pltpu.VMEM((6 * elems, LANES), f32),
            pltpu.VMEM((6 * elems, LANES), f32),
            pltpu.VMEM((tiles, fields, 6, FACE, LANES), f32),
            pltpu.VMEM((tiles, fields, 6, FACE, LANES), f32),
        ]
        + number_scratch
        + [dma((3,))],
        compiler_params=limits(32),
        name="combine",
    )(
        cross_slots,
        local_pairs,
        values,
        lifts,
        volume,
        right_side.reshape(slabs),
        jnp.asarray(lift_table()),
        modes,
    )

    totals = pl.pallas_call(
        functools.partial(reduce_kernel, n_sub),
        in_specs=[inside] * 2,
        out_specs=inside,
        out_shape=shaped(fields * NODES, row_cells),
        scratch_shapes=[
            pltpu.VMEM((fields * NODES, row_cells), f32),
            pltpu.VMEM((n_sub - 1, fields * NODES, row_cells), f32),
            dma((n_sub - 1,)),
            dma((n_sub - 1,)),
        ],
        compiler_params=limits(8, collective_id=1, has_side_effects=True),
        name="reduce",
    )(coarse, cells)

    chunk = min(elems, 256)
    corrected = pl.pallas_call(
        correct_kernel,
        grid=(elems // chunk,),
        in_specs=[
            whole((fields * NODES, row_cells)),
            whole((NODES, NODES, row_cells)),
            pl.BlockSpec((1, chunk), lambda t: (0, t)),
            whole((2 * NODES, LANES)),
            pl.BlockSpec((fields, NODES, FACE, chunk), lambda t: (0, 0, 0, t)),
        ],
        out_specs=pl.BlockSpec((fields, NODES, FACE, chunk), lambda t: (0, 0, 0, t)),
        out_shape=shaped(*slabs),
        compiler_params=limits(32),
        name="correct",
    )(totals, coarse_inverse, cells, modes, p)
    return residual.reshape(pressure.shape), corrected.reshape(pressure.shape)


def solution(mesh):
    return jax.shard_map(
        functools.partial(on_device, mesh.shape["blk"], mesh.shape["sub"]),
        mesh=mesh,
        in_specs=(
            P(None, None, None, None, ("blk", "sub")),
            P(None, None, None, None, ("blk", "sub")),
            P(None, None, None, None, ("blk", "sub")),
            P(None, None, ("blk", "sub")),
            P(None, None, ("blk", "sub")),
            P(None, ("blk", "sub"), None),
            P(None, ("blk", "sub")),
            P(("blk", "sub")),
            P(None, None, "blk"),
        ),
        out_specs=(
            P(None, None, None, None, ("blk", "sub")),
            P(None, None, None, None, ("blk", "sub")),
        ),
        check_vma=False,
    )
```

```python
import functools

import jax
import jax.numpy as jnp
import numpy as np
from jax import lax
from jax.experimental import pallas as pl
from jax.experimental.pallas import tpu as pltpu
from jax.sharding import PartitionSpec as P

NODES = 8
FACE = NODES * NODES
BRICK = NODES * FACE
LANES = 128
MESH = pl.DeviceIdType.MESH
VMEM = pltpu.MemorySpace.VMEM
SMEM = pltpu.MemorySpace.SMEM


def node_points():
    positive = [0.2092992179024789, 0.5917001814331423, 0.8717401485096066, 1.0]
    return np.array(sorted([-entry for entry in positive] + positive))


def derivative_matrix():
    points = node_points()
    count = len(points)
    weights = np.array(
        [
            1.0 / np.prod([points[row] - points[col] for col in range(count) if col != row])
            for row in range(count)
        ]
    )
    matrix = np.zeros((count, count))
    for row in range(count):
        for col in range(count):
            if row != col:
                matrix[row, col] = weights[col] / weights[row] / (points[row] - points[col])
        matrix[row, row] = -np.sum(matrix[row])
    return matrix


DERIV = derivative_matrix()
POINTS = node_points()
MODES = np.stack([(1.0 - POINTS) / 2.0, (1.0 + POINTS) / 2.0], axis=1)


def split_constant(matrix):
    high = matrix.astype(jnp.bfloat16)
    low = (matrix - high.astype(np.float64)).astype(jnp.bfloat16)
    return np.concatenate([high, low, high], axis=1)


def forward_table():
    eye = np.eye(NODES)
    return split_constant(np.kron(eye, DERIV))


def backward_table():
    eye = np.eye(NODES)
    return split_constant(np.kron(eye, DERIV.T))


def lift_table():
    eye = np.eye(NODES)
    rows = [eye[:, :1], -DERIV[:1].T, eye[:, -1:], DERIV[-1:].T]
    second = [np.kron(row, eye) for row in rows]
    third = [np.kron(eye, row) for row in rows]
    return split_constant(np.concatenate(second + third, axis=1))


def split_rows(values):
    high = values.astype(jnp.bfloat16)
    low = (values - high.astype(jnp.float32)).astype(jnp.bfloat16)
    return jnp.concatenate([high, high, low], axis=0)


def product(table, values):
    return lax.dot_general(
        table, split_rows(values), (((1,), (0,)), ((), ())), preferred_element_type=jnp.float32
    )


def even_odd(matrix, layers):
    half = NODES // 2
    sums = [layers[k] + layers[NODES - 1 - k] for k in range(half)]
    gaps = [layers[k] - layers[NODES - 1 - k] for k in range(half)]
    result = [None] * NODES
    for row in range(half):
        even = None
        odd = None
        for k in range(half):
            first = float((matrix[row, k] + matrix[row, NODES - 1 - k]) / 2)
            second = float((matrix[row, k] - matrix[row, NODES - 1 - k]) / 2)
            even = first * sums[k] if even is None else even + first * sums[k]
            odd = second * gaps[k] if odd is None else odd + second * gaps[k]
        result[row] = odd + even
        result[NODES - 1 - row] = odd - even
    return result


def weighted(coefficients, layers):
    total = None
    for factor, layer in zip(coefficients, layers):
        term = float(factor) * layer
        total = term if total is None else total + term
    return total


def turn_code(code, inverse):
    first = code & 1
    second = (code >> 1) & 1
    swap = (code >> 2) & 1
    if inverse:
        first, second = (
            jnp.where(swap != 0, second, first),
            jnp.where(swap != 0, first, second),
        )
    return first * 56 + second * 7 + swap * 128


def lane_pick(values, index):
    return jnp.take_along_axis(values, index, axis=1, mode="promise_in_bounds")


def lane_source(turn):
    lane = lax.broadcasted_iota(jnp.int32, turn.shape, 1)
    swapped = ((lane & 7) << 3) | ((lane >> 3) & 7) | (lane & FACE)
    return (jnp.where((turn & 128) != 0, swapped, lane) ^ turn) & (LANES - 1)


def spread_metric(both):
    low = lax.broadcasted_iota(jnp.int32, both.shape, 1) < FACE
    return jnp.where(low, pltpu.roll(both, FACE, 1), both)


def pair_flux(own, peer, turn):
    wm1, v1, g1 = own
    wm2, v2, g2 = peer
    source = lane_source(turn)
    low = lax.broadcasted_iota(jnp.int32, turn.shape, 1) < FACE
    penalty = NODES * (NODES + 1) / 2.0
    jump = v1 - lane_pick(v2, source)
    gap = g1 - lane_pick(g2, source)
    total = wm1 + lane_pick(wm2, source)
    turned = pltpu.roll(total, FACE, 1)
    weight = 0.5 * jnp.where(low, total, turned)
    tau = (penalty * 0.5) * jnp.where(low, turned, total)
    return weight * (tau * jump - 0.5 * gap), -0.5 * weight * jump


def row_numbers(slots, pairs, elems, staged, rows, sem):
    staged[0][...] = slots[1] * elems + slots[0]
    staged[1][...] = pairs[1:2] * elems + pairs[0:1]
    staged[2][...] = pairs[3:4] * elems + pairs[2:3]
    return [pltpu.make_async_copy(staged[n], rows[n], sem.at[n]) for n in range(3)]


def code_rows(slots, pairs, pad, cb):
    slot_total = slots.shape[2]
    pair_total = pairs.shape[1]
    raw = slots[4]
    code = jnp.where(slots[3] != 0, turn_code(raw, False), turn_code(raw, True)) + 256 * slots[2]
    pad[0:1, 0:slot_total] = code.astype(jnp.float32)
    pad[0:1, slot_total:] = jnp.zeros((1, pad.shape[1] - slot_total), jnp.float32)
    for t in range(pad.shape[1] // LANES):
        row = jnp.broadcast_to(pad[0:1, t * LANES : (t + 1) * LANES], (LANES, LANES))
        count = min(LANES, slot_total - t * LANES)
        cb[t * LANES : t * LANES + count, :] = row.T.astype(jnp.int32)[:count]
    local = pairs[4:5, :]
    for side, codes in enumerate((turn_code(local, False), turn_code(local, True))):
        for t in range(pair_total // LANES):
            row = codes[:, t * LANES : (t + 1) * LANES].astype(jnp.float32)
            start = slot_total + side * pair_total + t * LANES
            cb[start : start + LANES, :] = jnp.broadcast_to(row, (LANES, LANES)).T.astype(jnp.int32)


def aligned(start, size):
    return pl.ds(pl.multiple_of(start, size), size)


def node_layers(t, axis, start, p_s):
    layers = []
    for k in range(NODES):
        if axis == 0:
            layers.append(p_s[t, start + k * FACE : start + (k + 1) * FACE, :])
        elif axis == 1:
            rows = [
                p_s[t, start + i * FACE + k * NODES : start + i * FACE + (k + 1) * NODES, :]
                for i in range(NODES)
            ]
            layers.append(jnp.concatenate(rows, axis=0))
        else:
            layers.append(p_s[t, pl.ds(start + k, FACE, stride=NODES), :])
    return layers


def face_rows(face, t, elems):
    return aligned(face * elems + t * LANES, LANES)


def fixed_tile(t, elems, fw_s, fm_s, table):
    for face in range(6):
        both = jnp.concatenate([fw_s[t, face], fm_s[t, face]], axis=0)
        table[face_rows(face, t, elems), :] = both.T


def value_tile(t, elems, p_s, table):
    for axis in range(3):
        for side in range(2):
            ends = []
            for start in range(0, p_s.shape[1], BRICK):
                k = side * (NODES - 1)
                if axis == 0:
                    ends.append(p_s[t, start + k * FACE : start + (k + 1) * FACE, :])
                elif axis == 1:
                    ends += [
                        p_s[t, start + i * FACE + k * NODES : start + i * FACE + (k + 1) * NODES, :]
                        for i in range(NODES)
                    ]
                else:
                    ends.append(p_s[t, pl.ds(start + k, FACE, stride=NODES), :])
            table[face_rows(2 * axis + side, t, elems), :] = jnp.concatenate(ends, axis=0).T


def slope_tile(t, elems, p_s, fm_s, table):
    for axis in range(3):
        slopes = []
        for start in range(0, p_s.shape[1], BRICK):
            layers = node_layers(t, axis, start, p_s)
            slopes.append((weighted(-DERIV[0], layers), weighted(DERIV[-1], layers)))
        for side in range(2):
            face = 2 * axis + side
            slope = jnp.concatenate([entry[side] * fm_s[t, face] for entry in slopes], axis=0)
            table[face_rows(face, t, elems), :] = slope.T


def volume_half(h, p_s, g_s, fwd, bwd, out, s_ref):
    fields = p_s.shape[1] // BRICK
    tiles = (2 * h, 2 * h + 1)

    def wide(ref, rows):
        return jnp.concatenate([ref[tiles[0], rows, :], ref[tiles[1], rows, :]], axis=1)

    def first(n, carry):
        f = n // NODES
        r = n % NODES
        where = [aligned(f * BRICK + k * FACE + r * NODES, NODES) for k in range(NODES)]
        for q, value in enumerate(even_odd(DERIV, [wide(p_s, rows) for rows in where])):
            s_ref[where[q], :] = value
        return carry

    lax.fori_loop(0, fields * NODES, first, 0, unroll=4)

    def middle(i, carry):
        g = [wide(g_s, aligned(n * BRICK + i * FACE, FACE)) for n in range(6)]
        for f in range(fields):
            rows = aligned(f * BRICK + i * FACE, FACE)
            x = wide(p_s, rows)
            s3 = product(fwd[...], x)
            s2 = jnp.concatenate(
                even_odd(DERIV, [x[j * NODES : (j + 1) * NODES] for j in range(NODES)]), axis=0
            )
            s1 = s_ref[rows, :]
            q1 = g[0] * s1 + g[3] * s2 + g[4] * s3
            q2 = g[3] * s1 + g[1] * s2 + g[5] * s3
            q3 = g[4] * s1 + g[5] * s2 + g[2] * s3
            s_ref[rows, :] = q1
            r2 = jnp.concatenate(
                even_odd(DERIV.T, [q2[j * NODES : (j + 1) * NODES] for j in range(NODES)]), axis=0
            )
            r23 = product(bwd[...], q3) + r2
            out[tiles[0], rows, :] = r23[:, :LANES]
            out[tiles[1], rows, :] = r23[:, LANES:]
        return carry

    lax.fori_loop(0, NODES, middle, 0, unroll=4)

    def last(n, carry):
        f = n // NODES
        r = n % NODES
        where = [aligned(f * BRICK + k * FACE + r * NODES, NODES) for k in range(NODES)]
        for q, value in enumerate(even_odd(DERIV.T, [s_ref[rows, :] for rows in where])):
            out[tiles[0], where[q], :] += value[:, :LANES]
            out[tiles[1], where[q], :] += value[:, LANES:]
        return carry

    lax.fori_loop(0, fields * NODES, last, 0, unroll=4)


def front_kernel(
    n_blk, n_sub,
    slots_hbm, pairs_hbm, p_hbm, fw_hbm, fm_hbm, g_hbm, fwd_hbm, bwd_hbm,
    vol, vb, hb,
    slots, pairs, fwd, bwd, p_s, fw_s, fm_s, g_s, s_ref, tv, tg, tw, la, lb, lc, cb, pad, send, recv,
    st0, st1, st2, rw0, rw1, rw2,
    small_sem, load_sem, geo_sem, row_sem, send_sem, recv_sem,
):
    elems = tv.shape[0] // 6
    tiles = elems // LANES
    slot_total = slots.shape[2]
    pair_total = pairs.shape[1]
    width = slot_total // 9
    tables = (tw, tv, tg)
    locals_ = (la, lb, lc)
    place = lax.axis_index("blk")
    sub = lax.axis_index("sub")

    def peer(k):
        return (
            lax.rem(place + (k // 3 - 1) + n_blk, n_blk),
            lax.rem(sub + (k % 3 - 1) + n_sub, n_sub),
        )

    others = [2, 0, 8, 6, 5, 3, 1, 7]
    barrier = pltpu.get_barrier_semaphore()
    for k in others:
        pl.semaphore_signal(barrier, inc=1, device_id=peer(k), device_id_type=MESH)
    small = [
        pltpu.make_async_copy(source, target, small_sem.at[n])
        for n, (source, target) in enumerate(
            ((slots_hbm, slots), (pairs_hbm, pairs), (fwd_hbm, fwd), (bwd_hbm, bwd))
        )
    ]
    for copy in small[:2]:
        copy.start()
    loads = []
    geo = []
    for t in range(tiles):
        cols = pl.ds(t * LANES, LANES)
        geo.append(pltpu.make_async_copy(g_hbm.at[:, cols], g_s.at[t], geo_sem.at[t]))
        loads.append(
            [
                pltpu.make_async_copy(fw_hbm.at[:, :, cols], fw_s.at[t], load_sem.at[t, 0]),
                pltpu.make_async_copy(fm_hbm.at[:, :, cols], fm_s.at[t], load_sem.at[t, 1]),
                pltpu.make_async_copy(p_hbm.at[:, cols], p_s.at[t], load_sem.at[t, 2]),
            ]
        )
    for t in range(tiles):
        loads[t][0].start()
        loads[t][1].start()
    for t in range(tiles):
        loads[t][2].start()
    for copy in small[:2]:
        copy.wait()
    numbers = row_numbers(slots, pairs, elems, (st0, st1, st2), (rw0, rw1, rw2), row_sem)
    for copy in numbers:
        copy.start()
    for t in range(tiles):
        loads[t][0].wait()
        loads[t][1].wait()
        fixed_tile(t, elems, fw_s, fm_s, tw)
    for t in range(tiles):
        loads[t][2].wait()
        if t == tiles - 1:
            for copy in geo + small[2:]:
                copy.start()
        value_tile(t, elems, p_s, tv)
        slope_tile(t, elems, p_s, fm_s, tg)
    for copy in numbers:
        copy.wait()
    pl.semaphore_wait(barrier, len(others))
    copies = []
    for k in others:

        def gather(n, carry, k=k):
            base = n * 16
            rows = [rw0[0, k * width + base + u] for u in range(16)]
            for j in range(3):
                found = [tables[j][pl.ds(row, 1), :] for row in rows]
                for u in range(16):
                    send[k, j, pl.ds(base + u, 1), :] = found[u]
            return carry

        lax.fori_loop(0, width // 16, gather, 0)
        copies.append(
            pltpu.make_async_remote_copy(
                src_ref=send.at[k],
                dst_ref=recv.at[8 - k],
                send_sem=send_sem.at[k],
                recv_sem=recv_sem.at[8 - k],
                device_id=peer(k),
                device_id_type=MESH,
            )
        )
        copies[-1].start()
    code_rows(slots, pairs, pad, cb)

    for side, numbers in enumerate((rw1, rw2)):

        def gather_local(n, carry, side=side, numbers=numbers):
            base = n * 16
            rows = [numbers[0, base + u] for u in range(16)]
            for j in range(3):
                found = [tables[j][pl.ds(row, 1), :] for row in rows]
                for u in range(16):
                    locals_[j][pl.ds(side * pair_total + base + u, 1), :] = found[u]
            return carry

        lax.fori_loop(0, pair_total // 16, gather_local, 0)

    group = min(pair_total, 2 * LANES)

    def local_flux(n, carry):
        one = aligned(n * group, group)
        two = aligned(n * group + pair_total, group)
        rows = pl.ds(pl.multiple_of(n * group + slot_total, FACE), group)
        peers = pl.ds(pl.multiple_of(n * group + slot_total + pair_total, FACE), group)
        first = [table[one, :] for table in locals_]
        second = [table[two, :] for table in locals_]
        value, lift = pair_flux(first, second, cb[rows, :])
        vb[rows, :] = value
        hb[rows, :] = lift * spread_metric(first[0])
        back = lane_source(cb[peers, :])
        vb[peers, :] = -lane_pick(value, back)
        hb[peers, :] = -lane_pick(lift, back) * spread_metric(second[0])
        return carry

    lax.fori_loop(0, pair_total // group, local_flux, 0)
    for copy in geo + small[2:]:
        copy.wait()

    def volume(h, carry):
        volume_half(h, p_s, g_s, fwd, bwd, vol, s_ref)
        return carry

    lax.fori_loop(0, tiles // 2, volume, 0)
    for copy in copies:
        copy.wait()

    def cross_flux(n, carry):
        for shift in (0, 1, 5, 6):
            k = 2 * n + shift
            rows = aligned(k * width, FACE)
            turn = cb[rows, :]
            own = [send[k, j] for j in range(3)]
            value, lift = pair_flux(own, [recv[k, j] for j in range(3)], turn)
            live = turn >= 256
            vb[rows, :] = jnp.where(live, value, 0.0)
            hb[rows, :] = jnp.where(live, lift * spread_metric(own[0]), 0.0)
        return carry

    lax.fori_loop(0, 2, cross_flux, 0)
    vb[4 * width : 5 * width, :] = jnp.zeros((width, LANES), jnp.float32)
    hb[4 * width : 5 * width, :] = jnp.zeros((width, LANES), jnp.float32)


def combine_kernel(
    slots, pairs, vb, hb, vol, rhs, lift_ref, modes,
    res, cs,
    vt, lt, fv, fl, st0, st1, st2, rw0, rw1, rw2, row_sem,
):
    elems = vt.shape[0] // 6
    tiles = elems // LANES
    slot_total = slots.shape[2]
    pair_total = pairs.shape[1]
    fields = 2
    numbers = row_numbers(slots, pairs, elems, (st0, st1, st2), (rw0, rw1, rw2), row_sem)
    for copy in numbers:
        copy.start()

    def clear(n, carry):
        rows = aligned(n * LANES, LANES)
        zero = jnp.zeros((LANES, LANES), jnp.float32)
        vt[rows, :] = zero
        lt[rows, :] = zero
        return carry

    lax.fori_loop(0, vt.shape[0] // LANES, clear, 0)
    for copy in numbers:
        copy.wait()
    for start, count, numbers in (
        (0, slot_total, rw0),
        (slot_total, pair_total, rw1),
        (slot_total + pair_total, pair_total, rw2),
    ):

        def scatter(n, carry, start=start, numbers=numbers):
            base = n * 16
            rows = [numbers[0, base + u] for u in range(16)]
            for source, table in ((vb, vt), (hb, lt)):
                found = [source[pl.ds(start + base + u, 1), :] for u in range(16)]
                for u in range(16):
                    table[pl.ds(rows[u], 1), :] = found[u]
            return carry

        lax.fori_loop(0, count // 16, scatter, 0)

    for face in range(6):
        for t in range(tiles):
            rows = slice(face * elems + t * LANES, face * elems + (t + 1) * LANES)
            value = vt[rows, :].T
            lift = lt[rows, :].T
            for f in range(fields):
                fv[t, f, face] = value[f * FACE : (f + 1) * FACE]
                fl[t, f, face] = lift[f * FACE : (f + 1) * FACE]

    half = 2 * LANES

    def finish(n, carry):
        f = n // (tiles // 2)
        h = n % (tiles // 2)
        cols = aligned(h * half, half)

        def wide(ref, *where):
            return jnp.concatenate([ref[2 * h, *where], ref[2 * h + 1, *where]], axis=-1)

        low_lift = wide(fl, f, 0)
        high_lift = wide(fl, f, 1)
        coarse = [None, None]
        for i in range(NODES):
            part = slice(i * NODES, (i + 1) * NODES)
            stack = []
            for face in range(2, 6):
                stack += [wide(fv, f, face, part), wide(fl, f, face, part)]
            rows = aligned(f * BRICK + i * FACE, FACE)
            value = rhs[f, i, :, cols] - wide(vol, rows)
            value = value - product(lift_ref[...], jnp.concatenate(stack, axis=0))
            value = value + float(DERIV[0, i]) * low_lift - float(DERIV[-1, i]) * high_lift
            if i == 0:
                value = value - wide(fv, f, 0)
            if i == NODES - 1:
                value = value - wide(fv, f, 1)
            res[f, i, :, cols] = value
            for a in range(2):
                if MODES[i, a] != 0.0:
                    term = float(MODES[i, a]) * value
                    coarse[a] = term if coarse[a] is None else coarse[a] + term
        for a in range(2):
            for b in range(2):
                layers = [coarse[a][j * NODES : (j + 1) * NODES] for j in range(NODES)]
                level = weighted(MODES[:, b], layers)
                for c in range(2):
                    column = modes[c * NODES : (c + 1) * NODES, 0:1]
                    row = f * NODES + 4 * a + 2 * b + c
                    cs[pl.ds(row, 1), cols] = jnp.sum(level * column, axis=0, keepdims=True)
        return carry

    lax.fori_loop(0, fields * tiles // 2, finish, 0)


def reduce_kernel(n_sub, coarse_ref, cells, total_ref, sums_ref, box, send_sem, recv_sem):
    place = lax.axis_index("blk")
    sub = lax.axis_index("sub")
    barrier = pltpu.get_barrier_semaphore()
    peers = [(place, lax.rem(sub + step, n_sub)) for step in range(1, n_sub)]
    for peer in peers:
        pl.semaphore_signal(barrier, inc=1, device_id=peer, device_id_type=MESH)
    row_cells = sums_ref.shape[1]
    coarse = coarse_ref[...]
    hot = lax.broadcasted_iota(jnp.int32, (row_cells, coarse.shape[1]), 0) == cells[...]
    hot = hot.astype(jnp.float32).astype(jnp.bfloat16)
    high = coarse.astype(jnp.bfloat16)
    low = (coarse - high.astype(jnp.float32)).astype(jnp.bfloat16)
    both = lax.dot_general(
        jnp.concatenate([high, low], axis=0),
        hot,
        (((1,), (1,)), ((), ())),
        preferred_element_type=jnp.float32,
    )
    sums_ref[...] = both[: coarse.shape[0]] + both[coarse.shape[0] :]
    pl.semaphore_wait(barrier, n_sub - 1)
    copies = []
    for step, peer in enumerate(peers):
        copies.append(
            pltpu.make_async_remote_copy(
                src_ref=sums_ref,
                dst_ref=box.at[step],
                send_sem=send_sem.at[step],
                recv_sem=recv_sem.at[step],
                device_id=peer,
                device_id_type=MESH,
            )
        )
        copies[-1].start()
    for copy in copies:
        copy.wait()
    total = sums_ref[...]
    for step in range(n_sub - 1):
        total = total + box[step]
    total_ref[...] = total


def correct_kernel(total_ref, inverse_ref, cells_ref, modes_ref, p_ref, out_ref):
    fields = p_ref.shape[0]
    elems = p_ref.shape[-1]
    row_cells = total_ref.shape[1]
    rows = []
    for f in range(fields):
        level = None
        for j in range(NODES):
            term = inverse_ref[j] * total_ref[f * NODES + j : f * NODES + j + 1, :]
            level = term if level is None else level + term
        rows.append(level)
    level = jnp.concatenate(rows, axis=0)
    high = level.astype(jnp.bfloat16)
    low = (level - high.astype(jnp.float32)).astype(jnp.bfloat16)
    hot = lax.broadcasted_iota(jnp.int32, (row_cells, elems), 0) == cells_ref[...]
    hot = hot.astype(jnp.float32).astype(jnp.bfloat16)
    spread = lax.dot_general(
        jnp.concatenate([high, low], axis=0),
        hot,
        (((1,), (0,)), ((), ())),
        preferred_element_type=jnp.float32,
    )
    spread = spread[: level.shape[0]] + spread[level.shape[0] :]
    columns = [modes_ref[c * NODES : (c + 1) * NODES, 0:1] for c in range(2)]
    for f in range(fields):
        planes = []
        for a in range(2):
            lines = []
            for b in range(2):
                start = f * NODES + 4 * a + 2 * b
                lines.append(
                    columns[0] * spread[start : start + 1] + columns[1] * spread[start + 1 : start + 2]
                )
            planes.append([weighted(MODES[j], lines) for j in range(NODES)])
        for j in range(NODES):
            part = slice(j * NODES, (j + 1) * NODES)
            for i in range(NODES):
                grown = weighted(MODES[i], [planes[0][j], planes[1][j]])
                out_ref[f, i, part, :] = p_ref[f, i, part, :] + grown


def whole(shape, space=VMEM):
    return pl.BlockSpec(shape, lambda *_: (0,) * len(shape), memory_space=space)


def limits(mib, **extra):
    return pltpu.CompilerParams(vmem_limit_bytes=mib << 20, **extra)


def shaped(*shape):
    return jax.ShapeDtypeStruct(shape, jnp.float32)


def on_device(
    n_blk,
    n_sub,
    pressure,
    right_side,
    geometry,
    face_weight,
    face_metric,
    cross_slots,
    local_pairs,
    coarse_map,
    coarse_inverse,
):
    fields = pressure.shape[0]
    elems = pressure.shape[-1]
    slot_total = cross_slots.shape[2]
    pair_total = local_pairs.shape[1]
    row_cells = coarse_inverse.shape[-1]
    tiles = elems // LANES
    width = slot_total // 9
    slabs = (fields, NODES, FACE, elems)
    rows = fields * BRICK
    p = pressure.reshape(slabs)
    weights = jnp.transpose(face_weight, (1, 0, 2))
    metrics = jnp.transpose(face_metric, (1, 0, 2))
    cells = coarse_map.reshape(1, elems)
    modes = jnp.asarray(np.repeat(MODES.T.reshape(2 * NODES, 1), LANES, axis=1), jnp.float32)
    pad_width = -(-slot_total // LANES) * LANES
    side_total = slot_total + 2 * pair_total
    f32 = jnp.float32
    i32 = jnp.int32
    inside = pl.BlockSpec(memory_space=VMEM)
    outside = pl.BlockSpec(memory_space=pltpu.MemorySpace.HBM)
    number_scratch = [
        pltpu.VMEM((1, slot_total), i32),
        pltpu.VMEM((1, pair_total), i32),
        pltpu.VMEM((1, pair_total), i32),
        pltpu.SMEM((1, slot_total), i32),
        pltpu.SMEM((1, pair_total), i32),
        pltpu.SMEM((1, pair_total), i32),
    ]
    dma = pltpu.SemaphoreType.DMA

    volume, values, lifts = pl.pallas_call(
        functools.partial(front_kernel, n_blk, n_sub),
        in_specs=[outside] * 8,
        out_specs=[inside] * 3,
        out_shape=[shaped(tiles, rows, LANES), shaped(side_total, LANES), shaped(side_total, LANES)],
        scratch_shapes=[
            pltpu.VMEM(cross_slots.shape, i32),
            pltpu.VMEM(local_pairs.shape, i32),
            pltpu.VMEM((FACE, 3 * FACE), jnp.bfloat16),
            pltpu.VMEM((FACE, 3 * FACE), jnp.bfloat16),
            pltpu.VMEM((tiles, rows, LANES), f32),
            pltpu.VMEM((tiles, 6, FACE, LANES), f32),
            pltpu.VMEM((tiles, 6, FACE, LANES), f32),
            pltpu.VMEM((tiles, 6 * BRICK, LANES), f32),
            pltpu.VMEM((rows, 2 * LANES), f32),
        ]
        + [pltpu.VMEM((6 * elems, LANES), f32)] * 3
        + [pltpu.VMEM((2 * pair_total, LANES), f32)] * 3
        + [
            pltpu.VMEM((side_total, LANES), i32),
            pltpu.VMEM((8, pad_width), f32),
            pltpu.VMEM((9, 3, width, LANES), f32),
            pltpu.VMEM((9, 3, width, LANES), f32),
        ]
        + number_scratch
        + [dma((4,)), dma((tiles, 3)), dma((tiles,)), dma((3,)), dma((9,)), dma((9,))],
        compiler_params=limits(36, collective_id=0, has_side_effects=True),
        name="front",
    )(
        *[
            pltpu.with_memory_space_constraint(value, pltpu.MemorySpace.HBM)
            for value in (
                cross_slots,
                local_pairs,
                pressure.reshape(rows, elems),
                weights,
                metrics,
                geometry.reshape(6 * BRICK, elems),
                jnp.asarray(forward_table()),
                jnp.asarray(backward_table()),
            )
        ]
    )

    residual, coarse = pl.pallas_call(
        combine_kernel,
        in_specs=[inside] * 8,
        out_specs=[inside] * 2,
        out_shape=[shaped(*slabs), shaped(fields * NODES, elems)],
        scratch_shapes=[
            pltpu.VMEM((6 * elems, LANES), f32),
            pltpu.VMEM((6 * elems, LANES), f32),
            pltpu.VMEM((tiles, fields, 6, FACE, LANES), f32),
            pltpu.VMEM((tiles, fields, 6, FACE, LANES), f32),
        ]
        + number_scratch
        + [dma((3,))],
        compiler_params=limits(32),
        name="combine",
    )(
        cross_slots,
        local_pairs,
        values,
        lifts,
        volume,
        right_side.reshape(slabs),
        jnp.asarray(lift_table()),
        modes,
    )

    totals = pl.pallas_call(
        functools.partial(reduce_kernel, n_sub),
        in_specs=[inside] * 2,
        out_specs=inside,
        out_shape=shaped(fields * NODES, row_cells),
        scratch_shapes=[
            pltpu.VMEM((fields * NODES, row_cells), f32),
            pltpu.VMEM((n_sub - 1, fields * NODES, row_cells), f32),
            dma((n_sub - 1,)),
            dma((n_sub - 1,)),
        ],
        compiler_params=limits(8, collective_id=1, has_side_effects=True),
        name="reduce",
    )(coarse, cells)

    chunk = min(elems, 256)
    corrected = pl.pallas_call(
        correct_kernel,
        grid=(elems // chunk,),
        in_specs=[
            whole((fields * NODES, row_cells)),
            whole((NODES, NODES, row_cells)),
            pl.BlockSpec((1, chunk), lambda t: (0, t)),
            whole((2 * NODES, LANES)),
            pl.BlockSpec((fields, NODES, FACE, chunk), lambda t: (0, 0, 0, t)),
        ],
        out_specs=pl.BlockSpec((fields, NODES, FACE, chunk), lambda t: (0, 0, 0, t)),
        out_shape=shaped(*slabs),
        compiler_params=limits(32),
        name="correct",
    )(totals, coarse_inverse, cells, modes, p)
    return residual.reshape(pressure.shape), corrected.reshape(pressure.shape)


def solution(mesh):
    return jax.shard_map(
        functools.partial(on_device, mesh.shape["blk"], mesh.shape["sub"]),
        mesh=mesh,
        in_specs=(
            P(None, None, None, None, ("blk", "sub")),
            P(None, None, None, None, ("blk", "sub")),
            P(None, None, None, None, ("blk", "sub")),
            P(None, None, ("blk", "sub")),
            P(None, None, ("blk", "sub")),
            P(None, ("blk", "sub"), None),
            P(None, ("blk", "sub")),
            P(("blk", "sub")),
            P(None, None, "blk"),
        ),
        out_specs=(
            P(None, None, None, None, ("blk", "sub")),
            P(None, None, None, None, ("blk", "sub")),
        ),
        check_vma=False,
    )
```

```python
import functools

import jax
import jax.numpy as jnp
import numpy as np
from jax import lax
from jax.experimental import pallas as pl
from jax.experimental.pallas import tpu as pltpu
from jax.sharding import PartitionSpec as P

NODES = 8
FACE = NODES * NODES
BRICK = NODES * FACE
LANES = 128
MESH = pl.DeviceIdType.MESH
VMEM = pltpu.MemorySpace.VMEM
SMEM = pltpu.MemorySpace.SMEM


def node_points():
    positive = [0.2092992179024789, 0.5917001814331423, 0.8717401485096066, 1.0]
    return np.array(sorted([-entry for entry in positive] + positive))


def derivative_matrix():
    points = node_points()
    count = len(points)
    weights = np.array(
        [
            1.0 / np.prod([points[row] - points[col] for col in range(count) if col != row])
            for row in range(count)
        ]
    )
    matrix = np.zeros((count, count))
    for row in range(count):
        for col in range(count):
            if row != col:
                matrix[row, col] = weights[col] / weights[row] / (points[row] - points[col])
        matrix[row, row] = -np.sum(matrix[row])
    return matrix


DERIV = derivative_matrix()
POINTS = node_points()
MODES = np.stack([(1.0 - POINTS) / 2.0, (1.0 + POINTS) / 2.0], axis=1)


def split_constant(matrix):
    high = matrix.astype(jnp.bfloat16)
    low = (matrix - high.astype(np.float64)).astype(jnp.bfloat16)
    return np.concatenate([high, low, high], axis=1)


def forward_table():
    eye = np.eye(NODES)
    return split_constant(np.kron(eye, DERIV))


def backward_table():
    eye = np.eye(NODES)
    return split_constant(np.kron(eye, DERIV.T))


def lift_table():
    eye = np.eye(NODES)
    rows = [eye[:, :1], -DERIV[:1].T, eye[:, -1:], DERIV[-1:].T]
    second = [np.kron(row, eye) for row in rows]
    third = [np.kron(eye, row) for row in rows]
    return split_constant(np.concatenate(second + third, axis=1))


def split_rows(values):
    high = values.astype(jnp.bfloat16)
    low = (values - high.astype(jnp.float32)).astype(jnp.bfloat16)
    return jnp.concatenate([high, high, low], axis=0)


def product(table, values):
    return lax.dot_general(
        table, split_rows(values), (((1,), (0,)), ((), ())), preferred_element_type=jnp.float32
    )


def even_odd(matrix, layers):
    half = NODES // 2
    sums = [layers[k] + layers[NODES - 1 - k] for k in range(half)]
    gaps = [layers[k] - layers[NODES - 1 - k] for k in range(half)]
    result = [None] * NODES
    for row in range(half):
        even = None
        odd = None
        for k in range(half):
            first = float((matrix[row, k] + matrix[row, NODES - 1 - k]) / 2)
            second = float((matrix[row, k] - matrix[row, NODES - 1 - k]) / 2)
            even = first * sums[k] if even is None else even + first * sums[k]
            odd = second * gaps[k] if odd is None else odd + second * gaps[k]
        result[row] = odd + even
        result[NODES - 1 - row] = odd - even
    return result


def weighted(coefficients, layers):
    total = None
    for factor, layer in zip(coefficients, layers):
        term = float(factor) * layer
        total = term if total is None else total + term
    return total


def turn_code(code, inverse):
    first = code & 1
    second = (code >> 1) & 1
    swap = (code >> 2) & 1
    if inverse:
        first, second = (
            jnp.where(swap != 0, second, first),
            jnp.where(swap != 0, first, second),
        )
    return first * 56 + second * 7 + swap * 128


def lane_pick(values, index):
    return jnp.take_along_axis(values, index, axis=1, mode="promise_in_bounds")


def lane_source(turn):
    lane = lax.broadcasted_iota(jnp.int32, turn.shape, 1)
    swapped = ((lane & 7) << 3) | ((lane >> 3) & 7) | (lane & FACE)
    return (jnp.where((turn & 128) != 0, swapped, lane) ^ turn) & (LANES - 1)


def spread_metric(both):
    low = lax.broadcasted_iota(jnp.int32, both.shape, 1) < FACE
    return jnp.where(low, pltpu.roll(both, FACE, 1), both)


def pair_flux(own, peer, turn):
    wm1, v1, g1 = own
    wm2, v2, g2 = peer
    source = lane_source(turn)
    low = lax.broadcasted_iota(jnp.int32, turn.shape, 1) < FACE
    penalty = NODES * (NODES + 1) / 2.0
    jump = v1 - lane_pick(v2, source)
    gap = g1 - lane_pick(g2, source)
    total = wm1 + lane_pick(wm2, source)
    turned = pltpu.roll(total, FACE, 1)
    weight = 0.5 * jnp.where(low, total, turned)
    tau = (penalty * 0.5) * jnp.where(low, turned, total)
    return weight * (tau * jump - 0.5 * gap), -0.5 * weight * jump


def row_numbers(slots, pairs, elems, staged, rows, sem):
    staged[0][...] = slots[1] * elems + slots[0]
    staged[1][...] = pairs[1:2] * elems + pairs[0:1]
    staged[2][...] = pairs[3:4] * elems + pairs[2:3]
    return [pltpu.make_async_copy(staged[n], rows[n], sem.at[n]) for n in range(3)]


def code_rows(slots, pairs, pad, cb):
    slot_total = slots.shape[2]
    pair_total = pairs.shape[1]
    raw = slots[4]
    code = jnp.where(slots[3] != 0, turn_code(raw, False), turn_code(raw, True)) + 256 * slots[2]
    pad[0:1, 0:slot_total] = code.astype(jnp.float32)
    pad[0:1, slot_total:] = jnp.zeros((1, pad.shape[1] - slot_total), jnp.float32)
    for t in range(pad.shape[1] // LANES):
        row = jnp.broadcast_to(pad[0:1, t * LANES : (t + 1) * LANES], (LANES, LANES))
        count = min(LANES, slot_total - t * LANES)
        cb[t * LANES : t * LANES + count, :] = row.T.astype(jnp.int32)[:count]
    local = pairs[4:5, :]
    for side, codes in enumerate((turn_code(local, False), turn_code(local, True))):
        for t in range(pair_total // LANES):
            row = codes[:, t * LANES : (t + 1) * LANES].astype(jnp.float32)
            start = slot_total + side * pair_total + t * LANES
            cb[start : start + LANES, :] = jnp.broadcast_to(row, (LANES, LANES)).T.astype(jnp.int32)


def aligned(start, size):
    return pl.ds(pl.multiple_of(start, size), size)


def node_layers(t, axis, start, p_s):
    layers = []
    for k in range(NODES):
        if axis == 0:
            layers.append(p_s[t, start + k * FACE : start + (k + 1) * FACE, :])
        elif axis == 1:
            rows = [
                p_s[t, start + i * FACE + k * NODES : start + i * FACE + (k + 1) * NODES, :]
                for i in range(NODES)
            ]
            layers.append(jnp.concatenate(rows, axis=0))
        else:
            layers.append(p_s[t, pl.ds(start + k, FACE, stride=NODES), :])
    return layers


def face_rows(face, t, elems):
    return aligned(face * elems + t * LANES, LANES)


def fixed_tile(t, elems, fw_s, fm_s, table):
    for face in range(6):
        both = jnp.concatenate([fw_s[t, face], fm_s[t, face]], axis=0)
        table[face_rows(face, t, elems), :] = both.T


def value_tile(t, elems, p_s, table):
    for axis in range(3):
        for side in range(2):
            ends = []
            for start in range(0, p_s.shape[1], BRICK):
                k = side * (NODES - 1)
                if axis == 0:
                    ends.append(p_s[t, start + k * FACE : start + (k + 1) * FACE, :])
                elif axis == 1:
                    ends += [
                        p_s[t, start + i * FACE + k * NODES : start + i * FACE + (k + 1) * NODES, :]
                        for i in range(NODES)
                    ]
                else:
                    ends.append(p_s[t, pl.ds(start + k, FACE, stride=NODES), :])
            table[face_rows(2 * axis + side, t, elems), :] = jnp.concatenate(ends, axis=0).T


def slope_tile(t, elems, p_s, fm_s, table):
    for axis in range(3):
        slopes = []
        for start in range(0, p_s.shape[1], BRICK):
            layers = node_layers(t, axis, start, p_s)
            slopes.append((weighted(-DERIV[0], layers), weighted(DERIV[-1], layers)))
        for side in range(2):
            face = 2 * axis + side
            slope = jnp.concatenate([entry[side] * fm_s[t, face] for entry in slopes], axis=0)
            table[face_rows(face, t, elems), :] = slope.T


def volume_half(h, p_s, g_s, rhs_s, fwd, bwd, out, z, s_ref):
    fields = p_s.shape[1] // BRICK
    tiles = (2 * h, 2 * h + 1)

    def wide(ref, rows):
        return jnp.concatenate([ref[tiles[0], rows, :], ref[tiles[1], rows, :]], axis=1)

    def first(n, carry):
        f = n // NODES
        r = n % NODES
        where = [aligned(f * BRICK + k * FACE + r * NODES, NODES) for k in range(NODES)]
        for q, value in enumerate(even_odd(DERIV, [wide(p_s, rows) for rows in where])):
            s_ref[where[q], :] = value
        return carry

    lax.fori_loop(0, fields * NODES, first, 0, unroll=4)

    def middle(i, carry):
        g = [wide(g_s, aligned(n * BRICK + i * FACE, FACE)) for n in range(6)]
        for f in range(fields):
            rows = aligned(f * BRICK + i * FACE, FACE)
            x = wide(p_s, rows)
            s3 = product(fwd[...], x)
            s2 = jnp.concatenate(
                even_odd(DERIV, [x[j * NODES : (j + 1) * NODES] for j in range(NODES)]), axis=0
            )
            s1 = s_ref[rows, :]
            q1 = g[0] * s1 + g[3] * s2 + g[4] * s3
            q2 = g[3] * s1 + g[1] * s2 + g[5] * s3
            q3 = g[4] * s1 + g[5] * s2 + g[2] * s3
            s_ref[rows, :] = q1
            r2 = jnp.concatenate(
                even_odd(DERIV.T, [q2[j * NODES : (j + 1) * NODES] for j in range(NODES)]), axis=0
            )
            r23 = product(bwd[...], q3) + r2
            out[tiles[0], rows, :] = r23[:, :LANES]
            out[tiles[1], rows, :] = r23[:, LANES:]
        return carry

    lax.fori_loop(0, NODES, middle, 0, unroll=4)

    def last(n, carry):
        f = n // NODES
        r = n % NODES
        where = [aligned(f * BRICK + k * FACE + r * NODES, NODES) for k in range(NODES)]
        left = []
        for q, value in enumerate(even_odd(DERIV.T, [s_ref[rows, :] for rows in where])):
            left.append(wide(rhs_s, where[q]) - (wide(out, where[q]) + value))
            out[tiles[0], where[q], :] = left[q][:, :LANES]
            out[tiles[1], where[q], :] = left[q][:, LANES:]
        for a in range(2):
            rows = aligned((2 * f + a) * FACE + r * NODES, NODES)
            level = weighted(MODES[:, a], left)
            z[tiles[0], rows, :] = level[:, :LANES]
            z[tiles[1], rows, :] = level[:, LANES:]
        return carry

    lax.fori_loop(0, fields * NODES, last, 0, unroll=4)


def front_kernel(
    n_blk, n_sub,
    slots_hbm, pairs_hbm, p_hbm, fw_hbm, fm_hbm, g_hbm, rhs_hbm, fwd_hbm, bwd_hbm,
    rest, z, vb, hb,
    slots, pairs, fwd, bwd, p_s, fw_s, fm_s, g_s, rhs_s, s_ref, tv, tg, tw, la, lb, lc, cb, pad, send, recv,
    st0, st1, st2, rw0, rw1, rw2,
    small_sem, load_sem, geo_sem, row_sem, send_sem, recv_sem,
):
    elems = tv.shape[0] // 6
    tiles = elems // LANES
    slot_total = slots.shape[2]
    pair_total = pairs.shape[1]
    width = slot_total // 9
    tables = (tw, tv, tg)
    locals_ = (la, lb, lc)
    place = lax.axis_index("blk")
    sub = lax.axis_index("sub")

    def peer(k):
        return (
            lax.rem(place + (k // 3 - 1) + n_blk, n_blk),
            lax.rem(sub + (k % 3 - 1) + n_sub, n_sub),
        )

    others = [2, 0, 8, 6, 5, 3, 1, 7]
    barrier = pltpu.get_barrier_semaphore()
    for k in others:
        pl.semaphore_signal(barrier, inc=1, device_id=peer(k), device_id_type=MESH)
    small = [
        pltpu.make_async_copy(source, target, small_sem.at[n])
        for n, (source, target) in enumerate(
            ((slots_hbm, slots), (pairs_hbm, pairs), (fwd_hbm, fwd), (bwd_hbm, bwd))
        )
    ]
    for copy in small[:2]:
        copy.start()
    loads = []
    geo = []
    for t in range(tiles):
        cols = pl.ds(t * LANES, LANES)
        geo.append(pltpu.make_async_copy(g_hbm.at[:, cols], g_s.at[t], geo_sem.at[t, 0]))
        geo.append(pltpu.make_async_copy(rhs_hbm.at[:, cols], rhs_s.at[t], geo_sem.at[t, 1]))
        loads.append(
            [
                pltpu.make_async_copy(fw_hbm.at[:, :, cols], fw_s.at[t], load_sem.at[t, 0]),
                pltpu.make_async_copy(fm_hbm.at[:, :, cols], fm_s.at[t], load_sem.at[t, 1]),
                pltpu.make_async_copy(p_hbm.at[:, cols], p_s.at[t], load_sem.at[t, 2]),
            ]
        )
    for t in range(tiles):
        loads[t][0].start()
        loads[t][1].start()
    for t in range(tiles):
        loads[t][2].start()
    for copy in small[:2]:
        copy.wait()
    numbers = row_numbers(slots, pairs, elems, (st0, st1, st2), (rw0, rw1, rw2), row_sem)
    for copy in numbers:
        copy.start()
    for t in range(tiles):
        loads[t][0].wait()
        loads[t][1].wait()
        fixed_tile(t, elems, fw_s, fm_s, tw)
    for t in range(tiles):
        loads[t][2].wait()
        if t == tiles - 1:
            for copy in geo + small[2:]:
                copy.start()
        value_tile(t, elems, p_s, tv)
        slope_tile(t, elems, p_s, fm_s, tg)
    for copy in numbers:
        copy.wait()
    pl.semaphore_wait(barrier, len(others))
    copies = []
    for k in others:

        def gather(n, carry, k=k):
            base = n * 16
            rows = [rw0[0, k * width + base + u] for u in range(16)]
            for j in range(3):
                found = [tables[j][pl.ds(row, 1), :] for row in rows]
                for u in range(16):
                    send[k, j, pl.ds(base + u, 1), :] = found[u]
            return carry

        lax.fori_loop(0, width // 16, gather, 0)
        copies.append(
            pltpu.make_async_remote_copy(
                src_ref=send.at[k],
                dst_ref=recv.at[8 - k],
                send_sem=send_sem.at[k],
                recv_sem=recv_sem.at[8 - k],
                device_id=peer(k),
                device_id_type=MESH,
            )
        )
        copies[-1].start()
    code_rows(slots, pairs, pad, cb)

    for side, numbers in enumerate((rw1, rw2)):

        def gather_local(n, carry, side=side, numbers=numbers):
            base = n * 16
            rows = [numbers[0, base + u] for u in range(16)]
            for j in range(3):
                found = [tables[j][pl.ds(row, 1), :] for row in rows]
                for u in range(16):
                    locals_[j][pl.ds(side * pair_total + base + u, 1), :] = found[u]
            return carry

        lax.fori_loop(0, pair_total // 16, gather_local, 0)

    group = min(pair_total, 2 * LANES)

    def local_flux(n, carry):
        one = aligned(n * group, group)
        two = aligned(n * group + pair_total, group)
        rows = pl.ds(pl.multiple_of(n * group + slot_total, FACE), group)
        peers = pl.ds(pl.multiple_of(n * group + slot_total + pair_total, FACE), group)
        first = [table[one, :] for table in locals_]
        second = [table[two, :] for table in locals_]
        value, lift = pair_flux(first, second, cb[rows, :])
        vb[rows, :] = value
        hb[rows, :] = lift * spread_metric(first[0])
        back = lane_source(cb[peers, :])
        vb[peers, :] = -lane_pick(value, back)
        hb[peers, :] = -lane_pick(lift, back) * spread_metric(second[0])
        return carry

    lax.fori_loop(0, pair_total // group, local_flux, 0)
    for copy in geo + small[2:]:
        copy.wait()

    def volume(h, carry):
        volume_half(h, p_s, g_s, rhs_s, fwd, bwd, rest, z, s_ref)
        return carry

    lax.fori_loop(0, tiles // 2, volume, 0)
    for copy in copies:
        copy.wait()

    def cross_flux(n, carry):
        for shift in (0, 1, 5, 6):
            k = 2 * n + shift
            rows = aligned(k * width, FACE)
            turn = cb[rows, :]
            own = [send[k, j] for j in range(3)]
            value, lift = pair_flux(own, [recv[k, j] for j in range(3)], turn)
            live = turn >= 256
            vb[rows, :] = jnp.where(live, value, 0.0)
            hb[rows, :] = jnp.where(live, lift * spread_metric(own[0]), 0.0)
        return carry

    lax.fori_loop(0, 2, cross_flux, 0)
    vb[4 * width : 5 * width, :] = jnp.zeros((width, LANES), jnp.float32)
    hb[4 * width : 5 * width, :] = jnp.zeros((width, LANES), jnp.float32)


def scatter_kernel(slots, pairs, vb, hb, vt, lt, st0, st1, st2, rw0, rw1, rw2, row_sem):
    elems = vt.shape[0] // 6
    slot_total = slots.shape[2]
    pair_total = pairs.shape[1]
    numbers = row_numbers(slots, pairs, elems, (st0, st1, st2), (rw0, rw1, rw2), row_sem)
    for copy in numbers:
        copy.start()

    def clear(n, carry):
        rows = aligned(n * LANES, LANES)
        zero = jnp.zeros((LANES, LANES), jnp.float32)
        vt[rows, :] = zero
        lt[rows, :] = zero
        return carry

    lax.fori_loop(0, vt.shape[0] // LANES, clear, 0)
    for copy in numbers:
        copy.wait()
    for start, count, numbers in (
        (0, slot_total, rw0),
        (slot_total, pair_total, rw1),
        (slot_total + pair_total, pair_total, rw2),
    ):

        def scatter(n, carry, start=start, numbers=numbers):
            base = n * 16
            rows = [numbers[0, base + u] for u in range(16)]
            for source, table in ((vb, vt), (hb, lt)):
                found = [source[pl.ds(start + base + u, 1), :] for u in range(16)]
                for u in range(16):
                    table[pl.ds(rows[u], 1), :] = found[u]
            return carry

        lax.fori_loop(0, count // 16, scatter, 0)


def reduce_kernel(
    n_sub,
    vt, lt, rest, z, lift_ref, modes, cells,
    total_ref, res,
    fv, fl, cs, sums_ref, box, send_sem, recv_sem,
):
    elems = vt.shape[0] // 6
    tiles = elems // LANES
    fields = fv.shape[1]
    place = lax.axis_index("blk")
    sub = lax.axis_index("sub")
    barrier = pltpu.get_barrier_semaphore()
    peers = [(place, lax.rem(sub + step, n_sub)) for step in range(1, n_sub)]
    for peer in peers:
        pl.semaphore_signal(barrier, inc=1, device_id=peer, device_id_type=MESH)

    for face in range(6):
        for t in range(tiles):
            rows = slice(face * elems + t * LANES, face * elems + (t + 1) * LANES)
            value = vt[rows, :].T
            lift = lt[rows, :].T
            for f in range(fields):
                fv[t, f, face] = value[f * FACE : (f + 1) * FACE]
                fl[t, f, face] = lift[f * FACE : (f + 1) * FACE]

    half = 2 * LANES
    slopes = (-DERIV[0] @ MODES, DERIV[-1] @ MODES)

    def halves(n):
        f = n // (tiles // 2)
        h = n % (tiles // 2)

        def wide(ref, *where):
            return jnp.concatenate([ref[2 * h, *where], ref[2 * h + 1, *where]], axis=-1)

        return f, h, wide

    def groups(layer):
        return [layer[k * NODES : (k + 1) * NODES] for k in range(NODES)]

    def restrict(n, carry):
        f, h, wide = halves(n)
        cols = aligned(h * half, half)
        faces = []
        for axis in range(3):
            v0, l0 = wide(fv, f, 2 * axis), wide(fl, f, 2 * axis)
            v1, l1 = wide(fv, f, 2 * axis + 1), wide(fl, f, 2 * axis + 1)
            modes_here = []
            for m in range(2):
                level = float(slopes[0][m]) * l0 + float(slopes[1][m]) * l1
                modes_here.append(level + (v0 if m == 0 else v1))
            faces.append(modes_here)
        for a in range(2):
            first = groups(wide(z, aligned((2 * f + a) * FACE, FACE)) - faces[0][a])
            third = [weighted(MODES[:, a], groups(faces[2][c])) for c in range(2)]
            for b in range(2):
                level = weighted(MODES[:, b], first) - weighted(MODES[:, a], groups(faces[1][b]))
                for c in range(2):
                    column = modes[c * NODES : (c + 1) * NODES, 0:1]
                    other = modes[b * NODES : (b + 1) * NODES, 0:1]
                    row = f * NODES + 4 * a + 2 * b + c
                    value = level * column - third[c] * other
                    cs[pl.ds(row, 1), cols] = jnp.sum(value, axis=0, keepdims=True)
        return carry

    lax.fori_loop(0, fields * tiles // 2, restrict, 0)

    row_cells = sums_ref.shape[1]
    coarse = cs[...]
    hot = lax.broadcasted_iota(jnp.int32, (row_cells, elems), 0) == cells[...]
    hot = hot.astype(jnp.float32).astype(jnp.bfloat16)
    high = coarse.astype(jnp.bfloat16)
    low = (coarse - high.astype(jnp.float32)).astype(jnp.bfloat16)
    both = lax.dot_general(
        jnp.concatenate([high, low], axis=0),
        hot,
        (((1,), (1,)), ((), ())),
        preferred_element_type=jnp.float32,
    )
    sums_ref[...] = both[: coarse.shape[0]] + both[coarse.shape[0] :]
    pl.semaphore_wait(barrier, n_sub - 1)
    copies = []
    for step, peer in enumerate(peers):
        copies.append(
            pltpu.make_async_remote_copy(
                src_ref=sums_ref,
                dst_ref=box.at[step],
                send_sem=send_sem.at[step],
                recv_sem=recv_sem.at[step],
                device_id=peer,
                device_id_type=MESH,
            )
        )
        copies[-1].start()

    def finish(n, carry):
        f, h, wide = halves(n)
        low_lift = wide(fl, f, 0)
        high_lift = wide(fl, f, 1)
        for i in range(NODES):
            part = slice(i * NODES, (i + 1) * NODES)
            stack = []
            for face in range(2, 6):
                stack += [wide(fv, f, face, part), wide(fl, f, face, part)]
            rows = aligned(f * BRICK + i * FACE, FACE)
            value = wide(rest, rows) - product(lift_ref[...], jnp.concatenate(stack, axis=0))
            value = value + float(DERIV[0, i]) * low_lift - float(DERIV[-1, i]) * high_lift
            if i == 0:
                value = value - wide(fv, f, 0)
            if i == NODES - 1:
                value = value - wide(fv, f, 1)
            res[2 * h, rows, :] = value[:, :LANES]
            res[2 * h + 1, rows, :] = value[:, LANES:]
        return carry

    lax.fori_loop(0, fields * tiles // 2, finish, 0)
    for copy in copies:
        copy.wait()
    total = sums_ref[...]
    for step in range(n_sub - 1):
        total = total + box[step]
    total_ref[...] = total


def correct_kernel(
    total_ref, inverse_ref, cells_ref, modes_ref, p_ref, tiled, out_ref, res_hbm, res_sem
):
    copies = [
        pltpu.make_async_copy(tiled.at[t], res_hbm.at[:, pl.ds(t * LANES, LANES)], res_sem.at[t])
        for t in range(tiled.shape[0])
    ]

    @pl.when(pl.program_id(0) == 0)
    def _():
        for copy in copies:
            copy.start()

    fields = p_ref.shape[0]
    elems = p_ref.shape[-1]
    row_cells = total_ref.shape[1]
    rows = []
    for f in range(fields):
        level = None
        for j in range(NODES):
            term = inverse_ref[j] * total_ref[f * NODES + j : f * NODES + j + 1, :]
            level = term if level is None else level + term
        rows.append(level)
    level = jnp.concatenate(rows, axis=0)
    high = level.astype(jnp.bfloat16)
    low = (level - high.astype(jnp.float32)).astype(jnp.bfloat16)
    hot = lax.broadcasted_iota(jnp.int32, (row_cells, elems), 0) == cells_ref[...]
    hot = hot.astype(jnp.float32).astype(jnp.bfloat16)
    spread = lax.dot_general(
        jnp.concatenate([high, low], axis=0),
        hot,
        (((1,), (0,)), ((), ())),
        preferred_element_type=jnp.float32,
    )
    spread = spread[: level.shape[0]] + spread[level.shape[0] :]
    columns = [modes_ref[c * NODES : (c + 1) * NODES, 0:1] for c in range(2)]
    for f in range(fields):
        planes = []
        for a in range(2):
            lines = []
            for b in range(2):
                start = f * NODES + 4 * a + 2 * b
                lines.append(
                    columns[0] * spread[start : start + 1] + columns[1] * spread[start + 1 : start + 2]
                )
            planes.append([weighted(MODES[j], lines) for j in range(NODES)])
        for j in range(NODES):
            part = slice(j * NODES, (j + 1) * NODES)
            for i in range(NODES):
                grown = weighted(MODES[i], [planes[0][j], planes[1][j]])
                out_ref[f, i, part, :] = p_ref[f, i, part, :] + grown

    @pl.when(pl.program_id(0) == pl.num_programs(0) - 1)
    def _():
        for copy in copies:
            copy.wait()


def whole(shape, space=VMEM):
    return pl.BlockSpec(shape, lambda *_: (0,) * len(shape), memory_space=space)


def limits(mib, **extra):
    return pltpu.CompilerParams(vmem_limit_bytes=mib << 20, **extra)


def shaped(*shape):
    return jax.ShapeDtypeStruct(shape, jnp.float32)


def on_device(
    n_blk,
    n_sub,
    pressure,
    right_side,
    geometry,
    face_weight,
    face_metric,
    cross_slots,
    local_pairs,
    coarse_map,
    coarse_inverse,
):
    fields = pressure.shape[0]
    elems = pressure.shape[-1]
    slot_total = cross_slots.shape[2]
    pair_total = local_pairs.shape[1]
    row_cells = coarse_inverse.shape[-1]
    tiles = elems // LANES
    width = slot_total // 9
    slabs = (fields, NODES, FACE, elems)
    rows = fields * BRICK
    p = pressure.reshape(slabs)
    weights = jnp.transpose(face_weight, (1, 0, 2))
    metrics = jnp.transpose(face_metric, (1, 0, 2))
    cells = coarse_map.reshape(1, elems)
    modes = jnp.asarray(np.repeat(MODES.T.reshape(2 * NODES, 1), LANES, axis=1), jnp.float32)
    pad_width = -(-slot_total // LANES) * LANES
    side_total = slot_total + 2 * pair_total
    f32 = jnp.float32
    i32 = jnp.int32
    inside = pl.BlockSpec(memory_space=VMEM)
    outside = pl.BlockSpec(memory_space=pltpu.MemorySpace.HBM)
    number_scratch = [
        pltpu.VMEM((1, slot_total), i32),
        pltpu.VMEM((1, pair_total), i32),
        pltpu.VMEM((1, pair_total), i32),
        pltpu.SMEM((1, slot_total), i32),
        pltpu.SMEM((1, pair_total), i32),
        pltpu.SMEM((1, pair_total), i32),
    ]
    dma = pltpu.SemaphoreType.DMA

    rest, levels, values, lifts = pl.pallas_call(
        functools.partial(front_kernel, n_blk, n_sub),
        in_specs=[outside] * 9,
        out_specs=[inside] * 4,
        out_shape=[
            shaped(tiles, rows, LANES),
            shaped(tiles, 2 * fields * FACE, LANES),
            shaped(side_total, LANES),
            shaped(side_total, LANES),
        ],
        scratch_shapes=[
            pltpu.VMEM(cross_slots.shape, i32),
            pltpu.VMEM(local_pairs.shape, i32),
            pltpu.VMEM((FACE, 3 * FACE), jnp.bfloat16),
            pltpu.VMEM((FACE, 3 * FACE), jnp.bfloat16),
            pltpu.VMEM((tiles, rows, LANES), f32),
            pltpu.VMEM((tiles, 6, FACE, LANES), f32),
            pltpu.VMEM((tiles, 6, FACE, LANES), f32),
            pltpu.VMEM((tiles, 6 * BRICK, LANES), f32),
            pltpu.VMEM((tiles, rows, LANES), f32),
            pltpu.VMEM((rows, 2 * LANES), f32),
        ]
        + [pltpu.VMEM((6 * elems, LANES), f32)] * 3
        + [pltpu.VMEM((2 * pair_total, LANES), f32)] * 3
        + [
            pltpu.VMEM((side_total, LANES), i32),
            pltpu.VMEM((8, pad_width), f32),
            pltpu.VMEM((9, 3, width, LANES), f32),
            pltpu.VMEM((9, 3, width, LANES), f32),
        ]
        + number_scratch
        + [dma((4,)), dma((tiles, 3)), dma((tiles, 2)), dma((3,)), dma((9,)), dma((9,))],
        compiler_params=limits(36, collective_id=0, has_side_effects=True),
        name="front",
    )(
        *[
            pltpu.with_memory_space_constraint(value, pltpu.MemorySpace.HBM)
            for value in (
                cross_slots,
                local_pairs,
                pressure.reshape(rows, elems),
                weights,
                metrics,
                geometry.reshape(6 * BRICK, elems),
                right_side.reshape(rows, elems),
                jnp.asarray(forward_table()),
                jnp.asarray(backward_table()),
            )
        ]
    )

    value_table, lift_rows = pl.pallas_call(
        scatter_kernel,
        in_specs=[inside] * 4,
        out_specs=[inside] * 2,
        out_shape=[shaped(6 * elems, LANES), shaped(6 * elems, LANES)],
        scratch_shapes=number_scratch + [dma((3,))],
        compiler_params=limits(8),
        name="scatter",
    )(cross_slots, local_pairs, values, lifts)

    totals, tiled = pl.pallas_call(
        functools.partial(reduce_kernel, n_sub),
        in_specs=[inside] * 7,
        out_specs=[inside] * 2,
        out_shape=[shaped(fields * NODES, row_cells), shaped(tiles, rows, LANES)],
        scratch_shapes=[
            pltpu.VMEM((tiles, fields, 6, FACE, LANES), f32),
            pltpu.VMEM((tiles, fields, 6, FACE, LANES), f32),
            pltpu.VMEM((fields * NODES, elems), f32),
            pltpu.VMEM((fields * NODES, row_cells), f32),
            pltpu.VMEM((n_sub - 1, fields * NODES, row_cells), f32),
            dma((n_sub - 1,)),
            dma((n_sub - 1,)),
        ],
        compiler_params=limits(24, collective_id=1, has_side_effects=True),
        name="reduce",
    )(value_table, lift_rows, rest, levels, jnp.asarray(lift_table()), modes, cells)

    chunk = min(elems, 256)
    corrected, residual = pl.pallas_call(
        correct_kernel,
        grid=(elems // chunk,),
        in_specs=[
            whole((fields * NODES, row_cells)),
            whole((NODES, NODES, row_cells)),
            pl.BlockSpec((1, chunk), lambda t: (0, t)),
            whole((2 * NODES, LANES)),
            pl.BlockSpec((fields, NODES, FACE, chunk), lambda t: (0, 0, 0, t)),
            pl.BlockSpec(memory_space=pl.ANY),
        ],
        out_specs=[
            pl.BlockSpec((fields, NODES, FACE, chunk), lambda t: (0, 0, 0, t)),
            pl.BlockSpec(memory_space=pl.ANY),
        ],
        out_shape=[shaped(*slabs), shaped(rows, elems)],
        scratch_shapes=[dma((tiles,))],
        compiler_params=limits(16),
        name="correct",
    )(totals, coarse_inverse, cells, modes, p, tiled)
    return residual.reshape(pressure.shape), corrected.reshape(pressure.shape)


def solution(mesh):
    return jax.shard_map(
        functools.partial(on_device, mesh.shape["blk"], mesh.shape["sub"]),
        mesh=mesh,
        in_specs=(
            P(None, None, None, None, ("blk", "sub")),
            P(None, None, None, None, ("blk", "sub")),
            P(None, None, None, None, ("blk", "sub")),
            P(None, None, ("blk", "sub")),
            P(None, None, ("blk", "sub")),
            P(None, ("blk", "sub"), None),
            P(None, ("blk", "sub")),
            P(("blk", "sub")),
            P(None, None, "blk"),
        ),
        out_specs=(
            P(None, None, None, None, ("blk", "sub")),
            P(None, None, None, None, ("blk", "sub")),
        ),
        check_vma=False,
    )
```

```python
import functools

import jax
import jax.numpy as jnp
import numpy as np
from jax import lax
from jax.experimental import pallas as pl
from jax.experimental.pallas import tpu as pltpu
from jax.sharding import PartitionSpec as P

NODES = 8
FACE = NODES * NODES
BRICK = NODES * FACE
LANES = 128
MESH = pl.DeviceIdType.MESH
VMEM = pltpu.MemorySpace.VMEM
SMEM = pltpu.MemorySpace.SMEM


def node_points():
    positive = [0.2092992179024789, 0.5917001814331423, 0.8717401485096066, 1.0]
    return np.array(sorted([-entry for entry in positive] + positive))


def derivative_matrix():
    points = node_points()
    count = len(points)
    weights = np.array(
        [
            1.0 / np.prod([points[row] - points[col] for col in range(count) if col != row])
            for row in range(count)
        ]
    )
    matrix = np.zeros((count, count))
    for row in range(count):
        for col in range(count):
            if row != col:
                matrix[row, col] = weights[col] / weights[row] / (points[row] - points[col])
        matrix[row, row] = -np.sum(matrix[row])
    return matrix


DERIV = derivative_matrix()
POINTS = node_points()
MODES = np.stack([(1.0 - POINTS) / 2.0, (1.0 + POINTS) / 2.0], axis=1)


def split_constant(matrix):
    high = matrix.astype(jnp.bfloat16)
    low = (matrix - high.astype(np.float64)).astype(jnp.bfloat16)
    return np.concatenate([high, low, high], axis=1)


def forward_table():
    eye = np.eye(NODES)
    return split_constant(np.kron(eye, DERIV))


def backward_table():
    eye = np.eye(NODES)
    return split_constant(np.kron(eye, DERIV.T))


def lift_table():
    eye = np.eye(NODES)
    rows = [eye[:, :1], -DERIV[:1].T, eye[:, -1:], DERIV[-1:].T]
    second = [np.kron(row, eye) for row in rows]
    third = [np.kron(eye, row) for row in rows]
    return split_constant(np.concatenate(second + third, axis=1))


def split_rows(values):
    high = values.astype(jnp.bfloat16)
    low = (values - high.astype(jnp.float32)).astype(jnp.bfloat16)
    return jnp.concatenate([high, high, low], axis=0)


def product(table, values):
    return lax.dot_general(
        table, split_rows(values), (((1,), (0,)), ((), ())), preferred_element_type=jnp.float32
    )


def even_odd(matrix, layers):
    half = NODES // 2
    sums = [layers[k] + layers[NODES - 1 - k] for k in range(half)]
    gaps = [layers[k] - layers[NODES - 1 - k] for k in range(half)]
    result = [None] * NODES
    for row in range(half):
        even = None
        odd = None
        for k in range(half):
            first = float((matrix[row, k] + matrix[row, NODES - 1 - k]) / 2)
            second = float((matrix[row, k] - matrix[row, NODES - 1 - k]) / 2)
            even = first * sums[k] if even is None else even + first * sums[k]
            odd = second * gaps[k] if odd is None else odd + second * gaps[k]
        result[row] = odd + even
        result[NODES - 1 - row] = odd - even
    return result


def weighted(coefficients, layers):
    total = None
    for factor, layer in zip(coefficients, layers):
        term = float(factor) * layer
        total = term if total is None else total + term
    return total


def turn_code(code, inverse):
    first = code & 1
    second = (code >> 1) & 1
    swap = (code >> 2) & 1
    if inverse:
        first, second = (
            jnp.where(swap != 0, second, first),
            jnp.where(swap != 0, first, second),
        )
    return first * 56 + second * 7 + swap * 128


def lane_pick(values, index):
    return jnp.take_along_axis(values, index, axis=1, mode="promise_in_bounds")


def lane_source(turn):
    lane = lax.broadcasted_iota(jnp.int32, turn.shape, 1)
    swapped = ((lane & 7) << 3) | ((lane >> 3) & 7) | (lane & FACE)
    return (jnp.where((turn & 128) != 0, swapped, lane) ^ turn) & (LANES - 1)


def spread_metric(both):
    low = lax.broadcasted_iota(jnp.int32, both.shape, 1) < FACE
    return jnp.where(low, pltpu.roll(both, FACE, 1), both)


def pair_flux(own, peer, turn):
    wm1, v1, g1 = own
    wm2, v2, g2 = peer
    source = lane_source(turn)
    low = lax.broadcasted_iota(jnp.int32, turn.shape, 1) < FACE
    penalty = NODES * (NODES + 1) / 2.0
    jump = v1 - lane_pick(v2, source)
    gap = g1 - lane_pick(g2, source)
    total = wm1 + lane_pick(wm2, source)
    turned = pltpu.roll(total, FACE, 1)
    weight = 0.5 * jnp.where(low, total, turned)
    tau = (penalty * 0.5) * jnp.where(low, turned, total)
    return weight * (tau * jump - 0.5 * gap), -0.5 * weight * jump


def row_numbers(slots, pairs, elems, staged, rows, sem):
    staged[0][...] = slots[1] * elems + slots[0]
    staged[1][...] = pairs[1:2] * elems + pairs[0:1]
    staged[2][...] = pairs[3:4] * elems + pairs[2:3]
    return [pltpu.make_async_copy(staged[n], rows[n], sem.at[n]) for n in range(3)]


def code_rows(slots, pairs, pad, cb):
    slot_total = slots.shape[2]
    pair_total = pairs.shape[1]
    raw = slots[4]
    code = jnp.where(slots[3] != 0, turn_code(raw, False), turn_code(raw, True)) + 256 * slots[2]
    pad[0:1, 0:slot_total] = code.astype(jnp.float32)
    pad[0:1, slot_total:] = jnp.zeros((1, pad.shape[1] - slot_total), jnp.float32)
    for t in range(pad.shape[1] // LANES):
        row = jnp.broadcast_to(pad[0:1, t * LANES : (t + 1) * LANES], (LANES, LANES))
        count = min(LANES, slot_total - t * LANES)
        cb[t * LANES : t * LANES + count, :] = row.T.astype(jnp.int32)[:count]
    local = pairs[4:5, :]
    for side, codes in enumerate((turn_code(local, False), turn_code(local, True))):
        for t in range(pair_total // LANES):
            row = codes[:, t * LANES : (t + 1) * LANES].astype(jnp.float32)
            start = slot_total + side * pair_total + t * LANES
            cb[start : start + LANES, :] = jnp.broadcast_to(row, (LANES, LANES)).T.astype(jnp.int32)


def aligned(start, size):
    return pl.ds(pl.multiple_of(start, size), size)


def node_layers(t, axis, start, p_s):
    layers = []
    for k in range(NODES):
        if axis == 0:
            layers.append(p_s[t, start + k * FACE : start + (k + 1) * FACE, :])
        elif axis == 1:
            rows = [
                p_s[t, start + i * FACE + k * NODES : start + i * FACE + (k + 1) * NODES, :]
                for i in range(NODES)
            ]
            layers.append(jnp.concatenate(rows, axis=0))
        else:
            layers.append(p_s[t, pl.ds(start + k, FACE, stride=NODES), :])
    return layers


def face_rows(face, t, elems):
    return aligned(face * elems + t * LANES, LANES)


def fixed_tile(t, elems, fw_s, fm_s, table):
    for face in range(6):
        both = jnp.concatenate([fw_s[t, face], fm_s[t, face]], axis=0)
        table[face_rows(face, t, elems), :] = both.T


def value_tile(t, elems, p_s, table):
    for axis in range(3):
        for side in range(2):
            ends = []
            for start in range(0, p_s.shape[1], BRICK):
                k = side * (NODES - 1)
                if axis == 0:
                    ends.append(p_s[t, start + k * FACE : start + (k + 1) * FACE, :])
                elif axis == 1:
                    ends += [
                        p_s[t, start + i * FACE + k * NODES : start + i * FACE + (k + 1) * NODES, :]
                        for i in range(NODES)
                    ]
                else:
                    ends.append(p_s[t, pl.ds(start + k, FACE, stride=NODES), :])
            table[face_rows(2 * axis + side, t, elems), :] = jnp.concatenate(ends, axis=0).T


def slope_tile(t, elems, p_s, fm_s, table):
    for axis in range(3):
        slopes = []
        for start in range(0, p_s.shape[1], BRICK):
            layers = node_layers(t, axis, start, p_s)
            slopes.append((weighted(-DERIV[0], layers), weighted(DERIV[-1], layers)))
        for side in range(2):
            face = 2 * axis + side
            slope = jnp.concatenate([entry[side] * fm_s[t, face] for entry in slopes], axis=0)
            table[face_rows(face, t, elems), :] = slope.T


def volume_half(h, p_s, g_s, rhs_s, fwd, bwd, out, z, s_ref):
    fields = p_s.shape[1] // BRICK
    tiles = (2 * h, 2 * h + 1)

    def wide(ref, rows):
        return jnp.concatenate([ref[tiles[0], rows, :], ref[tiles[1], rows, :]], axis=1)

    def first(n, carry):
        f = n // NODES
        r = n % NODES
        where = [aligned(f * BRICK + k * FACE + r * NODES, NODES) for k in range(NODES)]
        for q, value in enumerate(even_odd(DERIV, [wide(p_s, rows) for rows in where])):
            s_ref[where[q], :] = value
        return carry

    lax.fori_loop(0, fields * NODES, first, 0, unroll=4)

    def middle(i, carry):
        g = [wide(g_s, aligned(n * BRICK + i * FACE, FACE)) for n in range(6)]
        for f in range(fields):
            rows = aligned(f * BRICK + i * FACE, FACE)
            x = wide(p_s, rows)
            s3 = product(fwd[...], x)
            s2 = jnp.concatenate(
                even_odd(DERIV, [x[j * NODES : (j + 1) * NODES] for j in range(NODES)]), axis=0
            )
            s1 = s_ref[rows, :]
            q1 = g[0] * s1 + g[3] * s2 + g[4] * s3
            q2 = g[3] * s1 + g[1] * s2 + g[5] * s3
            q3 = g[4] * s1 + g[5] * s2 + g[2] * s3
            s_ref[rows, :] = q1
            r2 = jnp.concatenate(
                even_odd(DERIV.T, [q2[j * NODES : (j + 1) * NODES] for j in range(NODES)]), axis=0
            )
            r23 = product(bwd[...], q3) + r2
            out[tiles[0], rows, :] = r23[:, :LANES]
            out[tiles[1], rows, :] = r23[:, LANES:]
        return carry

    lax.fori_loop(0, NODES, middle, 0, unroll=8)

    def last(n, carry):
        f = n // NODES
        r = n % NODES
        where = [aligned(f * BRICK + k * FACE + r * NODES, NODES) for k in range(NODES)]
        left = []
        for q, value in enumerate(even_odd(DERIV.T, [s_ref[rows, :] for rows in where])):
            left.append(wide(rhs_s, where[q]) - (wide(out, where[q]) + value))
            out[tiles[0], where[q], :] = left[q][:, :LANES]
            out[tiles[1], where[q], :] = left[q][:, LANES:]
        for a in range(2):
            rows = aligned((2 * f + a) * FACE + r * NODES, NODES)
            level = weighted(MODES[:, a], left)
            z[tiles[0], rows, :] = level[:, :LANES]
            z[tiles[1], rows, :] = level[:, LANES:]
        return carry

    lax.fori_loop(0, fields * NODES, last, 0, unroll=4)


def front_kernel(
    n_blk, n_sub,
    slots_hbm, pairs_hbm, p_hbm, fw_hbm, fm_hbm, g_hbm, rhs_hbm, fwd_hbm, bwd_hbm,
    rest, z, vb, hb,
    slots, pairs, fwd, bwd, p_s, fw_s, fm_s, g_s, rhs_s, s_ref, tv, tg, tw, la, lb, lc, cb, pad, send, recv,
    st0, st1, st2, rw0, rw1, rw2,
    small_sem, load_sem, geo_sem, row_sem, send_sem, recv_sem,
):
    elems = tv.shape[0] // 6
    tiles = elems // LANES
    slot_total = slots.shape[2]
    pair_total = pairs.shape[1]
    width = slot_total // 9
    tables = (tw, tv, tg)
    locals_ = (la, lb, lc)
    place = lax.axis_index("blk")
    sub = lax.axis_index("sub")

    def peer(k):
        return (
            lax.rem(place + (k // 3 - 1) + n_blk, n_blk),
            lax.rem(sub + (k % 3 - 1) + n_sub, n_sub),
        )

    others = [2, 0, 8, 6, 5, 3, 1, 7]
    barrier = pltpu.get_barrier_semaphore()
    for k in others:
        pl.semaphore_signal(barrier, inc=1, device_id=peer(k), device_id_type=MESH)
    small = [
        pltpu.make_async_copy(source, target, small_sem.at[n])
        for n, (source, target) in enumerate(
            ((slots_hbm, slots), (pairs_hbm, pairs), (fwd_hbm, fwd), (bwd_hbm, bwd))
        )
    ]
    for copy in small[:2]:
        copy.start()
    loads = []
    geo = []
    for t in range(tiles):
        cols = pl.ds(t * LANES, LANES)
        geo.append(pltpu.make_async_copy(g_hbm.at[:, cols], g_s.at[t], geo_sem.at[t, 0]))
        geo.append(pltpu.make_async_copy(rhs_hbm.at[:, cols], rhs_s.at[t], geo_sem.at[t, 1]))
        loads.append(
            [
                pltpu.make_async_copy(fw_hbm.at[:, :, cols], fw_s.at[t], load_sem.at[t, 0]),
                pltpu.make_async_copy(fm_hbm.at[:, :, cols], fm_s.at[t], load_sem.at[t, 1]),
                pltpu.make_async_copy(p_hbm.at[:, cols], p_s.at[t], load_sem.at[t, 2]),
            ]
        )
    for t in range(tiles):
        loads[t][0].start()
        loads[t][1].start()
    for t in range(tiles):
        loads[t][2].start()
    for copy in small[:2]:
        copy.wait()
    numbers = row_numbers(slots, pairs, elems, (st0, st1, st2), (rw0, rw1, rw2), row_sem)
    for copy in numbers:
        copy.start()
    for t in range(tiles):
        loads[t][0].wait()
        loads[t][1].wait()
        fixed_tile(t, elems, fw_s, fm_s, tw)
    for t in range(tiles):
        loads[t][2].wait()
        if t == tiles - 1:
            for copy in geo + small[2:]:
                copy.start()
        value_tile(t, elems, p_s, tv)
        slope_tile(t, elems, p_s, fm_s, tg)
    for copy in numbers:
        copy.wait()
    for k in others:

        def gather(n, carry, k=k):
            base = n * 16
            rows = [rw0[0, k * width + base + u] for u in range(16)]
            for j in range(3):
                found = [tables[j][pl.ds(row, 1), :] for row in rows]
                for u in range(16):
                    send[k, j, pl.ds(base + u, 1), :] = found[u]
            return carry

        lax.fori_loop(0, width // 16, gather, 0)
    pl.semaphore_wait(barrier, len(others))
    copies = []
    for k in others:
        copies.append(
            pltpu.make_async_remote_copy(
                src_ref=send.at[k],
                dst_ref=recv.at[8 - k],
                send_sem=send_sem.at[k],
                recv_sem=recv_sem.at[8 - k],
                device_id=peer(k),
                device_id_type=MESH,
            )
        )
        copies[-1].start()
    code_rows(slots, pairs, pad, cb)

    for side, numbers in enumerate((rw1, rw2)):

        def gather_local(n, carry, side=side, numbers=numbers):
            base = n * 16
            rows = [numbers[0, base + u] for u in range(16)]
            for j in range(3):
                found = [tables[j][pl.ds(row, 1), :] for row in rows]
                for u in range(16):
                    locals_[j][pl.ds(side * pair_total + base + u, 1), :] = found[u]
            return carry

        lax.fori_loop(0, pair_total // 16, gather_local, 0)

    group = min(pair_total, 2 * LANES)

    def local_flux(n, carry):
        one = aligned(n * group, group)
        two = aligned(n * group + pair_total, group)
        rows = pl.ds(pl.multiple_of(n * group + slot_total, FACE), group)
        peers = pl.ds(pl.multiple_of(n * group + slot_total + pair_total, FACE), group)
        first = [table[one, :] for table in locals_]
        second = [table[two, :] for table in locals_]
        value, lift = pair_flux(first, second, cb[rows, :])
        vb[rows, :] = value
        hb[rows, :] = lift * spread_metric(first[0])
        back = lane_source(cb[peers, :])
        vb[peers, :] = -lane_pick(value, back)
        hb[peers, :] = -lane_pick(lift, back) * spread_metric(second[0])
        return carry

    lax.fori_loop(0, pair_total // group, local_flux, 0)
    for copy in geo + small[2:]:
        copy.wait()

    def volume(h, carry):
        volume_half(h, p_s, g_s, rhs_s, fwd, bwd, rest, z, s_ref)
        return carry

    lax.fori_loop(0, tiles // 2, volume, 0)
    for first in range(0, len(others), 2):
        for copy in copies[first : first + 2]:
            copy.wait()
        for k in others[first : first + 2]:
            k = 8 - k
            rows = slice(k * width, (k + 1) * width)
            turn = cb[rows, :]
            own = [send[k, j] for j in range(3)]
            value, lift = pair_flux(own, [recv[k, j] for j in range(3)], turn)
            live = turn >= 256
            vb[rows, :] = jnp.where(live, value, 0.0)
            hb[rows, :] = jnp.where(live, lift * spread_metric(own[0]), 0.0)

    vb[4 * width : 5 * width, :] = jnp.zeros((width, LANES), jnp.float32)
    hb[4 * width : 5 * width, :] = jnp.zeros((width, LANES), jnp.float32)


def scatter_kernel(slots, pairs, vb, hb, vt, lt, st0, st1, st2, rw0, rw1, rw2, row_sem):
    elems = vt.shape[0] // 6
    slot_total = slots.shape[2]
    pair_total = pairs.shape[1]
    numbers = row_numbers(slots, pairs, elems, (st0, st1, st2), (rw0, rw1, rw2), row_sem)
    for copy in numbers:
        copy.start()

    def clear(n, carry):
        rows = aligned(n * LANES, LANES)
        zero = jnp.zeros((LANES, LANES), jnp.float32)
        vt[rows, :] = zero
        lt[rows, :] = zero
        return carry

    lax.fori_loop(0, vt.shape[0] // LANES, clear, 0)
    for copy in numbers:
        copy.wait()
    for start, count, numbers in (
        (0, slot_total, rw0),
        (slot_total, pair_total, rw1),
        (slot_total + pair_total, pair_total, rw2),
    ):

        def scatter(n, carry, start=start, numbers=numbers):
            base = n * 16
            rows = [numbers[0, base + u] for u in range(16)]
            for source, table in ((vb, vt), (hb, lt)):
                found = [source[pl.ds(start + base + u, 1), :] for u in range(16)]
                for u in range(16):
                    table[pl.ds(rows[u], 1), :] = found[u]
            return carry

        lax.fori_loop(0, count // 16, scatter, 0)


def reduce_kernel(
    n_sub,
    vt, lt, rest, z, lift_ref, modes, cells,
    total_ref, res,
    fv, fl, cs, sums_ref, box, send_sem, recv_sem,
):
    elems = vt.shape[0] // 6
    tiles = elems // LANES
    fields = fv.shape[1]
    place = lax.axis_index("blk")
    sub = lax.axis_index("sub")
    barrier = pltpu.get_barrier_semaphore()
    peers = [(place, lax.rem(sub + step, n_sub)) for step in range(1, n_sub)]
    for peer in peers:
        pl.semaphore_signal(barrier, inc=1, device_id=peer, device_id_type=MESH)

    for face in range(6):
        for t in range(tiles):
            rows = slice(face * elems + t * LANES, face * elems + (t + 1) * LANES)
            value = vt[rows, :].T
            lift = lt[rows, :].T
            for f in range(fields):
                fv[t, f, face] = value[f * FACE : (f + 1) * FACE]
                fl[t, f, face] = lift[f * FACE : (f + 1) * FACE]

    half = 2 * LANES
    slopes = (-DERIV[0] @ MODES, DERIV[-1] @ MODES)

    def halves(n):
        f = n // (tiles // 2)
        h = n % (tiles // 2)

        def wide(ref, *where):
            return jnp.concatenate([ref[2 * h, *where], ref[2 * h + 1, *where]], axis=-1)

        return f, h, wide

    def groups(layer):
        return [layer[k * NODES : (k + 1) * NODES] for k in range(NODES)]

    def restrict(n, carry):
        f, h, wide = halves(n)
        cols = aligned(h * half, half)
        faces = []
        for axis in range(3):
            v0, l0 = wide(fv, f, 2 * axis), wide(fl, f, 2 * axis)
            v1, l1 = wide(fv, f, 2 * axis + 1), wide(fl, f, 2 * axis + 1)
            modes_here = []
            for m in range(2):
                level = float(slopes[0][m]) * l0 + float(slopes[1][m]) * l1
                modes_here.append(level + (v0 if m == 0 else v1))
            faces.append(modes_here)
        for a in range(2):
            first = groups(wide(z, aligned((2 * f + a) * FACE, FACE)) - faces[0][a])
            third = [weighted(MODES[:, a], groups(faces[2][c])) for c in range(2)]
            for b in range(2):
                level = weighted(MODES[:, b], first) - weighted(MODES[:, a], groups(faces[1][b]))
                for c in range(2):
                    column = modes[c * NODES : (c + 1) * NODES, 0:1]
                    other = modes[b * NODES : (b + 1) * NODES, 0:1]
                    row = f * NODES + 4 * a + 2 * b + c
                    value = level * column - third[c] * other
                    cs[pl.ds(row, 1), cols] = jnp.sum(value, axis=0, keepdims=True)
        return carry

    lax.fori_loop(0, fields * tiles // 2, restrict, 0)

    row_cells = sums_ref.shape[1]
    coarse = cs[...]
    hot = lax.broadcasted_iota(jnp.int32, (row_cells, elems), 0) == cells[...]
    hot = hot.astype(jnp.float32).astype(jnp.bfloat16)
    high = coarse.astype(jnp.bfloat16)
    low = (coarse - high.astype(jnp.float32)).astype(jnp.bfloat16)
    both = lax.dot_general(
        jnp.concatenate([high, low], axis=0),
        hot,
        (((1,), (1,)), ((), ())),
        preferred_element_type=jnp.float32,
    )
    sums_ref[...] = both[: coarse.shape[0]] + both[coarse.shape[0] :]
    pl.semaphore_wait(barrier, n_sub - 1)
    copies = []
    for step, peer in enumerate(peers):
        copies.append(
            pltpu.make_async_remote_copy(
                src_ref=sums_ref,
                dst_ref=box.at[step],
                send_sem=send_sem.at[step],
                recv_sem=recv_sem.at[step],
                device_id=peer,
                device_id_type=MESH,
            )
        )
        copies[-1].start()

    def finish(n, carry):
        f, h, wide = halves(n)
        low_lift = wide(fl, f, 0)
        high_lift = wide(fl, f, 1)
        for i in range(NODES):
            part = slice(i * NODES, (i + 1) * NODES)
            stack = []
            for face in range(2, 6):
                stack += [wide(fv, f, face, part), wide(fl, f, face, part)]
            rows = aligned(f * BRICK + i * FACE, FACE)
            value = wide(rest, rows) - product(lift_ref[...], jnp.concatenate(stack, axis=0))
            value = value + float(DERIV[0, i]) * low_lift - float(DERIV[-1, i]) * high_lift
            if i == 0:
                value = value - wide(fv, f, 0)
            if i == NODES - 1:
                value = value - wide(fv, f, 1)
            res[2 * h, rows, :] = value[:, :LANES]
            res[2 * h + 1, rows, :] = value[:, LANES:]
        return carry

    lax.fori_loop(0, fields * tiles // 2, finish, 0)
    for copy in copies:
        copy.wait()
    total = sums_ref[...]
    for step in range(n_sub - 1):
        total = total + box[step]
    total_ref[...] = total


def correct_kernel(
    total_ref, inverse_ref, cells_ref, modes_ref, p_ref, tiled, out_ref, res_hbm, res_sem
):
    copies = [
        pltpu.make_async_copy(tiled.at[t], res_hbm.at[:, pl.ds(t * LANES, LANES)], res_sem.at[t])
        for t in range(tiled.shape[0])
    ]

    @pl.when(pl.program_id(0) == 0)
    def _():
        for copy in copies:
            copy.start()

    fields = p_ref.shape[0]
    elems = p_ref.shape[-1]
    row_cells = total_ref.shape[1]
    rows = []
    for f in range(fields):
        level = None
        for j in range(NODES):
            term = inverse_ref[j] * total_ref[f * NODES + j : f * NODES + j + 1, :]
            level = term if level is None else level + term
        rows.append(level)
    level = jnp.concatenate(rows, axis=0)
    high = level.astype(jnp.bfloat16)
    low = (level - high.astype(jnp.float32)).astype(jnp.bfloat16)
    hot = lax.broadcasted_iota(jnp.int32, (row_cells, elems), 0) == cells_ref[...]
    hot = hot.astype(jnp.float32).astype(jnp.bfloat16)
    spread = lax.dot_general(
        jnp.concatenate([high, low], axis=0),
        hot,
        (((1,), (0,)), ((), ())),
        preferred_element_type=jnp.float32,
    )
    spread = spread[: level.shape[0]] + spread[level.shape[0] :]
    columns = [modes_ref[c * NODES : (c + 1) * NODES, 0:1] for c in range(2)]
    for f in range(fields):
        planes = []
        for a in range(2):
            lines = []
            for b in range(2):
                start = f * NODES + 4 * a + 2 * b
                lines.append(
                    columns[0] * spread[start : start + 1] + columns[1] * spread[start + 1 : start + 2]
                )
            planes.append([weighted(MODES[j], lines) for j in range(NODES)])
        for j in range(NODES):
            part = slice(j * NODES, (j + 1) * NODES)
            for i in range(NODES):
                grown = weighted(MODES[i], [planes[0][j], planes[1][j]])
                out_ref[f, i, part, :] = p_ref[f, i, part, :] + grown

    @pl.when(pl.program_id(0) == pl.num_programs(0) - 1)
    def _():
        for copy in copies:
            copy.wait()


def whole(shape, space=VMEM):
    return pl.BlockSpec(shape, lambda *_: (0,) * len(shape), memory_space=space)


def limits(mib, **extra):
    return pltpu.CompilerParams(vmem_limit_bytes=mib << 20, **extra)


def shaped(*shape):
    return jax.ShapeDtypeStruct(shape, jnp.float32)


def on_device(
    n_blk,
    n_sub,
    pressure,
    right_side,
    geometry,
    face_weight,
    face_metric,
    cross_slots,
    local_pairs,
    coarse_map,
    coarse_inverse,
):
    fields = pressure.shape[0]
    elems = pressure.shape[-1]
    slot_total = cross_slots.shape[2]
    pair_total = local_pairs.shape[1]
    row_cells = coarse_inverse.shape[-1]
    tiles = elems // LANES
    width = slot_total // 9
    slabs = (fields, NODES, FACE, elems)
    rows = fields * BRICK
    p = pressure.reshape(slabs)
    weights = jnp.transpose(face_weight, (1, 0, 2))
    metrics = jnp.transpose(face_metric, (1, 0, 2))
    cells = coarse_map.reshape(1, elems)
    modes = jnp.asarray(np.repeat(MODES.T.reshape(2 * NODES, 1), LANES, axis=1), jnp.float32)
    pad_width = -(-slot_total // LANES) * LANES
    side_total = slot_total + 2 * pair_total
    f32 = jnp.float32
    i32 = jnp.int32
    inside = pl.BlockSpec(memory_space=VMEM)
    outside = pl.BlockSpec(memory_space=pltpu.MemorySpace.HBM)
    number_scratch = [
        pltpu.VMEM((1, slot_total), i32),
        pltpu.VMEM((1, pair_total), i32),
        pltpu.VMEM((1, pair_total), i32),
        pltpu.SMEM((1, slot_total), i32),
        pltpu.SMEM((1, pair_total), i32),
        pltpu.SMEM((1, pair_total), i32),
    ]
    dma = pltpu.SemaphoreType.DMA

    rest, levels, values, lifts = pl.pallas_call(
        functools.partial(front_kernel, n_blk, n_sub),
        in_specs=[outside] * 9,
        out_specs=[inside] * 4,
        out_shape=[
            shaped(tiles, rows, LANES),
            shaped(tiles, 2 * fields * FACE, LANES),
            shaped(side_total, LANES),
            shaped(side_total, LANES),
        ],
        scratch_shapes=[
            pltpu.VMEM(cross_slots.shape, i32),
            pltpu.VMEM(local_pairs.shape, i32),
            pltpu.VMEM((FACE, 3 * FACE), jnp.bfloat16),
            pltpu.VMEM((FACE, 3 * FACE), jnp.bfloat16),
            pltpu.VMEM((tiles, rows, LANES), f32),
            pltpu.VMEM((tiles, 6, FACE, LANES), f32),
            pltpu.VMEM((tiles, 6, FACE, LANES), f32),
            pltpu.VMEM((tiles, 6 * BRICK, LANES), f32),
            pltpu.VMEM((tiles, rows, LANES), f32),
            pltpu.VMEM((rows, 2 * LANES), f32),
        ]
        + [pltpu.VMEM((6 * elems, LANES), f32)] * 3
        + [pltpu.VMEM((2 * pair_total, LANES), f32)] * 3
        + [
            pltpu.VMEM((side_total, LANES), i32),
            pltpu.VMEM((8, pad_width), f32),
            pltpu.VMEM((9, 3, width, LANES), f32),
            pltpu.VMEM((9, 3, width, LANES), f32),
        ]
        + number_scratch
        + [dma((4,)), dma((tiles, 3)), dma((tiles, 2)), dma((3,)), dma((9,)), dma((9,))],
        compiler_params=limits(36, collective_id=0, has_side_effects=True),
        name="front",
    )(
        *[
            pltpu.with_memory_space_constraint(value, pltpu.MemorySpace.HBM)
            for value in (
                cross_slots,
                local_pairs,
                pressure.reshape(rows, elems),
                weights,
                metrics,
                geometry.reshape(6 * BRICK, elems),
                right_side.reshape(rows, elems),
                jnp.asarray(forward_table()),
                jnp.asarray(backward_table()),
            )
        ]
    )

    value_table, lift_rows = pl.pallas_call(
        scatter_kernel,
        in_specs=[inside] * 4,
        out_specs=[inside] * 2,
        out_shape=[shaped(6 * elems, LANES), shaped(6 * elems, LANES)],
        scratch_shapes=number_scratch + [dma((3,))],
        compiler_params=limits(8),
        name="scatter",
    )(cross_slots, local_pairs, values, lifts)

    totals, tiled = pl.pallas_call(
        functools.partial(reduce_kernel, n_sub),
        in_specs=[inside] * 7,
        out_specs=[inside] * 2,
        out_shape=[shaped(fields * NODES, row_cells), shaped(tiles, rows, LANES)],
        scratch_shapes=[
            pltpu.VMEM((tiles, fields, 6, FACE, LANES), f32),
            pltpu.VMEM((tiles, fields, 6, FACE, LANES), f32),
            pltpu.VMEM((fields * NODES, elems), f32),
            pltpu.VMEM((fields * NODES, row_cells), f32),
            pltpu.VMEM((n_sub - 1, fields * NODES, row_cells), f32),
            dma((n_sub - 1,)),
            dma((n_sub - 1,)),
        ],
        compiler_params=limits(24, collective_id=1, has_side_effects=True),
        name="reduce",
    )(value_table, lift_rows, rest, levels, jnp.asarray(lift_table()), modes, cells)

    chunk = min(elems, 256)
    corrected, residual = pl.pallas_call(
        correct_kernel,
        grid=(elems // chunk,),
        in_specs=[
            whole((fields * NODES, row_cells)),
            whole((NODES, NODES, row_cells)),
            pl.BlockSpec((1, chunk), lambda t: (0, t)),
            whole((2 * NODES, LANES)),
            pl.BlockSpec((fields, NODES, FACE, chunk), lambda t: (0, 0, 0, t)),
            pl.BlockSpec(memory_space=pl.ANY),
        ],
        out_specs=[
            pl.BlockSpec((fields, NODES, FACE, chunk), lambda t: (0, 0, 0, t)),
            pl.BlockSpec(memory_space=pl.ANY),
        ],
        out_shape=[shaped(*slabs), shaped(rows, elems)],
        scratch_shapes=[dma((tiles,))],
        compiler_params=limits(16),
        name="correct",
    )(totals, coarse_inverse, cells, modes, p, tiled)
    return residual.reshape(pressure.shape), corrected.reshape(pressure.shape)


def solution(mesh):
    return jax.shard_map(
        functools.partial(on_device, mesh.shape["blk"], mesh.shape["sub"]),
        mesh=mesh,
        in_specs=(
            P(None, None, None, None, ("blk", "sub")),
            P(None, None, None, None, ("blk", "sub")),
            P(None, None, None, None, ("blk", "sub")),
            P(None, None, ("blk", "sub")),
            P(None, None, ("blk", "sub")),
            P(None, ("blk", "sub"), None),
            P(None, ("blk", "sub")),
            P(("blk", "sub")),
            P(None, None, "blk"),
        ),
        out_specs=(
            P(None, None, None, None, ("blk", "sub")),
            P(None, None, None, None, ("blk", "sub")),
        ),
        check_vma=False,
    )
```

```python
import functools

import jax
import jax.numpy as jnp
import numpy as np
from jax import lax
from jax.experimental import pallas as pl
from jax.experimental.pallas import tpu as pltpu
from jax.sharding import PartitionSpec as P

NODES = 8
FACE = NODES * NODES
BRICK = NODES * FACE
LANES = 128
MESH = pl.DeviceIdType.MESH
VMEM = pltpu.MemorySpace.VMEM
SMEM = pltpu.MemorySpace.SMEM


def node_points():
    positive = [0.2092992179024789, 0.5917001814331423, 0.8717401485096066, 1.0]
    return np.array(sorted([-entry for entry in positive] + positive))


def derivative_matrix():
    points = node_points()
    count = len(points)
    weights = np.array(
        [
            1.0 / np.prod([points[row] - points[col] for col in range(count) if col != row])
            for row in range(count)
        ]
    )
    matrix = np.zeros((count, count))
    for row in range(count):
        for col in range(count):
            if row != col:
                matrix[row, col] = weights[col] / weights[row] / (points[row] - points[col])
        matrix[row, row] = -np.sum(matrix[row])
    return matrix


DERIV = derivative_matrix()
POINTS = node_points()
MODES = np.stack([(1.0 - POINTS) / 2.0, (1.0 + POINTS) / 2.0], axis=1)


def split_constant(matrix):
    high = matrix.astype(jnp.bfloat16)
    low = (matrix - high.astype(np.float64)).astype(jnp.bfloat16)
    return np.concatenate([high, low, high], axis=1)


def forward_table():
    eye = np.eye(NODES)
    return split_constant(np.kron(eye, DERIV))


def backward_table():
    eye = np.eye(NODES)
    return split_constant(np.kron(eye, DERIV.T))


def lift_table():
    eye = np.eye(NODES)
    rows = [eye[:, :1], -DERIV[:1].T, eye[:, -1:], DERIV[-1:].T]
    second = [np.kron(row, eye) for row in rows]
    third = [np.kron(eye, row) for row in rows]
    return split_constant(np.concatenate(second + third, axis=1))


def split_rows(values):
    high = values.astype(jnp.bfloat16)
    low = (values - high.astype(jnp.float32)).astype(jnp.bfloat16)
    return jnp.concatenate([high, high, low], axis=0)


def product(table, values):
    return lax.dot_general(
        table, split_rows(values), (((1,), (0,)), ((), ())), preferred_element_type=jnp.float32
    )


def even_odd(matrix, layers):
    half = NODES // 2
    sums = [layers[k] + layers[NODES - 1 - k] for k in range(half)]
    gaps = [layers[k] - layers[NODES - 1 - k] for k in range(half)]
    result = [None] * NODES
    for row in range(half):
        even = None
        odd = None
        for k in range(half):
            first = float((matrix[row, k] + matrix[row, NODES - 1 - k]) / 2)
            second = float((matrix[row, k] - matrix[row, NODES - 1 - k]) / 2)
            even = first * sums[k] if even is None else even + first * sums[k]
            odd = second * gaps[k] if odd is None else odd + second * gaps[k]
        result[row] = odd + even
        result[NODES - 1 - row] = odd - even
    return result


def weighted(coefficients, layers):
    total = None
    for factor, layer in zip(coefficients, layers):
        term = float(factor) * layer
        total = term if total is None else total + term
    return total


def turn_code(code, inverse):
    first = code & 1
    second = (code >> 1) & 1
    swap = (code >> 2) & 1
    if inverse:
        first, second = (
            jnp.where(swap != 0, second, first),
            jnp.where(swap != 0, first, second),
        )
    return first * 56 + second * 7 + swap * 128


def lane_pick(values, index):
    return jnp.take_along_axis(values, index, axis=1, mode="promise_in_bounds")


def lane_source(turn):
    lane = lax.broadcasted_iota(jnp.int32, turn.shape, 1)
    swapped = ((lane & 7) << 3) | ((lane >> 3) & 7) | (lane & FACE)
    return (jnp.where((turn & 128) != 0, swapped, lane) ^ turn) & (LANES - 1)


def spread_metric(both):
    low = lax.broadcasted_iota(jnp.int32, both.shape, 1) < FACE
    return jnp.where(low, pltpu.roll(both, FACE, 1), both)


def pair_flux(own, peer, turn):
    wm1, v1, g1 = own
    wm2, v2, g2 = peer
    source = lane_source(turn)
    low = lax.broadcasted_iota(jnp.int32, turn.shape, 1) < FACE
    penalty = NODES * (NODES + 1) / 2.0
    jump = v1 - lane_pick(v2, source)
    gap = g1 - lane_pick(g2, source)
    total = wm1 + lane_pick(wm2, source)
    turned = pltpu.roll(total, FACE, 1)
    weight = 0.5 * jnp.where(low, total, turned)
    tau = (penalty * 0.5) * jnp.where(low, turned, total)
    return weight * (tau * jump - 0.5 * gap), -0.5 * weight * jump


def row_numbers(slots, pairs, elems, staged, rows, sem):
    staged[0][...] = slots[1] * elems + slots[0]
    staged[1][...] = pairs[1:2] * elems + pairs[0:1]
    staged[2][...] = pairs[3:4] * elems + pairs[2:3]
    return [pltpu.make_async_copy(staged[n], rows[n], sem.at[n]) for n in range(3)]


def code_rows(slots, pairs, pad, cb):
    slot_total = slots.shape[2]
    pair_total = pairs.shape[1]
    raw = slots[4]
    code = jnp.where(slots[3] != 0, turn_code(raw, False), turn_code(raw, True)) + 256 * slots[2]
    pad[0:1, 0:slot_total] = code.astype(jnp.float32)
    pad[0:1, slot_total:] = jnp.zeros((1, pad.shape[1] - slot_total), jnp.float32)
    for t in range(pad.shape[1] // LANES):
        row = jnp.broadcast_to(pad[0:1, t * LANES : (t + 1) * LANES], (LANES, LANES))
        count = min(LANES, slot_total - t * LANES)
        cb[t * LANES : t * LANES + count, :] = row.T.astype(jnp.int32)[:count]
    local = pairs[4:5, :]
    for side, codes in enumerate((turn_code(local, False), turn_code(local, True))):
        for t in range(pair_total // LANES):
            row = codes[:, t * LANES : (t + 1) * LANES].astype(jnp.float32)
            start = slot_total + side * pair_total + t * LANES
            cb[start : start + LANES, :] = jnp.broadcast_to(row, (LANES, LANES)).T.astype(jnp.int32)


def aligned(start, size):
    return pl.ds(pl.multiple_of(start, size), size)


def node_layers(t, axis, start, p_s):
    layers = []
    for k in range(NODES):
        if axis == 0:
            layers.append(p_s[t, start + k * FACE : start + (k + 1) * FACE, :])
        elif axis == 1:
            rows = [
                p_s[t, start + i * FACE + k * NODES : start + i * FACE + (k + 1) * NODES, :]
                for i in range(NODES)
            ]
            layers.append(jnp.concatenate(rows, axis=0))
        else:
            layers.append(p_s[t, pl.ds(start + k, FACE, stride=NODES), :])
    return layers


def face_rows(face, t, elems):
    return aligned(face * elems + t * LANES, LANES)


def fixed_tile(t, elems, fw_s, fm_s, table):
    for face in range(6):
        both = jnp.concatenate([fw_s[t, face], fm_s[t, face]], axis=0)
        table[face_rows(face, t, elems), :] = both.T


def value_tile(t, elems, p_s, table):
    for axis in range(3):
        for side in range(2):
            ends = []
            for start in range(0, p_s.shape[1], BRICK):
                k = side * (NODES - 1)
                if axis == 0:
                    ends.append(p_s[t, start + k * FACE : start + (k + 1) * FACE, :])
                elif axis == 1:
                    ends += [
                        p_s[t, start + i * FACE + k * NODES : start + i * FACE + (k + 1) * NODES, :]
                        for i in range(NODES)
                    ]
                else:
                    ends.append(p_s[t, pl.ds(start + k, FACE, stride=NODES), :])
            table[face_rows(2 * axis + side, t, elems), :] = jnp.concatenate(ends, axis=0).T


def slope_tile(t, elems, p_s, fm_s, table):
    for axis in range(3):
        slopes = []
        for start in range(0, p_s.shape[1], BRICK):
            layers = node_layers(t, axis, start, p_s)
            slopes.append((weighted(-DERIV[0], layers), weighted(DERIV[-1], layers)))
        for side in range(2):
            face = 2 * axis + side
            slope = jnp.concatenate([entry[side] * fm_s[t, face] for entry in slopes], axis=0)
            table[face_rows(face, t, elems), :] = slope.T


def volume_half(h, p_s, g_s, rhs_s, fwd, bwd, out, z, s_ref):
    fields = p_s.shape[1] // BRICK
    tiles = (2 * h, 2 * h + 1)

    def wide(ref, rows):
        return jnp.concatenate([ref[tiles[0], rows, :], ref[tiles[1], rows, :]], axis=1)

    def first(n, carry):
        f = n // NODES
        r = n % NODES
        where = [aligned(f * BRICK + k * FACE + r * NODES, NODES) for k in range(NODES)]
        for q, value in enumerate(even_odd(DERIV, [wide(p_s, rows) for rows in where])):
            s_ref[where[q], :] = value
        return carry

    lax.fori_loop(0, fields * NODES, first, 0, unroll=4)

    def middle(i, carry):
        g = [wide(g_s, aligned(n * BRICK + i * FACE, FACE)) for n in range(6)]
        for f in range(fields):
            rows = aligned(f * BRICK + i * FACE, FACE)
            x = wide(p_s, rows)
            s3 = product(fwd[...], x)
            s2 = jnp.concatenate(
                even_odd(DERIV, [x[j * NODES : (j + 1) * NODES] for j in range(NODES)]), axis=0
            )
            s1 = s_ref[rows, :]
            q1 = g[0] * s1 + g[3] * s2 + g[4] * s3
            q2 = g[3] * s1 + g[1] * s2 + g[5] * s3
            q3 = g[4] * s1 + g[5] * s2 + g[2] * s3
            s_ref[rows, :] = q1
            r2 = jnp.concatenate(
                even_odd(DERIV.T, [q2[j * NODES : (j + 1) * NODES] for j in range(NODES)]), axis=0
            )
            r23 = product(bwd[...], q3) + r2
            out[tiles[0], rows, :] = r23[:, :LANES]
            out[tiles[1], rows, :] = r23[:, LANES:]
        return carry

    lax.fori_loop(0, NODES, middle, 0, unroll=8)

    def last(n, carry):
        f = n // NODES
        r = n % NODES
        where = [aligned(f * BRICK + k * FACE + r * NODES, NODES) for k in range(NODES)]
        left = []
        for q, value in enumerate(even_odd(DERIV.T, [s_ref[rows, :] for rows in where])):
            left.append(wide(rhs_s, where[q]) - (wide(out, where[q]) + value))
            out[tiles[0], where[q], :] = left[q][:, :LANES]
            out[tiles[1], where[q], :] = left[q][:, LANES:]
        for a in range(2):
            rows = aligned((2 * f + a) * FACE + r * NODES, NODES)
            level = weighted(MODES[:, a], left)
            z[tiles[0], rows, :] = level[:, :LANES]
            z[tiles[1], rows, :] = level[:, LANES:]
        return carry

    lax.fori_loop(0, fields * NODES, last, 0, unroll=4)


def front_kernel(
    n_blk, n_sub,
    slots_hbm, pairs_hbm, p_hbm, fw_hbm, fm_hbm, g_hbm, rhs_hbm, fwd_hbm, bwd_hbm,
    rest, z, vb, hb,
    slots, pairs, fwd, bwd, p_s, fw_s, fm_s, g_s, rhs_s, s_ref, tv, tg, tw, la, lb, lc, cb, pad, send, recv,
    st0, st1, st2, rw0, rw1, rw2,
    small_sem, load_sem, geo_sem, row_sem, send_sem, recv_sem,
):
    elems = tv.shape[0] // 6
    tiles = elems // LANES
    slot_total = slots.shape[2]
    pair_total = pairs.shape[1]
    width = slot_total // 9
    tables = (tw, tv, tg)
    locals_ = (la, lb, lc)
    place = lax.axis_index("blk")
    sub = lax.axis_index("sub")

    def peer(k):
        return (
            lax.rem(place + (k // 3 - 1) + n_blk, n_blk),
            lax.rem(sub + (k % 3 - 1) + n_sub, n_sub),
        )

    others = [2, 0, 8, 6, 5, 3, 1, 7]
    barrier = pltpu.get_barrier_semaphore()
    for k in others:
        pl.semaphore_signal(barrier, inc=1, device_id=peer(k), device_id_type=MESH)
    small = [
        pltpu.make_async_copy(source, target, small_sem.at[n])
        for n, (source, target) in enumerate(
            ((slots_hbm, slots), (pairs_hbm, pairs), (fwd_hbm, fwd), (bwd_hbm, bwd))
        )
    ]
    for copy in small[:2]:
        copy.start()
    loads = []
    geo = []
    for t in range(tiles):
        cols = pl.ds(t * LANES, LANES)
        geo.append(pltpu.make_async_copy(g_hbm.at[:, cols], g_s.at[t], geo_sem.at[t, 0]))
        geo.append(pltpu.make_async_copy(rhs_hbm.at[:, cols], rhs_s.at[t], geo_sem.at[t, 1]))
        loads.append(
            [
                pltpu.make_async_copy(fw_hbm.at[:, :, cols], fw_s.at[t], load_sem.at[t, 0]),
                pltpu.make_async_copy(fm_hbm.at[:, :, cols], fm_s.at[t], load_sem.at[t, 1]),
                pltpu.make_async_copy(p_hbm.at[:, cols], p_s.at[t], load_sem.at[t, 2]),
            ]
        )
    for t in range(tiles):
        loads[t][0].start()
        loads[t][1].start()
    for t in range(tiles):
        loads[t][2].start()
    for copy in small[:2]:
        copy.wait()
    numbers = row_numbers(slots, pairs, elems, (st0, st1, st2), (rw0, rw1, rw2), row_sem)
    for copy in numbers:
        copy.start()
    for t in range(tiles):
        loads[t][0].wait()
        loads[t][1].wait()
        fixed_tile(t, elems, fw_s, fm_s, tw)
    for t in range(tiles):
        loads[t][2].wait()
        if t == tiles - 1:
            for copy in geo + small[2:]:
                copy.start()
        value_tile(t, elems, p_s, tv)
        slope_tile(t, elems, p_s, fm_s, tg)
    for copy in numbers:
        copy.wait()
    for k in others:

        def gather(n, carry, k=k):
            base = n * 16
            rows = [rw0[0, k * width + base + u] for u in range(16)]
            for j in range(3):
                found = [tables[j][pl.ds(row, 1), :] for row in rows]
                for u in range(16):
                    send[k, j, pl.ds(base + u, 1), :] = found[u]
            return carry

        lax.fori_loop(0, width // 16, gather, 0)
    pl.semaphore_wait(barrier, len(others))
    copies = []
    for k in others:
        copies.append(
            pltpu.make_async_remote_copy(
                src_ref=send.at[k],
                dst_ref=recv.at[8 - k],
                send_sem=send_sem.at[k],
                recv_sem=recv_sem.at[8 - k],
                device_id=peer(k),
                device_id_type=MESH,
            )
        )
        copies[-1].start()
    code_rows(slots, pairs, pad, cb)

    for side, numbers in enumerate((rw1, rw2)):

        def gather_local(n, carry, side=side, numbers=numbers):
            base = n * 16
            rows = [numbers[0, base + u] for u in range(16)]
            for j in range(3):
                found = [tables[j][pl.ds(row, 1), :] for row in rows]
                for u in range(16):
                    locals_[j][pl.ds(side * pair_total + base + u, 1), :] = found[u]
            return carry

        lax.fori_loop(0, pair_total // 16, gather_local, 0)

    group = min(pair_total, 2 * LANES)

    def local_flux(n, carry):
        one = aligned(n * group, group)
        two = aligned(n * group + pair_total, group)
        rows = pl.ds(pl.multiple_of(n * group + slot_total, FACE), group)
        peers = pl.ds(pl.multiple_of(n * group + slot_total + pair_total, FACE), group)
        first = [table[one, :] for table in locals_]
        second = [table[two, :] for table in locals_]
        value, lift = pair_flux(first, second, cb[rows, :])
        vb[rows, :] = value
        hb[rows, :] = lift * spread_metric(first[0])
        back = lane_source(cb[peers, :])
        vb[peers, :] = -lane_pick(value, back)
        hb[peers, :] = -lane_pick(lift, back) * spread_metric(second[0])
        return carry

    lax.fori_loop(0, pair_total // group, local_flux, 0)
    for copy in geo + small[2:]:
        copy.wait()

    def volume(h, carry):
        volume_half(h, p_s, g_s, rhs_s, fwd, bwd, rest, z, s_ref)
        return carry

    lax.fori_loop(0, tiles // 2, volume, 0)
    for first in range(0, len(others), 2):
        for copy in copies[first : first + 2]:
            copy.wait()
        for k in others[first : first + 2]:
            k = 8 - k
            rows = slice(k * width, (k + 1) * width)
            turn = cb[rows, :]
            own = [send[k, j] for j in range(3)]
            value, lift = pair_flux(own, [recv[k, j] for j in range(3)], turn)
            live = turn >= 256
            vb[rows, :] = jnp.where(live, value, 0.0)
            hb[rows, :] = jnp.where(live, lift * spread_metric(own[0]), 0.0)

    vb[4 * width : 5 * width, :] = jnp.zeros((width, LANES), jnp.float32)
    hb[4 * width : 5 * width, :] = jnp.zeros((width, LANES), jnp.float32)


def scatter_kernel(slots, pairs, vb, hb, vt, lt, st0, st1, st2, rw0, rw1, rw2, row_sem):
    elems = vt.shape[0] // 6
    slot_total = slots.shape[2]
    pair_total = pairs.shape[1]
    numbers = row_numbers(slots, pairs, elems, (st0, st1, st2), (rw0, rw1, rw2), row_sem)
    for copy in numbers:
        copy.start()

    def clear(n, carry):
        rows = aligned(n * LANES, LANES)
        zero = jnp.zeros((LANES, LANES), jnp.float32)
        vt[rows, :] = zero
        lt[rows, :] = zero
        return carry

    lax.fori_loop(0, vt.shape[0] // LANES, clear, 0)
    for copy in numbers:
        copy.wait()
    for start, count, numbers in (
        (0, slot_total, rw0),
        (slot_total, pair_total, rw1),
        (slot_total + pair_total, pair_total, rw2),
    ):

        def scatter(n, carry, start=start, numbers=numbers):
            base = n * 16
            rows = [numbers[0, base + u] for u in range(16)]
            for source, table in ((vb, vt), (hb, lt)):
                found = [source[pl.ds(start + base + u, 1), :] for u in range(16)]
                for u in range(16):
                    table[pl.ds(rows[u], 1), :] = found[u]
            return carry

        lax.fori_loop(0, count // 16, scatter, 0)


def reduce_kernel(
    n_sub,
    vt, lt, rest, z, lift_ref, modes, cells,
    total_ref, res,
    fv, fl, cs, sums_ref, box, send_sem, recv_sem,
):
    elems = vt.shape[0] // 6
    tiles = elems // LANES
    fields = fv.shape[1]
    place = lax.axis_index("blk")
    sub = lax.axis_index("sub")
    barrier = pltpu.get_barrier_semaphore()
    peers = [(place, lax.rem(sub + step, n_sub)) for step in range(1, n_sub)]
    for peer in peers:
        pl.semaphore_signal(barrier, inc=1, device_id=peer, device_id_type=MESH)

    for face in range(6):
        for t in range(tiles):
            rows = slice(face * elems + t * LANES, face * elems + (t + 1) * LANES)
            value = vt[rows, :].T
            lift = lt[rows, :].T
            for f in range(fields):
                fv[t, f, face] = value[f * FACE : (f + 1) * FACE]
                fl[t, f, face] = lift[f * FACE : (f + 1) * FACE]

    half = 2 * LANES
    slopes = (-DERIV[0] @ MODES, DERIV[-1] @ MODES)

    def halves(n):
        f = n // (tiles // 2)
        h = n % (tiles // 2)

        def wide(ref, *where):
            return jnp.concatenate([ref[2 * h, *where], ref[2 * h + 1, *where]], axis=-1)

        return f, h, wide

    def groups(layer):
        return [layer[k * NODES : (k + 1) * NODES] for k in range(NODES)]

    def restrict(n, carry):
        f, h, wide = halves(n)
        cols = aligned(h * half, half)
        faces = []
        for axis in range(3):
            v0, l0 = wide(fv, f, 2 * axis), wide(fl, f, 2 * axis)
            v1, l1 = wide(fv, f, 2 * axis + 1), wide(fl, f, 2 * axis + 1)
            modes_here = []
            for m in range(2):
                level = float(slopes[0][m]) * l0 + float(slopes[1][m]) * l1
                modes_here.append(level + (v0 if m == 0 else v1))
            faces.append(modes_here)
        for a in range(2):
            first = groups(wide(z, aligned((2 * f + a) * FACE, FACE)) - faces[0][a])
            third = [weighted(MODES[:, a], groups(faces[2][c])) for c in range(2)]
            for b in range(2):
                level = weighted(MODES[:, b], first) - weighted(MODES[:, a], groups(faces[1][b]))
                for c in range(2):
                    column = modes[c * NODES : (c + 1) * NODES, 0:1]
                    other = modes[b * NODES : (b + 1) * NODES, 0:1]
                    row = f * NODES + 4 * a + 2 * b + c
                    value = level * column - third[c] * other
                    cs[pl.ds(row, 1), cols] = jnp.sum(value, axis=0, keepdims=True)
        return carry

    lax.fori_loop(0, fields * tiles // 2, restrict, 0)

    row_cells = sums_ref.shape[1]
    coarse = cs[...]
    hot = lax.broadcasted_iota(jnp.int32, (row_cells, elems), 0) == cells[...]
    hot = hot.astype(jnp.float32).astype(jnp.bfloat16)
    high = coarse.astype(jnp.bfloat16)
    low = (coarse - high.astype(jnp.float32)).astype(jnp.bfloat16)
    both = lax.dot_general(
        jnp.concatenate([high, low], axis=0),
        hot,
        (((1,), (1,)), ((), ())),
        preferred_element_type=jnp.float32,
    )
    sums_ref[...] = both[: coarse.shape[0]] + both[coarse.shape[0] :]
    pl.semaphore_wait(barrier, n_sub - 1)
    copies = []
    for step, peer in enumerate(peers):
        copies.append(
            pltpu.make_async_remote_copy(
                src_ref=sums_ref,
                dst_ref=box.at[step],
                send_sem=send_sem.at[step],
                recv_sem=recv_sem.at[step],
                device_id=peer,
                device_id_type=MESH,
            )
        )
        copies[-1].start()

    def finish(n, carry):
        f, h, wide = halves(n)
        low_lift = wide(fl, f, 0)
        high_lift = wide(fl, f, 1)
        for i in range(NODES):
            part = slice(i * NODES, (i + 1) * NODES)
            stack = []
            for face in range(2, 6):
                stack += [wide(fv, f, face, part), wide(fl, f, face, part)]
            rows = aligned(f * BRICK + i * FACE, FACE)
            value = wide(rest, rows) - product(lift_ref[...], jnp.concatenate(stack, axis=0))
            value = value + float(DERIV[0, i]) * low_lift - float(DERIV[-1, i]) * high_lift
            if i == 0:
                value = value - wide(fv, f, 0)
            if i == NODES - 1:
                value = value - wide(fv, f, 1)
            res[2 * h, rows, :] = value[:, :LANES]
            res[2 * h + 1, rows, :] = value[:, LANES:]
        return carry

    lax.fori_loop(0, fields * tiles // 2, finish, 0)
    for copy in copies:
        copy.wait()
    total = sums_ref[...]
    for step in range(n_sub - 1):
        total = total + box[step]
    total_ref[...] = total


def correct_kernel(
    total_ref, inverse_ref, cells_ref, modes_ref, p_ref, tiled,
    out_hbm, res_hbm,
    out_s, res_sem, out_sem,
):
    fields = p_ref.shape[0]
    elems = p_ref.shape[-1]
    row_cells = total_ref.shape[1]
    half = 2 * LANES
    copies = [
        pltpu.make_async_copy(tiled.at[t], res_hbm.at[:, pl.ds(t * LANES, LANES)], res_sem.at[t])
        for t in range(tiled.shape[0])
    ]
    for copy in copies:
        copy.start()
    rows = []
    for f in range(fields):
        level = None
        for j in range(NODES):
            term = inverse_ref[j] * total_ref[f * NODES + j : f * NODES + j + 1, :]
            level = term if level is None else level + term
        rows.append(level)
    level = jnp.concatenate(rows, axis=0)
    high = level.astype(jnp.bfloat16)
    low = (level - high.astype(jnp.float32)).astype(jnp.bfloat16)
    both = jnp.concatenate([high, low], axis=0)
    columns = [modes_ref[c * NODES : (c + 1) * NODES, 0:1] for c in range(2)]
    for h in range(elems // half):
        cols = slice(h * half, (h + 1) * half)
        hot = lax.broadcasted_iota(jnp.int32, (row_cells, half), 0) == cells_ref[:, cols]
        hot = hot.astype(jnp.float32).astype(jnp.bfloat16)
        spread = lax.dot_general(
            both, hot, (((1,), (0,)), ((), ())), preferred_element_type=jnp.float32
        )
        spread = spread[: level.shape[0]] + spread[level.shape[0] :]
        for f in range(fields):
            planes = []
            for a in range(2):
                lines = []
                for b in range(2):
                    start = f * NODES + 4 * a + 2 * b
                    lines.append(
                        columns[0] * spread[start : start + 1]
                        + columns[1] * spread[start + 1 : start + 2]
                    )
                planes.append([weighted(MODES[j], lines) for j in range(NODES)])
            for j in range(NODES):
                part = slice(j * NODES, (j + 1) * NODES)
                for i in range(NODES):
                    grown = weighted(MODES[i], [planes[0][j], planes[1][j]])
                    out_s[f, i, part, cols] = p_ref[f, i, part, cols] + grown
            where = (f, slice(None), slice(None), pl.ds(h * half, half))
            copies.append(
                pltpu.make_async_copy(out_s.at[where], out_hbm.at[where], out_sem.at[h, f])
            )
            copies[-1].start()
    for copy in copies:
        copy.wait()


def limits(mib, **extra):
    return pltpu.CompilerParams(vmem_limit_bytes=mib << 20, **extra)


def shaped(*shape):
    return jax.ShapeDtypeStruct(shape, jnp.float32)


def on_device(
    n_blk,
    n_sub,
    pressure,
    right_side,
    geometry,
    face_weight,
    face_metric,
    cross_slots,
    local_pairs,
    coarse_map,
    coarse_inverse,
):
    fields = pressure.shape[0]
    elems = pressure.shape[-1]
    slot_total = cross_slots.shape[2]
    pair_total = local_pairs.shape[1]
    row_cells = coarse_inverse.shape[-1]
    tiles = elems // LANES
    width = slot_total // 9
    slabs = (fields, NODES, FACE, elems)
    rows = fields * BRICK
    p = pressure.reshape(slabs)
    weights = jnp.transpose(face_weight, (1, 0, 2))
    metrics = jnp.transpose(face_metric, (1, 0, 2))
    cells = coarse_map.reshape(1, elems)
    modes = jnp.asarray(np.repeat(MODES.T.reshape(2 * NODES, 1), LANES, axis=1), jnp.float32)
    pad_width = -(-slot_total // LANES) * LANES
    side_total = slot_total + 2 * pair_total
    f32 = jnp.float32
    i32 = jnp.int32
    inside = pl.BlockSpec(memory_space=VMEM)
    outside = pl.BlockSpec(memory_space=pltpu.MemorySpace.HBM)
    number_scratch = [
        pltpu.VMEM((1, slot_total), i32),
        pltpu.VMEM((1, pair_total), i32),
        pltpu.VMEM((1, pair_total), i32),
        pltpu.SMEM((1, slot_total), i32),
        pltpu.SMEM((1, pair_total), i32),
        pltpu.SMEM((1, pair_total), i32),
    ]
    dma = pltpu.SemaphoreType.DMA

    rest, levels, values, lifts = pl.pallas_call(
        functools.partial(front_kernel, n_blk, n_sub),
        in_specs=[outside] * 9,
        out_specs=[inside] * 4,
        out_shape=[
            shaped(tiles, rows, LANES),
            shaped(tiles, 2 * fields * FACE, LANES),
            shaped(side_total, LANES),
            shaped(side_total, LANES),
        ],
        scratch_shapes=[
            pltpu.VMEM(cross_slots.shape, i32),
            pltpu.VMEM(local_pairs.shape, i32),
            pltpu.VMEM((FACE, 3 * FACE), jnp.bfloat16),
            pltpu.VMEM((FACE, 3 * FACE), jnp.bfloat16),
            pltpu.VMEM((tiles, rows, LANES), f32),
            pltpu.VMEM((tiles, 6, FACE, LANES), f32),
            pltpu.VMEM((tiles, 6, FACE, LANES), f32),
            pltpu.VMEM((tiles, 6 * BRICK, LANES), f32),
            pltpu.VMEM((tiles, rows, LANES), f32),
            pltpu.VMEM((rows, 2 * LANES), f32),
        ]
        + [pltpu.VMEM((6 * elems, LANES), f32)] * 3
        + [pltpu.VMEM((2 * pair_total, LANES), f32)] * 3
        + [
            pltpu.VMEM((side_total, LANES), i32),
            pltpu.VMEM((8, pad_width), f32),
            pltpu.VMEM((9, 3, width, LANES), f32),
            pltpu.VMEM((9, 3, width, LANES), f32),
        ]
        + number_scratch
        + [dma((4,)), dma((tiles, 3)), dma((tiles, 2)), dma((3,)), dma((9,)), dma((9,))],
        compiler_params=limits(36, collective_id=0, has_side_effects=True),
        name="front",
    )(
        *[
            pltpu.with_memory_space_constraint(value, pltpu.MemorySpace.HBM)
            for value in (
                cross_slots,
                local_pairs,
                pressure.reshape(rows, elems),
                weights,
                metrics,
                geometry.reshape(6 * BRICK, elems),
                right_side.reshape(rows, elems),
                jnp.asarray(forward_table()),
                jnp.asarray(backward_table()),
            )
        ]
    )

    value_table, lift_rows = pl.pallas_call(
        scatter_kernel,
        in_specs=[inside] * 4,
        out_specs=[inside] * 2,
        out_shape=[shaped(6 * elems, LANES), shaped(6 * elems, LANES)],
        scratch_shapes=number_scratch + [dma((3,))],
        compiler_params=limits(8),
        name="scatter",
    )(cross_slots, local_pairs, values, lifts)

    totals, tiled = pl.pallas_call(
        functools.partial(reduce_kernel, n_sub),
        in_specs=[inside] * 7,
        out_specs=[inside] * 2,
        out_shape=[shaped(fields * NODES, row_cells), shaped(tiles, rows, LANES)],
        scratch_shapes=[
            pltpu.VMEM((tiles, fields, 6, FACE, LANES), f32),
            pltpu.VMEM((tiles, fields, 6, FACE, LANES), f32),
            pltpu.VMEM((fields * NODES, elems), f32),
            pltpu.VMEM((fields * NODES, row_cells), f32),
            pltpu.VMEM((n_sub - 1, fields * NODES, row_cells), f32),
            dma((n_sub - 1,)),
            dma((n_sub - 1,)),
        ],
        compiler_params=limits(24, collective_id=1, has_side_effects=True),
        name="reduce",
    )(value_table, lift_rows, rest, levels, jnp.asarray(lift_table()), modes, cells)

    corrected, residual = pl.pallas_call(
        correct_kernel,
        in_specs=[inside] * 5 + [pl.BlockSpec(memory_space=pl.ANY)],
        out_specs=[outside] * 2,
        out_shape=[shaped(*slabs), shaped(rows, elems)],
        scratch_shapes=[
            pltpu.VMEM(slabs, f32),
            dma((tiles,)),
            dma((elems // (2 * LANES), fields)),
        ],
        compiler_params=limits(16),
        name="correct",
    )(totals, coarse_inverse, cells, modes, p, tiled)
    return residual.reshape(pressure.shape), corrected.reshape(pressure.shape)


def solution(mesh):
    return jax.shard_map(
        functools.partial(on_device, mesh.shape["blk"], mesh.shape["sub"]),
        mesh=mesh,
        in_specs=(
            P(None, None, None, None, ("blk", "sub")),
            P(None, None, None, None, ("blk", "sub")),
            P(None, None, None, None, ("blk", "sub")),
            P(None, None, ("blk", "sub")),
            P(None, None, ("blk", "sub")),
            P(None, ("blk", "sub"), None),
            P(None, ("blk", "sub")),
            P(("blk", "sub")),
            P(None, None, "blk"),
        ),
        out_specs=(
            P(None, None, None, None, ("blk", "sub")),
            P(None, None, None, None, ("blk", "sub")),
        ),
        check_vma=False,
    )
```

```python
import functools

import jax
import jax.numpy as jnp
import numpy as np
from jax import lax
from jax.experimental import pallas as pl
from jax.experimental.pallas import tpu as pltpu
from jax.sharding import PartitionSpec as P

NODES = 8
FACE = NODES * NODES
BRICK = NODES * FACE
LANES = 128
MESH = pl.DeviceIdType.MESH
VMEM = pltpu.MemorySpace.VMEM
SMEM = pltpu.MemorySpace.SMEM


def node_points():
    positive = [0.2092992179024789, 0.5917001814331423, 0.8717401485096066, 1.0]
    return np.array(sorted([-entry for entry in positive] + positive))


def derivative_matrix():
    points = node_points()
    count = len(points)
    weights = np.array(
        [
            1.0 / np.prod([points[row] - points[col] for col in range(count) if col != row])
            for row in range(count)
        ]
    )
    matrix = np.zeros((count, count))
    for row in range(count):
        for col in range(count):
            if row != col:
                matrix[row, col] = weights[col] / weights[row] / (points[row] - points[col])
        matrix[row, row] = -np.sum(matrix[row])
    return matrix


DERIV = derivative_matrix()
POINTS = node_points()
MODES = np.stack([(1.0 - POINTS) / 2.0, (1.0 + POINTS) / 2.0], axis=1)


def split_constant(matrix):
    high = matrix.astype(jnp.bfloat16)
    low = (matrix - high.astype(np.float64)).astype(jnp.bfloat16)
    return np.concatenate([high, low, high], axis=1)


def forward_table():
    eye = np.eye(NODES)
    return split_constant(np.kron(eye, DERIV))


def backward_table():
    eye = np.eye(NODES)
    return split_constant(np.kron(eye, DERIV.T))


def lift_table():
    eye = np.eye(NODES)
    rows = [eye[:, :1], -DERIV[:1].T, eye[:, -1:], DERIV[-1:].T]
    second = [np.kron(row, eye) for row in rows]
    third = [np.kron(eye, row) for row in rows]
    return split_constant(np.concatenate(second + third, axis=1))


def split_rows(values):
    high = values.astype(jnp.bfloat16)
    low = (values - high.astype(jnp.float32)).astype(jnp.bfloat16)
    return jnp.concatenate([high, high, low], axis=0)


def product(table, values):
    return lax.dot_general(
        table, split_rows(values), (((1,), (0,)), ((), ())), preferred_element_type=jnp.float32
    )


def even_odd(matrix, layers):
    half = NODES // 2
    sums = [layers[k] + layers[NODES - 1 - k] for k in range(half)]
    gaps = [layers[k] - layers[NODES - 1 - k] for k in range(half)]
    result = [None] * NODES
    for row in range(half):
        even = None
        odd = None
        for k in range(half):
            first = float((matrix[row, k] + matrix[row, NODES - 1 - k]) / 2)
            second = float((matrix[row, k] - matrix[row, NODES - 1 - k]) / 2)
            even = first * sums[k] if even is None else even + first * sums[k]
            odd = second * gaps[k] if odd is None else odd + second * gaps[k]
        result[row] = odd + even
        result[NODES - 1 - row] = odd - even
    return result


def weighted(coefficients, layers):
    total = None
    for factor, layer in zip(coefficients, layers):
        term = float(factor) * layer
        total = term if total is None else total + term
    return total


def turn_code(code, inverse):
    first = code & 1
    second = (code >> 1) & 1
    swap = (code >> 2) & 1
    if inverse:
        first, second = (
            jnp.where(swap != 0, second, first),
            jnp.where(swap != 0, first, second),
        )
    return first * 56 + second * 7 + swap * 128


def lane_pick(values, index):
    return jnp.take_along_axis(values, index, axis=1, mode="promise_in_bounds")


def lane_source(turn):
    lane = lax.broadcasted_iota(jnp.int32, turn.shape, 1)
    swapped = ((lane & 7) << 3) | ((lane >> 3) & 7) | (lane & FACE)
    return (jnp.where((turn & 128) != 0, swapped, lane) ^ turn) & (LANES - 1)


def spread_metric(both):
    low = lax.broadcasted_iota(jnp.int32, both.shape, 1) < FACE
    return jnp.where(low, pltpu.roll(both, FACE, 1), both)


def pair_flux(own, peer, turn):
    wm1, v1, g1 = own
    wm2, v2, g2 = peer
    source = lane_source(turn)
    low = lax.broadcasted_iota(jnp.int32, turn.shape, 1) < FACE
    penalty = NODES * (NODES + 1) / 2.0
    jump = v1 - lane_pick(v2, source)
    gap = g1 - lane_pick(g2, source)
    total = wm1 + lane_pick(wm2, source)
    turned = pltpu.roll(total, FACE, 1)
    weight = 0.5 * jnp.where(low, total, turned)
    tau = (penalty * 0.5) * jnp.where(low, turned, total)
    return weight * (tau * jump - 0.5 * gap), -0.5 * weight * jump


def row_numbers(slots, pairs, elems, staged, rows, sem):
    staged[0][...] = slots[1] * elems + slots[0]
    staged[1][...] = pairs[1:2] * elems + pairs[0:1]
    staged[2][...] = pairs[3:4] * elems + pairs[2:3]
    return [pltpu.make_async_copy(staged[n], rows[n], sem.at[n]) for n in range(3)]


def code_rows(slots, pairs, pad, cb):
    slot_total = slots.shape[2]
    pair_total = pairs.shape[1]
    raw = slots[4]
    code = jnp.where(slots[3] != 0, turn_code(raw, False), turn_code(raw, True)) + 256 * slots[2]
    pad[0:1, 0:slot_total] = code.astype(jnp.float32)
    pad[0:1, slot_total:] = jnp.zeros((1, pad.shape[1] - slot_total), jnp.float32)
    for t in range(pad.shape[1] // LANES):
        row = jnp.broadcast_to(pad[0:1, t * LANES : (t + 1) * LANES], (LANES, LANES))
        count = min(LANES, slot_total - t * LANES)
        cb[t * LANES : t * LANES + count, :] = row.T.astype(jnp.int32)[:count]
    local = pairs[4:5, :]
    for side, codes in enumerate((turn_code(local, False), turn_code(local, True))):
        for t in range(pair_total // LANES):
            row = codes[:, t * LANES : (t + 1) * LANES].astype(jnp.float32)
            start = slot_total + side * pair_total + t * LANES
            cb[start : start + LANES, :] = jnp.broadcast_to(row, (LANES, LANES)).T.astype(jnp.int32)


def aligned(start, size):
    return pl.ds(pl.multiple_of(start, size), size)


def node_layers(t, axis, start, p_s):
    layers = []
    for k in range(NODES):
        if axis == 0:
            layers.append(p_s[t, start + k * FACE : start + (k + 1) * FACE, :])
        elif axis == 1:
            rows = [
                p_s[t, start + i * FACE + k * NODES : start + i * FACE + (k + 1) * NODES, :]
                for i in range(NODES)
            ]
            layers.append(jnp.concatenate(rows, axis=0))
        else:
            layers.append(p_s[t, pl.ds(start + k, FACE, stride=NODES), :])
    return layers


def face_rows(face, t, elems):
    return aligned(face * elems + t * LANES, LANES)


def fixed_tile(t, elems, fw_s, fm_s, table):
    for face in range(6):
        both = jnp.concatenate([fw_s[t, face], fm_s[t, face]], axis=0)
        table[face_rows(face, t, elems), :] = both.T


def value_tile(t, elems, p_s, table):
    for axis in range(3):
        for side in range(2):
            ends = []
            for start in range(0, p_s.shape[1], BRICK):
                k = side * (NODES - 1)
                if axis == 0:
                    ends.append(p_s[t, start + k * FACE : start + (k + 1) * FACE, :])
                elif axis == 1:
                    ends += [
                        p_s[t, start + i * FACE + k * NODES : start + i * FACE + (k + 1) * NODES, :]
                        for i in range(NODES)
                    ]
                else:
                    ends.append(p_s[t, pl.ds(start + k, FACE, stride=NODES), :])
            table[face_rows(2 * axis + side, t, elems), :] = jnp.concatenate(ends, axis=0).T


def slope_tile(t, elems, p_s, fm_s, table):
    for axis in range(3):
        slopes = []
        for start in range(0, p_s.shape[1], BRICK):
            layers = node_layers(t, axis, start, p_s)
            slopes.append((weighted(-DERIV[0], layers), weighted(DERIV[-1], layers)))
        for side in range(2):
            face = 2 * axis + side
            slope = jnp.concatenate([entry[side] * fm_s[t, face] for entry in slopes], axis=0)
            table[face_rows(face, t, elems), :] = slope.T


def volume_half(h, p_s, g_s, rhs_s, fwd, bwd, out, z, s_ref):
    fields = p_s.shape[1] // BRICK
    tiles = (2 * h, 2 * h + 1)

    def wide(ref, rows):
        return jnp.concatenate([ref[tiles[0], rows, :], ref[tiles[1], rows, :]], axis=1)

    def first(n, carry):
        f = n // NODES
        r = n % NODES
        where = [aligned(f * BRICK + k * FACE + r * NODES, NODES) for k in range(NODES)]
        for q, value in enumerate(even_odd(DERIV, [wide(p_s, rows) for rows in where])):
            s_ref[where[q], :] = value
        return carry

    lax.fori_loop(0, fields * NODES, first, 0, unroll=4)

    def middle(i, carry):
        g = [wide(g_s, aligned(n * BRICK + i * FACE, FACE)) for n in range(6)]
        for f in range(fields):
            rows = aligned(f * BRICK + i * FACE, FACE)
            x = wide(p_s, rows)
            s3 = product(fwd[...], x)
            s2 = jnp.concatenate(
                even_odd(DERIV, [x[j * NODES : (j + 1) * NODES] for j in range(NODES)]), axis=0
            )
            s1 = s_ref[rows, :]
            q1 = g[0] * s1 + g[3] * s2 + g[4] * s3
            q2 = g[3] * s1 + g[1] * s2 + g[5] * s3
            q3 = g[4] * s1 + g[5] * s2 + g[2] * s3
            s_ref[rows, :] = q1
            r2 = jnp.concatenate(
                even_odd(DERIV.T, [q2[j * NODES : (j + 1) * NODES] for j in range(NODES)]), axis=0
            )
            r23 = product(bwd[...], q3) + r2
            out[tiles[0], rows, :] = r23[:, :LANES]
            out[tiles[1], rows, :] = r23[:, LANES:]
        return carry

    lax.fori_loop(0, NODES, middle, 0, unroll=8)

    def last(n, carry):
        f = n // NODES
        r = n % NODES
        where = [aligned(f * BRICK + k * FACE + r * NODES, NODES) for k in range(NODES)]
        left = []
        for q, value in enumerate(even_odd(DERIV.T, [s_ref[rows, :] for rows in where])):
            left.append(wide(rhs_s, where[q]) - (wide(out, where[q]) + value))
            out[tiles[0], where[q], :] = left[q][:, :LANES]
            out[tiles[1], where[q], :] = left[q][:, LANES:]
        for a in range(2):
            rows = aligned((2 * f + a) * FACE + r * NODES, NODES)
            level = weighted(MODES[:, a], left)
            z[tiles[0], rows, :] = level[:, :LANES]
            z[tiles[1], rows, :] = level[:, LANES:]
        return carry

    lax.fori_loop(0, fields * NODES, last, 0, unroll=4)


def front_kernel(
    n_blk, n_sub,
    slots_hbm, pairs_hbm, p_hbm, fw_hbm, fm_hbm, g_hbm, rhs_hbm, fwd_hbm, bwd_hbm,
    rest, z, vb, hb,
    slots, pairs, fwd, bwd, p_s, fw_s, fm_s, g_s, rhs_s, s_ref, tv, tg, tw, la, lb, lc, cb, pad, send, recv,
    st0, st1, st2, rw0, rw1, rw2,
    small_sem, load_sem, geo_sem, row_sem, send_sem, recv_sem,
):
    elems = tv.shape[0] // 6
    tiles = elems // LANES
    slot_total = slots.shape[2]
    pair_total = pairs.shape[1]
    width = slot_total // 9
    tables = (tw, tv, tg)
    locals_ = (la, lb, lc)
    place = lax.axis_index("blk")
    sub = lax.axis_index("sub")

    def peer(k):
        return (
            lax.rem(place + (k // 3 - 1) + n_blk, n_blk),
            lax.rem(sub + (k % 3 - 1) + n_sub, n_sub),
        )

    others = [2, 0, 8, 6, 5, 3, 1, 7]
    barrier = pltpu.get_barrier_semaphore()
    for k in others:
        pl.semaphore_signal(barrier, inc=1, device_id=peer(k), device_id_type=MESH)
    small = [
        pltpu.make_async_copy(source, target, small_sem.at[n])
        for n, (source, target) in enumerate(
            ((slots_hbm, slots), (pairs_hbm, pairs), (fwd_hbm, fwd), (bwd_hbm, bwd))
        )
    ]
    for copy in small[:2]:
        copy.start()
    loads = []
    geo = []
    for t in range(tiles):
        cols = pl.ds(t * LANES, LANES)
        geo.append(pltpu.make_async_copy(g_hbm.at[:, cols], g_s.at[t], geo_sem.at[t, 0]))
        geo.append(pltpu.make_async_copy(rhs_hbm.at[:, cols], rhs_s.at[t], geo_sem.at[t, 1]))
        loads.append(
            [
                pltpu.make_async_copy(fw_hbm.at[:, :, cols], fw_s.at[t], load_sem.at[t, 0]),
                pltpu.make_async_copy(fm_hbm.at[:, :, cols], fm_s.at[t], load_sem.at[t, 1]),
                pltpu.make_async_copy(p_hbm.at[:, cols], p_s.at[t], load_sem.at[t, 2]),
            ]
        )
    for t in range(tiles):
        loads[t][0].start()
        loads[t][1].start()
    for t in range(tiles):
        loads[t][2].start()
    for copy in small[:2]:
        copy.wait()
    numbers = row_numbers(slots, pairs, elems, (st0, st1, st2), (rw0, rw1, rw2), row_sem)
    for copy in numbers:
        copy.start()
    for t in range(tiles):
        loads[t][0].wait()
        loads[t][1].wait()
        fixed_tile(t, elems, fw_s, fm_s, tw)
    for t in range(tiles):
        loads[t][2].wait()
        if t == tiles - 1:
            for copy in geo + small[2:]:
                copy.start()
        value_tile(t, elems, p_s, tv)
        slope_tile(t, elems, p_s, fm_s, tg)
    for copy in numbers:
        copy.wait()
    for k in others:

        def gather(n, carry, k=k):
            base = n * 16
            rows = [rw0[0, k * width + base + u] for u in range(16)]
            for j in range(3):
                found = [tables[j][pl.ds(row, 1), :] for row in rows]
                for u in range(16):
                    send[k, j, pl.ds(base + u, 1), :] = found[u]
            return carry

        lax.fori_loop(0, width // 16, gather, 0)
    pl.semaphore_wait(barrier, len(others))
    copies = []
    for k in others:
        copies.append(
            pltpu.make_async_remote_copy(
                src_ref=send.at[k],
                dst_ref=recv.at[8 - k],
                send_sem=send_sem.at[k],
                recv_sem=recv_sem.at[8 - k],
                device_id=peer(k),
                device_id_type=MESH,
            )
        )
        copies[-1].start()
    for side, numbers in enumerate((rw1, rw2)):

        def gather_local(n, carry, side=side, numbers=numbers):
            base = n * 16
            rows = [numbers[0, base + u] for u in range(16)]
            for j in range(3):
                found = [tables[j][pl.ds(row, 1), :] for row in rows]
                for u in range(16):
                    locals_[j][pl.ds(side * pair_total + base + u, 1), :] = found[u]
            return carry

        lax.fori_loop(0, pair_total // 16, gather_local, 0)

    code_rows(slots, pairs, pad, cb)
    group = pair_total

    def local_flux(n, carry):
        one = aligned(n * group, group)
        two = aligned(n * group + pair_total, group)
        rows = pl.ds(pl.multiple_of(n * group + slot_total, FACE), group)
        peers = pl.ds(pl.multiple_of(n * group + slot_total + pair_total, FACE), group)
        first = [table[one, :] for table in locals_]
        second = [table[two, :] for table in locals_]
        value, lift = pair_flux(first, second, cb[rows, :])
        vb[rows, :] = value
        hb[rows, :] = lift * spread_metric(first[0])
        back = lane_source(cb[peers, :])
        vb[peers, :] = -lane_pick(value, back)
        hb[peers, :] = -lane_pick(lift, back) * spread_metric(second[0])
        return carry

    lax.fori_loop(0, pair_total // group, local_flux, 0)
    for copy in geo + small[2:]:
        copy.wait()

    def volume(h, carry):
        volume_half(h, p_s, g_s, rhs_s, fwd, bwd, rest, z, s_ref)
        return carry

    lax.fori_loop(0, tiles // 2, volume, 0)
    for first in range(0, len(others), 2):
        for copy in copies[first : first + 2]:
            copy.wait()
        for k in others[first : first + 2]:
            k = 8 - k
            rows = slice(k * width, (k + 1) * width)
            turn = cb[rows, :]
            own = [send[k, j] for j in range(3)]
            value, lift = pair_flux(own, [recv[k, j] for j in range(3)], turn)
            live = turn >= 256
            vb[rows, :] = jnp.where(live, value, 0.0)
            hb[rows, :] = jnp.where(live, lift * spread_metric(own[0]), 0.0)

    vb[4 * width : 5 * width, :] = jnp.zeros((width, LANES), jnp.float32)
    hb[4 * width : 5 * width, :] = jnp.zeros((width, LANES), jnp.float32)


def scatter_kernel(slots, pairs, vb, hb, vt, lt, st0, st1, st2, rw0, rw1, rw2, row_sem):
    elems = vt.shape[0] // 6
    slot_total = slots.shape[2]
    pair_total = pairs.shape[1]
    numbers = row_numbers(slots, pairs, elems, (st0, st1, st2), (rw0, rw1, rw2), row_sem)
    for copy in numbers:
        copy.start()

    def clear(n, carry):
        rows = aligned(n * LANES, LANES)
        zero = jnp.zeros((LANES, LANES), jnp.float32)
        vt[rows, :] = zero
        lt[rows, :] = zero
        return carry

    lax.fori_loop(0, vt.shape[0] // LANES, clear, 0)
    for copy in numbers:
        copy.wait()
    for start, count, numbers in (
        (0, slot_total, rw0),
        (slot_total, pair_total, rw1),
        (slot_total + pair_total, pair_total, rw2),
    ):

        def scatter(n, carry, start=start, numbers=numbers):
            base = n * 32
            rows = [numbers[0, base + u] for u in range(32)]
            for source, table in ((vb, vt), (hb, lt)):
                found = [source[pl.ds(start + base + u, 1), :] for u in range(32)]
                for u in range(32):
                    table[pl.ds(rows[u], 1), :] = found[u]
            return carry

        lax.fori_loop(0, count // 32, scatter, 0)


def reduce_kernel(
    n_sub,
    vt, lt, rest, z, lift_ref, modes, cells,
    total_ref, res,
    fv, fl, cs, sums_ref, box, send_sem, recv_sem,
):
    elems = vt.shape[0] // 6
    tiles = elems // LANES
    fields = fv.shape[1]
    place = lax.axis_index("blk")
    sub = lax.axis_index("sub")
    barrier = pltpu.get_barrier_semaphore()
    peers = [(place, lax.rem(sub + step, n_sub)) for step in range(1, n_sub)]
    for peer in peers:
        pl.semaphore_signal(barrier, inc=1, device_id=peer, device_id_type=MESH)

    for face in range(6):
        for t in range(tiles):
            rows = slice(face * elems + t * LANES, face * elems + (t + 1) * LANES)
            value = vt[rows, :].T
            lift = lt[rows, :].T
            for f in range(fields):
                fv[t, f, face] = value[f * FACE : (f + 1) * FACE]
                fl[t, f, face] = lift[f * FACE : (f + 1) * FACE]

    half = 2 * LANES
    slopes = (-DERIV[0] @ MODES, DERIV[-1] @ MODES)

    def halves(n):
        f = n // (tiles // 2)
        h = n % (tiles // 2)

        def wide(ref, *where):
            return jnp.concatenate([ref[2 * h, *where], ref[2 * h + 1, *where]], axis=-1)

        return f, h, wide

    def groups(layer):
        return [layer[k * NODES : (k + 1) * NODES] for k in range(NODES)]

    def restrict(n, carry):
        f, h, wide = halves(n)
        cols = aligned(h * half, half)
        faces = []
        for axis in range(3):
            v0, l0 = wide(fv, f, 2 * axis), wide(fl, f, 2 * axis)
            v1, l1 = wide(fv, f, 2 * axis + 1), wide(fl, f, 2 * axis + 1)
            modes_here = []
            for m in range(2):
                level = float(slopes[0][m]) * l0 + float(slopes[1][m]) * l1
                modes_here.append(level + (v0 if m == 0 else v1))
            faces.append(modes_here)
        for a in range(2):
            first = groups(wide(z, aligned((2 * f + a) * FACE, FACE)) - faces[0][a])
            third = [weighted(MODES[:, a], groups(faces[2][c])) for c in range(2)]
            for b in range(2):
                level = weighted(MODES[:, b], first) - weighted(MODES[:, a], groups(faces[1][b]))
                for c in range(2):
                    column = modes[c * NODES : (c + 1) * NODES, 0:1]
                    other = modes[b * NODES : (b + 1) * NODES, 0:1]
                    row = f * NODES + 4 * a + 2 * b + c
                    value = level * column - third[c] * other
                    cs[pl.ds(row, 1), cols] = jnp.sum(value, axis=0, keepdims=True)
        return carry

    lax.fori_loop(0, fields * tiles // 2, restrict, 0)

    row_cells = sums_ref.shape[1]
    coarse = cs[...]
    hot = lax.broadcasted_iota(jnp.int32, (row_cells, elems), 0) == cells[...]
    hot = hot.astype(jnp.float32).astype(jnp.bfloat16)
    high = coarse.astype(jnp.bfloat16)
    low = (coarse - high.astype(jnp.float32)).astype(jnp.bfloat16)
    both = lax.dot_general(
        jnp.concatenate([high, low], axis=0),
        hot,
        (((1,), (1,)), ((), ())),
        preferred_element_type=jnp.float32,
    )
    sums_ref[...] = both[: coarse.shape[0]] + both[coarse.shape[0] :]
    pl.semaphore_wait(barrier, n_sub - 1)
    copies = []
    for step, peer in enumerate(peers):
        copies.append(
            pltpu.make_async_remote_copy(
                src_ref=sums_ref,
                dst_ref=box.at[step],
                send_sem=send_sem.at[step],
                recv_sem=recv_sem.at[step],
                device_id=peer,
                device_id_type=MESH,
            )
        )
        copies[-1].start()

    def finish(n, carry):
        f, h, wide = halves(n)
        low_lift = wide(fl, f, 0)
        high_lift = wide(fl, f, 1)
        for i in range(NODES):
            part = slice(i * NODES, (i + 1) * NODES)
            stack = []
            for face in range(2, 6):
                stack += [wide(fv, f, face, part), wide(fl, f, face, part)]
            rows = aligned(f * BRICK + i * FACE, FACE)
            value = wide(rest, rows) - product(lift_ref[...], jnp.concatenate(stack, axis=0))
            value = value + float(DERIV[0, i]) * low_lift - float(DERIV[-1, i]) * high_lift
            if i == 0:
                value = value - wide(fv, f, 0)
            if i == NODES - 1:
                value = value - wide(fv, f, 1)
            res[2 * h, rows, :] = value[:, :LANES]
            res[2 * h + 1, rows, :] = value[:, LANES:]
        return carry

    lax.fori_loop(0, fields * tiles // 2, finish, 0)
    for copy in copies:
        copy.wait()
    total = sums_ref[...]
    for step in range(n_sub - 1):
        total = total + box[step]
    total_ref[...] = total


def correct_kernel(
    total_ref, inverse_ref, cells_ref, modes_ref, p_ref, tiled,
    out_hbm, res_hbm,
    out_s, res_sem, out_sem,
):
    fields = p_ref.shape[0]
    elems = p_ref.shape[-1]
    row_cells = total_ref.shape[1]
    half = 2 * LANES
    copies = [
        pltpu.make_async_copy(tiled.at[t], res_hbm.at[:, pl.ds(t * LANES, LANES)], res_sem.at[t])
        for t in range(tiled.shape[0])
    ]
    for copy in copies:
        copy.start()
    rows = []
    for f in range(fields):
        level = None
        for j in range(NODES):
            term = inverse_ref[j] * total_ref[f * NODES + j : f * NODES + j + 1, :]
            level = term if level is None else level + term
        rows.append(level)
    level = jnp.concatenate(rows, axis=0)
    high = level.astype(jnp.bfloat16)
    low = (level - high.astype(jnp.float32)).astype(jnp.bfloat16)
    both = jnp.concatenate([high, low], axis=0)
    columns = [modes_ref[c * NODES : (c + 1) * NODES, 0:1] for c in range(2)]
    for h in range(elems // half):
        cols = slice(h * half, (h + 1) * half)
        hot = lax.broadcasted_iota(jnp.int32, (row_cells, half), 0) == cells_ref[:, cols]
        hot = hot.astype(jnp.float32).astype(jnp.bfloat16)
        spread = lax.dot_general(
            both, hot, (((1,), (0,)), ((), ())), preferred_element_type=jnp.float32
        )
        spread = spread[: level.shape[0]] + spread[level.shape[0] :]
        for f in range(fields):
            planes = []
            for a in range(2):
                lines = []
                for b in range(2):
                    start = f * NODES + 4 * a + 2 * b
                    lines.append(
                        columns[0] * spread[start : start + 1]
                        + columns[1] * spread[start + 1 : start + 2]
                    )
                planes.append([weighted(MODES[j], lines) for j in range(NODES)])
            for j in range(NODES):
                part = slice(j * NODES, (j + 1) * NODES)
                for i in range(NODES):
                    grown = weighted(MODES[i], [planes[0][j], planes[1][j]])
                    out_s[f, i, part, cols] = p_ref[f, i, part, cols] + grown
            where = (f, slice(None), slice(None), pl.ds(h * half, half))
            copies.append(
                pltpu.make_async_copy(out_s.at[where], out_hbm.at[where], out_sem.at[h, f])
            )
            copies[-1].start()
    for copy in copies:
        copy.wait()


def limits(mib, **extra):
    return pltpu.CompilerParams(vmem_limit_bytes=mib << 20, **extra)


def shaped(*shape):
    return jax.ShapeDtypeStruct(shape, jnp.float32)


def on_device(
    n_blk,
    n_sub,
    pressure,
    right_side,
    geometry,
    face_weight,
    face_metric,
    cross_slots,
    local_pairs,
    coarse_map,
    coarse_inverse,
):
    fields = pressure.shape[0]
    elems = pressure.shape[-1]
    slot_total = cross_slots.shape[2]
    pair_total = local_pairs.shape[1]
    row_cells = coarse_inverse.shape[-1]
    tiles = elems // LANES
    width = slot_total // 9
    slabs = (fields, NODES, FACE, elems)
    rows = fields * BRICK
    p = pressure.reshape(slabs)
    weights = jnp.transpose(face_weight, (1, 0, 2))
    metrics = jnp.transpose(face_metric, (1, 0, 2))
    cells = coarse_map.reshape(1, elems)
    modes = jnp.asarray(np.repeat(MODES.T.reshape(2 * NODES, 1), LANES, axis=1), jnp.float32)
    pad_width = -(-slot_total // LANES) * LANES
    side_total = slot_total + 2 * pair_total
    f32 = jnp.float32
    i32 = jnp.int32
    inside = pl.BlockSpec(memory_space=VMEM)
    outside = pl.BlockSpec(memory_space=pltpu.MemorySpace.HBM)
    number_scratch = [
        pltpu.VMEM((1, slot_total), i32),
        pltpu.VMEM((1, pair_total), i32),
        pltpu.VMEM((1, pair_total), i32),
        pltpu.SMEM((1, slot_total), i32),
        pltpu.SMEM((1, pair_total), i32),
        pltpu.SMEM((1, pair_total), i32),
    ]
    dma = pltpu.SemaphoreType.DMA

    rest, levels, values, lifts = pl.pallas_call(
        functools.partial(front_kernel, n_blk, n_sub),
        in_specs=[outside] * 9,
        out_specs=[inside] * 4,
        out_shape=[
            shaped(tiles, rows, LANES),
            shaped(tiles, 2 * fields * FACE, LANES),
            shaped(side_total, LANES),
            shaped(side_total, LANES),
        ],
        scratch_shapes=[
            pltpu.VMEM(cross_slots.shape, i32),
            pltpu.VMEM(local_pairs.shape, i32),
            pltpu.VMEM((FACE, 3 * FACE), jnp.bfloat16),
            pltpu.VMEM((FACE, 3 * FACE), jnp.bfloat16),
            pltpu.VMEM((tiles, rows, LANES), f32),
            pltpu.VMEM((tiles, 6, FACE, LANES), f32),
            pltpu.VMEM((tiles, 6, FACE, LANES), f32),
            pltpu.VMEM((tiles, 6 * BRICK, LANES), f32),
            pltpu.VMEM((tiles, rows, LANES), f32),
            pltpu.VMEM((rows, 2 * LANES), f32),
        ]
        + [pltpu.VMEM((6 * elems, LANES), f32)] * 3
        + [pltpu.VMEM((2 * pair_total, LANES), f32)] * 3
        + [
            pltpu.VMEM((side_total, LANES), i32),
            pltpu.VMEM((8, pad_width), f32),
            pltpu.VMEM((9, 3, width, LANES), f32),
            pltpu.VMEM((9, 3, width, LANES), f32),
        ]
        + number_scratch
        + [dma((4,)), dma((tiles, 3)), dma((tiles, 2)), dma((3,)), dma((9,)), dma((9,))],
        compiler_params=limits(36, collective_id=0, has_side_effects=True),
        name="front",
    )(
        *[
            pltpu.with_memory_space_constraint(value, pltpu.MemorySpace.HBM)
            for value in (
                cross_slots,
                local_pairs,
                pressure.reshape(rows, elems),
                weights,
                metrics,
                geometry.reshape(6 * BRICK, elems),
                right_side.reshape(rows, elems),
                jnp.asarray(forward_table()),
                jnp.asarray(backward_table()),
            )
        ]
    )

    value_table, lift_rows = pl.pallas_call(
        scatter_kernel,
        in_specs=[inside] * 4,
        out_specs=[inside] * 2,
        out_shape=[shaped(6 * elems, LANES), shaped(6 * elems, LANES)],
        scratch_shapes=number_scratch + [dma((3,))],
        compiler_params=limits(8),
        name="scatter",
    )(cross_slots, local_pairs, values, lifts)

    totals, tiled = pl.pallas_call(
        functools.partial(reduce_kernel, n_sub),
        in_specs=[inside] * 7,
        out_specs=[inside] * 2,
        out_shape=[shaped(fields * NODES, row_cells), shaped(tiles, rows, LANES)],
        scratch_shapes=[
            pltpu.VMEM((tiles, fields, 6, FACE, LANES), f32),
            pltpu.VMEM((tiles, fields, 6, FACE, LANES), f32),
            pltpu.VMEM((fields * NODES, elems), f32),
            pltpu.VMEM((fields * NODES, row_cells), f32),
            pltpu.VMEM((n_sub - 1, fields * NODES, row_cells), f32),
            dma((n_sub - 1,)),
            dma((n_sub - 1,)),
        ],
        compiler_params=limits(24, collective_id=1, has_side_effects=True),
        name="reduce",
    )(value_table, lift_rows, rest, levels, jnp.asarray(lift_table()), modes, cells)

    corrected, residual = pl.pallas_call(
        correct_kernel,
        in_specs=[inside] * 5 + [pl.BlockSpec(memory_space=pl.ANY)],
        out_specs=[outside] * 2,
        out_shape=[shaped(*slabs), shaped(rows, elems)],
        scratch_shapes=[
            pltpu.VMEM(slabs, f32),
            dma((tiles,)),
            dma((elems // (2 * LANES), fields)),
        ],
        compiler_params=limits(16),
        name="correct",
    )(totals, coarse_inverse, cells, modes, p, tiled)
    return residual.reshape(pressure.shape), corrected.reshape(pressure.shape)


def solution(mesh):
    return jax.shard_map(
        functools.partial(on_device, mesh.shape["blk"], mesh.shape["sub"]),
        mesh=mesh,
        in_specs=(
            P(None, None, None, None, ("blk", "sub")),
            P(None, None, None, None, ("blk", "sub")),
            P(None, None, None, None, ("blk", "sub")),
            P(None, None, ("blk", "sub")),
            P(None, None, ("blk", "sub")),
            P(None, ("blk", "sub"), None),
            P(None, ("blk", "sub")),
            P(("blk", "sub")),
            P(None, None, "blk"),
        ),
        out_specs=(
            P(None, None, None, None, ("blk", "sub")),
            P(None, None, None, None, ("blk", "sub")),
        ),
        check_vma=False,
    )
```
